256 devices in a mesh: mem: 32 (over y, x, core), tile: 8 (over z).
Axes of the slice: x: 4, y: 4, z: 8, core: 2. Of those that a mesh axis runs over, the one named last changes fastest.
Arguments:
- perturbations: bfloat16 [64, 4, 256, 1024], P('mem', None, 'tile'), may hold values from -6 to 6
- right_side: float32 [4, 256, 1024], P(None, 'tile'), may hold values from -14 to 14
- fine_taps: float32 [2, 4, 5], replicated, may hold values from 0.3 to 1
- coarse_lat: float32 [64, 64], replicated, may hold values from -4 to 16, as said below
- coarse_lon: float32 [256, 256], replicated, may hold values from -4 to 16, as said below
Outputs:
- solution: float32 [4, 256, 1024], P(None, 'tile', 'mem')
- residual: float32 [4, 256, 1024], P(None, 'tile', 'mem')
The draws below stay inside these ranges and needn't reach their ends.
Inputs may be any that keep to these rules, and one draw needn't show every extreme that they name: `coarse_lat`: symmetric. `coarse_lon`: symmetric.
All inputs are finite; a program needn't handle non-finite values.
Results may differ from the reference program's by a relative error of at most 0.0003.
Values may be sent and summed in bfloat16 or wider, within the bound.
No kernel may reach another device: no remote copies, remote signals or barrier semaphores. Data moves between devices by JAX's collectives and lax.ppermute only.
A program may use at most 64 MiB of HBM per device.

```python
import jax
import jax.numpy as jnp
from jax import lax

LON = 1024
LEV = 4
ITERS = 2
MEMBERS = 64
LAT = 256
CLAT = 64
CLON = 256


def coarse_matrix(key, order_size, decay_len):
    positions = jnp.arange(order_size)
    distance = jnp.abs(positions[:, None] - positions[None, :]).astype(jnp.float32)
    uniform_draw = jax.random.uniform(key, (order_size, order_size), jnp.float32, -1.0, 1.0)
    off_diag = 0.5 * (uniform_draw + uniform_draw.T) * jnp.exp(-distance / decay_len) * (1.0 - jnp.eye(order_size, dtype=jnp.float32))
    row_weight = 1.0 + jnp.sum(jnp.abs(off_diag), axis=1)
    return 4.0 * (off_diag + jnp.diag(row_weight)) / jnp.mean(row_weight)


def draw_coarse_lat(key, part):
    return coarse_matrix(jax.random.fold_in(key, 17), CLAT, CLAT / 4.0)


def draw_coarse_lon(key, part):
    return coarse_matrix(jax.random.fold_in(key, 29), CLON, CLON / 4.0)


def draw_right_side(key, part):
    lat_pos = jnp.arange(LAT, dtype=jnp.float32)[None, :, None] / LAT
    lon_pos = jnp.arange(LON, dtype=jnp.float32)[None, None, :] / LON
    noise_draw = jnp.clip(jax.random.normal(jax.random.fold_in(key, 7), (LEV, LAT, LON), jnp.float32), -4.0, 4.0)
    return noise_draw * jnp.exp(0.6 * lat_pos + 0.6 * lon_pos)


def strengthened(values, key, source, target, parts, factor):
    owner, partner = [(jnp.arange(values.shape[position]) // (values.shape[position] // parts)).reshape([-1 if axis == position else 1 for axis in range(values.ndim)]) for position in (source, target)]
    chosen = jax.random.permutation(key, parts)[partner]
    strong = (owner == chosen) | (owner == (partner + parts // 2) % parts)
    return jnp.where(strong, factor * values, values)


def shard_levels(key, dims, cuts, smallest, high):
    gain = 1.0
    for position, blocks in cuts:
        heights = jax.random.uniform(jax.random.fold_in(jax.random.fold_in(key, 6), position), (blocks,), jnp.float32, smallest / len(cuts), high / len(cuts))
        gain = gain * jnp.repeat(jnp.exp(heights), dims[position] // blocks).reshape((-1,) + (1,) * (len(dims) - 1 - position))
    return gain


def heavy_noise(own_key, shape, scale, most, cuts, heavy, kind=jnp.bfloat16):
    values = scale * jax.random.normal(own_key, shape, jnp.float32)
    if cuts:
        values = values * shard_levels(own_key, shape, cuts, -0.22, 0.18)
    return jnp.clip(strengthened(values, jax.random.fold_in(own_key, 3), *heavy), -most, most).astype(kind)


def setup_inputs(seed: int = 0) -> dict:
    splits = jax.random.split(jax.random.key(seed), 6)
    perturbations = heavy_noise(splits[0], (MEMBERS, LEV, LAT, LON), 1.0, 6.0, ((0, 32), (2, 8)), (0, 3, 32, 2.75))
    right_side = draw_right_side(jax.random.fold_in(splits[5], 71), 0)
    fine_taps = jnp.clip(jax.random.uniform(splits[2], (2, LEV, 5), jnp.float32, 0.3, 1.0), 0.3, 1.0)
    coarse_lat = draw_coarse_lat(jax.random.fold_in(splits[5], 71), 0)
    coarse_lon = draw_coarse_lon(jax.random.fold_in(splits[5], 71), 0)
    return {"perturbations": perturbations, "right_side": right_side, "fine_taps": fine_taps, "coarse_lat": coarse_lat, "coarse_lon": coarse_lon}


exact_mode = lax.Precision.HIGHEST

def normalized(fine_taps):
    energy = fine_taps[:, :, 0] ** 2 + 2.0 * lax.optimization_barrier(jnp.sum(fine_taps[:, :, 1:] ** 2, axis=2))
    return fine_taps / jnp.sqrt(energy)[:, :, None]

def lat_pass(values, kernel):
    height = values.shape[1]
    padded = jnp.pad(values, ((0, 0), (4, 4), (0, 0)))
    result = kernel[:, 0, None, None] * values
    for offset in range(1, 5):
        result = result + kernel[:, offset, None, None] * (padded[:, 4 + offset:4 + offset + height] + padded[:, 4 - offset:4 - offset + height])
    return result

def lon_pass(values, kernel):
    result = kernel[:, 0, None, None] * values
    for offset in range(1, 5):
        result = result + kernel[:, offset, None, None] * (jnp.roll(values, offset, axis=2) + jnp.roll(values, -offset, axis=2))
    return result

def block_mean(values):
    levels, height, extent = values.shape
    return lax.optimization_barrier(jnp.mean(values.reshape(levels, height // 4, 4, extent // 4, 4), axis=(2, 4)))

def prolong(coarse):
    levels, height, extent = coarse.shape
    return jnp.broadcast_to(coarse[:, :, None, :, None], (levels, height, 4, extent, 4)).reshape(levels, height * 4, extent * 4)

def smooth(coarse, coarse_lat, coarse_lon):
    across = jnp.einsum('ab,lbc->lac', coarse_lat, coarse, precision=exact_mode)
    return jnp.einsum('lac,cd->lad', across, coarse_lon, precision=exact_mode)

def reference(perturbations, right_side, fine_taps, coarse_lat, coarse_lon):
    kernel = normalized(fine_taps)
    members = perturbations.shape[0]

    def apply_operator(vector):

        def advance(summed, member):
            spread = member.astype(jnp.float32)
            weighted = spread * vector
            coarse = block_mean(weighted)
            detail = weighted - prolong(coarse)
            detail = lat_pass(lat_pass(detail, kernel[0]), kernel[0])
            detail = lon_pass(lon_pass(detail, kernel[1]), kernel[1])
            blended = detail - prolong(block_mean(detail)) + prolong(smooth(coarse, coarse_lat, coarse_lon))
            return (summed + spread * blended, None)
        summed, _ = lax.scan(advance, jnp.zeros_like(vector), perturbations)
        return vector + summed / (members - 1)
    solution = jnp.zeros_like(right_side)
    residual = right_side
    squares = jnp.sum(residual * residual)
    for iteration in range(ITERS):
        applied = apply_operator(residual)
        step_size = squares / jnp.sum(residual * applied)
        solution = solution + step_size * residual
        residual = residual - step_size * applied
        squares = jnp.sum(residual * residual)
    return (solution, residual)
```

```python
import functools

import jax
import jax.numpy as jnp
from jax import lax
from jax.experimental import pallas as pl
from jax.experimental.pallas import tpu as pltpu
from jax.sharding import Mesh
from jax.sharding import PartitionSpec as P

MEM = ("mem_0", "mem_1", "mem_2")
F32 = jnp.float32
BF16 = jnp.bfloat16
EXACT = lax.Precision.HIGHEST
PAIRS, ROWS, LON = 8, 32, 1024
GROUPS, TILES = 32, 8


def mm(a, b):
    return jnp.dot(a, b, preferred_element_type=F32)


def exact_mm(a, b):
    return jnp.dot(a, b, preferred_element_type=F32, precision=EXACT)


def split2(x):
    high = x.astype(BF16)
    return high, (x - high.astype(F32)).astype(BF16)


def split3(x):
    high = x.astype(BF16)
    rest = x - high.astype(F32)
    mid = rest.astype(BF16)
    return high, mid, (rest - mid.astype(F32)).astype(BF16)


def iotas(rows, cols):
    return (
        lax.broadcasted_iota(jnp.int32, (rows, cols), 0),
        lax.broadcasted_iota(jnp.int32, (rows, cols), 1),
    )


def shrink_table(rows, cols, along_rows):
    i, j = iotas(rows, cols)
    hit = (i >> 2) == j if along_rows else i == (j >> 2)
    return jnp.where(hit, 0.25, 0.0).astype(BF16)


def expand_table(rows, cols, along_rows):
    i, j = iotas(rows, cols)
    hit = (i >> 2) == j if along_rows else i == (j >> 2)
    return jnp.where(hit, 1.0, 0.0).astype(BF16)


def block_mean(w):
    table = shrink_table(64, 256, False)
    part = sum(mm(table, piece) for piece in split3(w))
    stacked = jnp.concatenate([part[:, :512], part[:, 512:]], axis=0)
    table = shrink_table(512, 128, True)
    small = sum(mm(piece, table) for piece in split3(stacked))
    return jnp.concatenate([small[:64], small[64:]], axis=1)


def prolong(c):
    table = expand_table(256, 64, True)
    tall = sum(mm(table, piece) for piece in split2(c))
    stacked = jnp.concatenate([tall[:, :128], tall[:, 128:]], axis=0)
    table = expand_table(128, 512, False)
    wide = sum(mm(piece, table) for piece in split2(stacked))
    return jnp.concatenate([wide[:256], wide[256:]], axis=1)


def natural(blocks):
    rows = []
    for tall in range(16):
        lanes = [
            blocks[2 * tall + wide // 4, 8 * (wide % 4) : 8 * (wide % 4) + 8, :]
            for wide in range(8)
        ]
        rows.append(jnp.concatenate(lanes, axis=1))
    return jnp.concatenate(rows, axis=0)


def vector_of(ref):
    return natural(ref) if len(ref.shape) == 3 else ref[...]


def detail_kernel(x_ref, v_ref, c_ref, d_ref, top_ref, bottom_ref):
    v = vector_of(v_ref)
    w = x_ref[...].astype(F32) * jnp.concatenate([v, v], axis=0)
    c = block_mean(w)
    c_ref[...] = c.reshape(PAIRS, 8, 256)
    d = w - prolong(c)
    d_ref[...] = d
    for pair in range(PAIRS):
        top_ref[pair] = d[ROWS * pair : ROWS * pair + 8]
        bottom_ref[pair] = d[ROWS * pair + 24 : ROWS * pair + 32]


def table_kernel(tile_ref, lat_ref, lon_ref, high_ref, low_ref, band_ref):
    i, j = iotas(160, 192)
    first = jnp.zeros((160, 192), F32)
    for level in range(4):
        row = i - 40 * level
        dist = jnp.abs(j - 48 * level - row - 4)
        spot = tile_ref[0] * ROWS - 4 + row
        fits = (row >= 0) & (row < 40) & (j >= 48 * level) & (j < 48 * level + 48)
        fits = fits & (spot >= 0) & (spot < ROWS * TILES)
        for offset in range(5):
            first = jnp.where(fits & (dist == offset), lat_ref[level, offset], first)
    i, j = iotas(128, 160)
    second = jnp.zeros((128, 160), F32)
    for level in range(4):
        row = i - 32 * level
        dist = jnp.abs(j - 40 * level - row - 4)
        fits = (row >= 0) & (row < 32) & (j >= 40 * level) & (j < 40 * level + 40)
        for offset in range(5):
            second = jnp.where(fits & (dist == offset), lat_ref[level, offset], second)
    both = exact_mm(second, first)
    i, j = iotas(128, 128)
    mean = jnp.where((i >> 2) == (j >> 2), 0.25, 0.0)
    high, low = split2(jnp.concatenate([both, exact_mm(mean, both)], axis=0))
    high_ref[...] = high
    low_ref[...] = low
    for place in range(3):
        dist = jnp.abs(i + 128 * (place - 1) - j)
        for level in range(4):
            band = jnp.zeros((128, 128), F32)
            for offset in range(9):
                band = jnp.where(dist == offset, lon_ref[level, offset], band)
            high, low = split2(band)
            band_ref[level, 0, place] = high
            band_ref[level, 1, place] = low
            high, low = split2(-exact_mm(band, mean))
            band_ref[level, 2, place] = high
            band_ref[level, 3, place] = low


def banded(band_ref, level, kind):
    a, b, c = (band_ref[level, kind, place] for place in range(3))
    zero = jnp.zeros_like(a)
    left = jnp.concatenate([a, b, c, zero], axis=0)
    right = jnp.concatenate([zero, a, b, c], axis=0)
    return jnp.concatenate([left, right], axis=1)


def windows(parts, first_row):
    rows = []
    for block in range(4):
        for part in parts:
            lanes = [
                part[first_row : first_row + ROWS, 128 * tile : 128 * tile + 128]
                for tile in ((2 * block - 1) % 8, 2 * block, 2 * block + 1, (2 * block + 2) % 8)
            ]
            rows.append(jnp.concatenate(lanes, axis=1))
    return jnp.concatenate(rows, axis=0)


def lane_sums(values):
    i, j = iotas(8, 128)
    result = jnp.zeros((8, 128), F32)
    for lane, value in values:
        result = jnp.where((i == 0) & (j == lane), value, result)
    return result


def total(x):
    return jnp.sum(x, axis=(0, 1), keepdims=True)


def fine_kernel(scalars, *refs):
    if scalars:
        r_ref, a_ref, *refs = refs
    x_ref, d_ref, before_ref, after_ref, high_ref, low_ref, band_ref, *outs = refs
    fine_ref = outs[0]
    highs, lows = [], []
    for member in range(2):
        rows = []
        for level in range(4):
            pair = 4 * member + level
            rows += [
                before_ref[pair],
                d_ref[ROWS * pair : ROWS * pair + ROWS],
                after_ref[pair],
            ]
        high, low = split2(jnp.concatenate(rows, axis=0))
        passed = mm(high_ref[...], high) + mm(high_ref[...], low) + mm(low_ref[...], high)
        high, low = split2(passed)
        highs.append(high)
        lows.append(low)
    for level in range(4):
        result = None
        for kind in range(2):
            high = windows(highs, 128 * kind + ROWS * level)
            low = windows(lows, 128 * kind + ROWS * level)
            table_high = banded(band_ref, level, 2 * kind)
            table_low = banded(band_ref, level, 2 * kind + 1)
            term = mm(high, table_high) + mm(low, table_high) + mm(high, table_low)
            result = term if result is None else result + term
        for block in range(4):
            summed = None
            for member in range(2):
                row = ROWS * (4 * member + level)
                x = x_ref[row : row + ROWS, 256 * block : 256 * block + 256].astype(F32)
                at = 64 * block + ROWS * member
                term = x * result[at : at + ROWS]
                summed = term if summed is None else summed + term
            fine_ref[ROWS * level : ROWS * level + ROWS, 256 * block : 256 * block + 256] = summed
    if scalars:
        r, a, fine = r_ref[...], natural(a_ref), fine_ref[...]
        pairs = ((r, r), (r, a), (a, a), (r, fine), (a, fine))
        outs[1][...] = lane_sums([(k, total(p * q)) for k, (p, q) in enumerate(pairs)])


def smooth_kernel(c_ref, lat_ref, lon_ref, out_ref):
    c = c_ref[...].reshape(64, 256)
    out_ref[...] = exact_mm(exact_mm(lat_ref[...], c), lon_ref[...]).reshape(TILES, 8, 256)


def smooth_dots_kernel(c_ref, first_ref, lat_ref, lon_ref, sums_ref, out_ref):
    c = c_ref[...].reshape(64, 256)
    smoothed = exact_mm(exact_mm(lat_ref[...], c), lon_ref[...])
    out_ref[:, :8, :] = smoothed.reshape(TILES, 8, 256)
    dots = (total(first_ref[...].reshape(64, 256) * smoothed), total(c * smoothed))
    sums = sums_ref[...] + lane_sums([(5 + k, dot * 16.0) for k, dot in enumerate(dots)])
    sums = jnp.concatenate([sums, jnp.zeros_like(sums)], axis=1)
    for tile in range(TILES):
        out_ref[tile, 8:16, :] = sums


def blended(x_ref, fine_ref, smoothed):
    spread = prolong(smoothed.reshape(64, 256))
    return (
        fine_ref[...]
        + x_ref[:128].astype(F32) * spread[:128]
        + x_ref[128:].astype(F32) * spread[128:]
    )


def partial_kernel(x_ref, fine_ref, smoothed_ref, out_ref):
    p = blended(x_ref, fine_ref, smoothed_ref[...])
    for tall in range(16):
        for wide in range(8):
            out_ref[2 * tall + wide // 4, 8 * (wide % 4) : 8 * (wide % 4) + 8, :] = p[
                8 * tall : 8 * tall + 8, 128 * wide : 128 * wide + 128
            ]


def last_partial_kernel(x_ref, fine_ref, smoothed_ref, out_ref):
    p = blended(x_ref, fine_ref, smoothed_ref[:, :8, :])
    turned = p.T
    sums = jnp.sum(smoothed_ref[:, 8:16, :128], axis=0)
    for group in range(GROUPS):
        out_ref[group, :32, :] = turned[32 * group : 32 * group + 32]
        out_ref[group, 32:40, :] = sums


def share_kernel(scale, group_ref, arrived_ref, r_ref, out_ref):
    group = group_ref[0]
    share = r_ref[
        pl.ds(pl.multiple_of(8 * (group >> 1), 8), 8),
        pl.ds(pl.multiple_of(512 * (group & 1), 512), 512),
    ]
    share = jnp.concatenate([share[:, 128 * k : 128 * k + 128] for k in range(4)], axis=0)
    share = share + jnp.sum(arrived_ref[...], axis=0) * scale
    for other in range(GROUPS):
        out_ref[other] = share


def final_kernel(scale, group_ref, arrived_ref, r_ref, a_ref, x_out, res_out, r_turned, a_turned):
    group = group_ref[0]
    wide = group >> 2
    lanes = pl.ds(pl.multiple_of(128 * wide, 128), 128)
    r_turned[...] = r_ref[:, lanes].T
    rows = [
        a_ref[2 * tall + (wide >> 2), pl.ds(pl.multiple_of(8 * (wide & 3), 8), 8), :]
        for tall in range(16)
    ]
    a_turned[...] = jnp.concatenate(rows, axis=0).T
    mine = pl.ds(pl.multiple_of(32 * (group & 3), 32), 32)
    r, a = r_turned[mine, :], a_turned[mine, :]
    arrived = jnp.sum(arrived_ref[...], axis=0)
    b = a + arrived[:32] * scale
    i, j = iotas(8, 128)
    rr, ra, aa, rf, af, rc, ac = (
        total(jnp.where((i == 0) & (j == k), arrived[32:40], 0.0)) for k in range(7)
    )
    rr, ra, aa = rr / GROUPS, ra / GROUPS, aa / GROUPS
    step = rr / ra
    rb = ra + (rf + rc) * scale
    ab = aa + (af + ac) * scale
    squares = step * step * aa - rr
    next_step = squares / ((ra - step * aa) - step * (rb - step * ab))
    r_next = r - step * a
    x_out[...] = (step * r + next_step * r_next).T.reshape(4, ROWS, 32)
    res_out[...] = (r_next - next_step * (a - step * b)).T.reshape(4, ROWS, 32)


VMEM = pl.BlockSpec(memory_space=pltpu.VMEM)
SMEM = pl.BlockSpec(memory_space=pltpu.SMEM)


def call(kernel, outs, specs, args, flops, scratch=(), limit=48):
    shapes = [jax.ShapeDtypeStruct(*out) for out in outs]
    size = sum(a.size * a.dtype.itemsize for a in args)
    return pl.pallas_call(
        kernel,
        out_shape=shapes if len(shapes) > 1 else shapes[0],
        in_specs=specs,
        out_specs=[VMEM] * len(shapes) if len(shapes) > 1 else VMEM,
        scratch_shapes=list(scratch),
        compiler_params=pltpu.CompilerParams(vmem_limit_bytes=limit << 20),
        cost_estimate=pl.CostEstimate(flops=flops, bytes_accessed=size, transcendentals=0),
    )(*args)


def exchange(blocks, axis):
    return lax.all_to_all(blocks, axis, 0, 0, tiled=True)


def normalized(fine_taps):
    energy = fine_taps[:, :, 0] ** 2 + 2.0 * jnp.sum(fine_taps[:, :, 1:] ** 2, axis=2)
    return fine_taps / jnp.sqrt(energy)[:, :, None]


def twice(taps):
    full = jnp.concatenate([taps[:, :0:-1], taps], axis=1)
    padded = jnp.pad(full, ((0, 0), (8, 8)))
    return jnp.stack(
        [jnp.sum(full * padded[:, 8 - o : 17 - o], axis=1) for o in range(9)], axis=1
    )


def local(perturbations, right_side, fine_taps, coarse_lat, coarse_lon):
    count, levels, height, extent = perturbations.shape
    members = count * lax.axis_size(MEM)
    scale = 1.0 / (members - 1)
    kernel = normalized(fine_taps)
    tile = lax.axis_index("tile").astype(jnp.int32).reshape(1)
    group = lax.axis_index(MEM).astype(jnp.int32).reshape(1)
    x = perturbations.reshape(count * levels * height, extent)
    r = right_side.reshape(levels * height, extent)
    full, half = ((256, LON), F32), ((128, LON), F32)
    coarse, edge = ((PAIRS, 8, 256), F32), ((PAIRS, 8, LON), F32)
    up = [(i, i + 1) for i in range(TILES - 1)]
    down = [(i + 1, i) for i in range(TILES - 1)]

    tables = call(
        table_kernel,
        [((256, 192), BF16), ((256, 192), BF16), ((4, 4, 3, 128, 128), BF16)],
        [SMEM] * 3,
        (tile, kernel[0], twice(kernel[1])),
        10**9,
    )

    def details(v):
        c, d, top, bottom = call(
            detail_kernel, [coarse, full, edge, edge], [VMEM] * 2, (x, v), 10**9
        )
        before = lax.ppermute(bottom, "tile", up)
        after = lax.ppermute(top, "tile", down)
        return exchange(c, "tile"), (x, d, before, after, *tables)

    c_first, fine_args = details(r)
    fine = call(
        functools.partial(fine_kernel, False), [half], [VMEM] * 7, fine_args, 5 * 10**9
    )
    smoothed = call(
        smooth_kernel, [coarse], [VMEM] * 3, (c_first, coarse_lat, coarse_lon), 10**8
    )
    smoothed = exchange(smoothed, "tile")
    shares = call(
        partial_kernel, [((GROUPS, 32, 128), F32)], [VMEM] * 3, (x, fine, smoothed), 10**9
    )
    arrived = exchange(shares, MEM)
    share = call(
        functools.partial(share_kernel, scale),
        [((GROUPS, 32, 128), F32)],
        [SMEM, VMEM, VMEM],
        (group, arrived, r),
        10**6,
    )
    a = exchange(share, MEM)

    c_next, fine_args = details(a)
    fine, sums = call(
        functools.partial(fine_kernel, True),
        [half, ((8, 128), F32)],
        [VMEM] * 9,
        (r, a, *fine_args),
        5 * 10**9,
    )
    smoothed = call(
        smooth_dots_kernel,
        [((TILES, 16, 256), F32)],
        [VMEM] * 5,
        (c_next, c_first, coarse_lat, coarse_lon, sums),
        10**8,
    )
    smoothed = exchange(smoothed, "tile")
    shares = call(
        last_partial_kernel, [((GROUPS, 40, 128), F32)], [VMEM] * 3, (x, fine, smoothed), 10**9
    )
    arrived = exchange(shares, MEM)
    out = ((levels, height, extent // GROUPS), F32)
    return tuple(
        call(
            functools.partial(final_kernel, scale),
            [out, out],
            [SMEM, VMEM, VMEM, VMEM],
            (group, arrived, r, a),
            10**6,
            scratch=(pltpu.VMEM((128, 128), F32), pltpu.VMEM((128, 128), F32)),
        )
    )


def solution(mesh):
    torus = Mesh(
        mesh.devices.reshape(4, 4, 2, mesh.shape["tile"]), ("mem_0", "mem_1", "mem_2", "tile")
    )
    placed = (P(MEM, None, "tile", None), P(None, "tile", None), P(), P(), P())
    return jax.shard_map(
        local,
        mesh=torus,
        in_specs=placed,
        out_specs=(P(None, "tile", MEM), P(None, "tile", MEM)),
        check_vma=False,
    )
```

```python
import functools

import jax
import jax.numpy as jnp
from jax import lax
from jax.experimental import pallas as pl
from jax.experimental.pallas import tpu as pltpu
from jax.sharding import Mesh
from jax.sharding import PartitionSpec as P

MEM = ("mem_0", "mem_1", "mem_2")
F32 = jnp.float32
BF16 = jnp.bfloat16
EXACT = lax.Precision.HIGHEST
PAIRS, ROWS, LON = 8, 32, 1024
GROUPS, TILES = 32, 8


def mm(a, b):
    return jnp.dot(a, b, preferred_element_type=F32)


def exact_mm(a, b):
    return jnp.dot(a, b, preferred_element_type=F32, precision=EXACT)


def split2(x):
    high = x.astype(BF16)
    return high, (x - high.astype(F32)).astype(BF16)


def split3(x):
    high = x.astype(BF16)
    rest = x - high.astype(F32)
    mid = rest.astype(BF16)
    return high, mid, (rest - mid.astype(F32)).astype(BF16)


def iotas(rows, cols):
    return (
        lax.broadcasted_iota(jnp.int32, (rows, cols), 0),
        lax.broadcasted_iota(jnp.int32, (rows, cols), 1),
    )


def shrink_table(rows, cols, along_rows):
    i, j = iotas(rows, cols)
    hit = (i >> 2) == j if along_rows else i == (j >> 2)
    return jnp.where(hit, 0.25, 0.0).astype(BF16)


def expand_table(rows, cols, along_rows):
    i, j = iotas(rows, cols)
    hit = (i >> 2) == j if along_rows else i == (j >> 2)
    return jnp.where(hit, 1.0, 0.0).astype(BF16)


def block_mean(w):
    table = shrink_table(64, 256, False)
    part = sum(mm(table, piece) for piece in split3(w))
    stacked = jnp.concatenate([part[:, :512], part[:, 512:]], axis=0)
    table = shrink_table(512, 128, True)
    small = sum(mm(piece, table) for piece in split3(stacked))
    return jnp.concatenate([small[:64], small[64:]], axis=1)


def prolong(c):
    table = expand_table(256, 64, True)
    tall = sum(mm(table, piece) for piece in split2(c))
    stacked = jnp.concatenate([tall[:, :128], tall[:, 128:]], axis=0)
    table = expand_table(128, 512, False)
    wide = sum(mm(piece, table) for piece in split2(stacked))
    return jnp.concatenate([wide[:256], wide[256:]], axis=1)


def natural(blocks):
    rows = []
    for tall in range(16):
        lanes = [
            blocks[2 * tall + wide // 4, 8 * (wide % 4) : 8 * (wide % 4) + 8, :]
            for wide in range(8)
        ]
        rows.append(jnp.concatenate(lanes, axis=1))
    return jnp.concatenate(rows, axis=0)


def detail_kernel(x_ref, v_ref, *out_refs):
    detail(x_ref[...], natural(v_ref), *out_refs)


def first_detail_kernel(x_hbm, v_hbm, *refs):
    *out_refs, x_ref, v_ref, x_sems, v_sems = refs
    copies = []
    for k in range(4):
        rows = pl.ds(32 * k, 32)
        copies.append(pltpu.make_async_copy(v_hbm.at[rows], v_ref.at[rows], v_sems.at[k]))
        rows = pl.ds(64 * k, 64)
        copies.append(pltpu.make_async_copy(x_hbm.at[rows], x_ref.at[rows], x_sems.at[k]))
    for copy in copies:
        copy.start()
    for copy in copies:
        copy.wait()
    detail(x_ref[...], v_ref[...], *out_refs)


def detail(x, v, c_ref, own_ref, top_ref, bottom_ref):
    w = x.astype(F32) * jnp.concatenate([v, v], axis=0)
    c = block_mean(w)
    if c_ref.shape == (TILES, 64, 256):
        for tile in range(TILES):
            c_ref[tile] = c
    else:
        c_ref[...] = c.reshape(PAIRS, 8, 256)
    own_ref[...] = c
    d = w - prolong(c)
    for pair in range(PAIRS):
        top_ref[pair] = d[ROWS * pair : ROWS * pair + 8]
        bottom_ref[pair] = d[ROWS * pair + 24 : ROWS * pair + 32]


def table_kernel(place_ref, taps_ref, lat_ref, *refs):
    *hbm_refs, mix_ref, high_ref, low_ref, band_ref, sems = refs
    tile = place_ref[0]
    taps = taps_ref[...]
    square = taps * taps
    energy = square[:, 0:1] + 2.0 * jnp.sum(square[:, 1:5], axis=1, keepdims=True)
    taps = taps / jnp.sqrt(energy)
    single = [taps[:, o : o + 1] for o in range(5)]
    once = [single[abs(o)] for o in range(-4, 5)]
    double = []
    for o in range(9):
        terms = [once[i] * once[o + 8 - i] for i in range(o, 9)]
        double.append(functools.reduce(jnp.add, terms))
    i, j = iotas(160, 192)
    first = jnp.zeros((160, 192), F32)
    for level in range(4):
        row, col = i - 40 * level, j - 48 * level
        dist = jnp.abs(col - row - 4)
        spot, source = tile * ROWS - 4 + row, tile * ROWS - 8 + col
        fits = (row >= 0) & (row < 40) & (col >= 0) & (col < 48)
        fits = fits & (spot >= 0) & (spot < ROWS * TILES)
        fits = fits & (source >= 0) & (source < ROWS * TILES)
        dist = jnp.where(fits, dist, 9)
        for o in range(5):
            first = jnp.where(dist == o, single[o][level : level + 1], first)
    i, j = iotas(128, 160)
    second = jnp.zeros((128, 160), F32)
    for level in range(4):
        row, col = i - 32 * level, j - 40 * level
        fits = (row >= 0) & (row < 32) & (col >= 0) & (col < 40)
        dist = jnp.where(fits, jnp.abs(col - row - 4), 9)
        for o in range(5):
            second = jnp.where(dist == o, single[o][level : level + 1], second)
    both = exact_mm(second, first)
    i, j = iotas(128, 128)
    mean = jnp.where((i >> 2) == (j >> 2), 0.25, 0.0)
    high, low = split2(jnp.concatenate([both, exact_mm(mean, both)], axis=0))
    high_ref[...] = high
    low_ref[...] = low
    i, j = iotas(8, 128)
    before = jnp.abs(i - 8 - j)
    after = jnp.abs(i + 128 - j)
    i, j = iotas(128, 128)
    inner = jnp.abs(i - j)
    for level in range(4):
        corner = (jnp.zeros((8, 128), F32), jnp.zeros((8, 128), F32))
        middle = jnp.zeros((128, 128), F32)
        for o in range(9):
            tap = double[o][4 + level : 5 + level]
            corner = tuple(
                jnp.where(dist == o, tap, c) for dist, c in zip((before, after), corner)
            )
            middle = jnp.where(inner == o, tap, middle)
        rest = jnp.zeros((120, 128), F32)
        bands = jnp.concatenate([rest, corner[0], middle, corner[1], rest], axis=0)
        parts = jnp.concatenate([corner[0], middle, corner[1]], axis=0)
        meant = -exact_mm(parts, mean)
        meant = jnp.concatenate([rest, meant, rest], axis=0)
        for kind, piece in enumerate((*split2(bands), *split2(meant))):
            band_ref[level, kind] = piece
    i, j = iotas(64, 512)
    repeat = jnp.where((i >> 3) == (j >> 6), jnp.where((i & 7) == (j & 7), 1.0, 0.0), 0.0)
    mine = lat_ref[pl.ds(pl.multiple_of(8 * tile, 8), 8), :]
    wide = exact_mm(mine, repeat)
    mix = jnp.concatenate([wide] * PAIRS, axis=0)
    mix_ref[...] = jnp.where((i >> 3) == ((j >> 3) & 7), mix, 0.0)
    copies = [
        pltpu.make_async_copy(source, target, sems.at[k])
        for k, (source, target) in enumerate(zip((high_ref, low_ref, band_ref), hbm_refs))
    ]
    for copy in copies:
        copy.start()
    for copy in copies:
        copy.wait()


def banded(band_ref, level, kind):
    band = band_ref[level, kind]
    zero = jnp.zeros((128, 128), BF16)
    left = jnp.concatenate([band, zero], axis=0)
    right = jnp.concatenate([zero, band], axis=0)
    return jnp.concatenate([left, right], axis=1)


def windows(parts, first_row):
    rows = []
    for block in range(4):
        for part in parts:
            lanes = [
                part[first_row : first_row + ROWS, 128 * tile : 128 * tile + 128]
                for tile in ((2 * block - 1) % 8, 2 * block, 2 * block + 1, (2 * block + 2) % 8)
            ]
            rows.append(jnp.concatenate(lanes, axis=1))
    return jnp.concatenate(rows, axis=0)


def lane_sums(values):
    i, j = iotas(8, 128)
    result = jnp.zeros((8, 128), F32)
    for lane, value in values:
        result = jnp.where((i == 0) & (j == lane), value, result)
    return result


def total(x):
    return jnp.sum(x, axis=(0, 1), keepdims=True)


def fine_kernel(last, *refs):
    if last:
        r_ref, *refs = refs
    v_ref, x_ref, c_ref, before_ref, after_ref, *refs = refs
    *refs, high_ref, low_ref, band_ref, sems = refs
    copies = [
        pltpu.make_async_copy(source, target, sems.at[k])
        for k, (source, target) in enumerate(zip(refs[:3], (high_ref, low_ref, band_ref)))
    ]
    for copy in copies:
        copy.start()
    outs = refs[3:]
    fine_ref = outs[0]
    v = natural(v_ref) if last else v_ref[...]
    d = x_ref[...].astype(F32) * jnp.concatenate([v, v], axis=0) - prolong(c_ref[...])
    copies[0].wait()
    copies[1].wait()
    highs, lows = [], []
    for member in range(2):
        rows = []
        for level in range(4):
            pair = 4 * member + level
            rows += [before_ref[pair], d[ROWS * pair : ROWS * pair + ROWS], after_ref[pair]]
        high, low = split2(jnp.concatenate(rows, axis=0))
        passed = mm(high_ref[...], high) + mm(high_ref[...], low) + mm(low_ref[...], high)
        high, low = split2(passed)
        highs.append(high)
        lows.append(low)
    copies[2].wait()
    for level in range(4):
        result = None
        for kind in range(2):
            high = windows(highs, 128 * kind + ROWS * level)
            low = windows(lows, 128 * kind + ROWS * level)
            table_high = banded(band_ref, level, 2 * kind)
            table_low = banded(band_ref, level, 2 * kind + 1)
            term = mm(high, table_high) + mm(low, table_high) + mm(high, table_low)
            result = term if result is None else result + term
        for block in range(4):
            summed = None
            for member in range(2):
                row = ROWS * (4 * member + level)
                x = x_ref[row : row + ROWS, 256 * block : 256 * block + 256].astype(F32)
                at = 64 * block + ROWS * member
                term = x * result[at : at + ROWS]
                summed = term if summed is None else summed + term
            fine_ref[ROWS * level : ROWS * level + ROWS, 256 * block : 256 * block + 256] = summed
    if last:
        r, fine = r_ref[...], fine_ref[...]
        pairs = ((r, r), (r, v), (v, v), (r, fine), (v, fine))
        outs[1][...] = lane_sums([(k, total(p * q)) for k, (p, q) in enumerate(pairs)])


def smooth_dots_kernel(c_ref, first_ref, lat_ref, lon_ref, sums_ref, out_ref):
    c = c_ref[...].reshape(64, 256)
    first = first_ref[...]
    smoothed = exact_mm(exact_mm(lat_ref[...], c), lon_ref[...])
    dots = (total(first * smoothed), total(c * smoothed))
    sums = sums_ref[...] + lane_sums([(5 + k, dot * 16.0) for k, dot in enumerate(dots)])
    for tile in range(TILES):
        out_ref[tile, 0:8, :] = smoothed[8 * tile : 8 * tile + 8, :128]
        out_ref[tile, 8:16, :] = smoothed[8 * tile : 8 * tile + 8, 128:]
        out_ref[tile, 16:24, :] = sums


def blended(x_ref, fine_ref, smoothed):
    spread = prolong(smoothed)
    return (
        fine_ref[...]
        + x_ref[:128].astype(F32) * spread[:128]
        + x_ref[128:].astype(F32) * spread[128:]
    )


def partial_kernel(place_ref, x_ref, fine_ref, c_ref, mix_ref, lon_ref, out_ref, mine_ref):
    mine = pl.ds(pl.multiple_of(8 * place_ref[0], 8), 8)
    for tile in range(TILES):
        mine_ref[8 * tile : 8 * tile + 8, :] = c_ref[tile, mine, :]
    across = exact_mm(mix_ref[...], c_ref[...].reshape(512, 256))
    p = blended(x_ref, fine_ref, exact_mm(across, lon_ref[...]))
    for tall in range(16):
        for wide in range(8):
            out_ref[2 * tall + wide // 4, 8 * (wide % 4) : 8 * (wide % 4) + 8, :] = p[
                8 * tall : 8 * tall + 8, 128 * wide : 128 * wide + 128
            ]


def last_partial_kernel(x_ref, fine_ref, smoothed_ref, out_ref):
    halves = [smoothed_ref[:, 8 * k : 8 * k + 8, :].reshape(64, 128) for k in range(2)]
    p = blended(x_ref, fine_ref, jnp.concatenate(halves, axis=1))
    turned = p.T
    sums = jnp.sum(smoothed_ref[:, 16:24, :], axis=0)
    for group in range(GROUPS):
        out_ref[group, :32, :] = turned[32 * group : 32 * group + 32]
        out_ref[group, 32:40, :] = sums


def share_kernel(scale, place_ref, arrived_ref, r_ref, out_ref):
    group = place_ref[1]
    share = r_ref[
        pl.ds(pl.multiple_of(8 * (group >> 1), 8), 8),
        pl.ds(pl.multiple_of(512 * (group & 1), 512), 512),
    ]
    share = jnp.concatenate([share[:, 128 * k : 128 * k + 128] for k in range(4)], axis=0)
    share = share + jnp.sum(arrived_ref[...], axis=0) * scale
    for other in range(GROUPS):
        out_ref[other] = share


def final_kernel(scale, place_ref, arrived_ref, r_ref, a_ref, x_out, res_out, r_turned, a_turned):
    group = place_ref[1]
    wide = group >> 2
    lanes = pl.ds(pl.multiple_of(128 * wide, 128), 128)
    r_turned[...] = r_ref[:, lanes].T
    rows = [
        a_ref[2 * tall + (wide >> 2), pl.ds(pl.multiple_of(8 * (wide & 3), 8), 8), :]
        for tall in range(16)
    ]
    a_turned[...] = jnp.concatenate(rows, axis=0).T
    mine = pl.ds(pl.multiple_of(32 * (group & 3), 32), 32)
    r, a = r_turned[mine, :], a_turned[mine, :]
    arrived = jnp.sum(arrived_ref[...], axis=0)
    b = a + arrived[:32] * scale
    i, j = iotas(8, 128)
    rr, ra, aa, rf, af, rc, ac = (
        total(jnp.where((i == 0) & (j == k), arrived[32:40], 0.0)) for k in range(7)
    )
    rr, ra, aa = rr / GROUPS, ra / GROUPS, aa / GROUPS
    step = rr / ra
    rb = ra + (rf + rc) * scale
    ab = aa + (af + ac) * scale
    squares = step * step * aa - rr
    next_step = squares / ((ra - step * aa) - step * (rb - step * ab))
    r_next = r - step * a
    x_out[...] = (step * r + next_step * r_next).T.reshape(4, ROWS, 32)
    res_out[...] = (r_next - next_step * (a - step * b)).T.reshape(4, ROWS, 32)


VMEM = pl.BlockSpec(memory_space=pltpu.VMEM)
SMEM = pl.BlockSpec(memory_space=pltpu.SMEM)
HBM = pl.BlockSpec(memory_space=pltpu.HBM)


def call(kernel, outs, specs, args, flops, limit, scratch=(), out_specs=None):
    out_specs = out_specs or [VMEM] * len(outs)
    shapes = [
        pltpu.HBM(*out) if spec is HBM else jax.ShapeDtypeStruct(*out)
        for out, spec in zip(outs, out_specs)
    ]
    size = sum(a.size * a.dtype.itemsize for a in args)
    args = [
        pltpu.with_memory_space_constraint(arg, pltpu.HBM) if spec is HBM else arg
        for arg, spec in zip(args, specs)
    ]
    return pl.pallas_call(
        kernel,
        out_shape=shapes if len(shapes) > 1 else shapes[0],
        in_specs=specs,
        out_specs=out_specs if len(shapes) > 1 else out_specs[0],
        scratch_shapes=list(scratch),
        compiler_params=pltpu.CompilerParams(vmem_limit_bytes=limit << 20),
        cost_estimate=pl.CostEstimate(flops=flops, bytes_accessed=size, transcendentals=0),
    )(*args)


def exchange(blocks, axis):
    return lax.all_to_all(blocks, axis, 0, 0, tiled=True)


def local(perturbations, right_side, fine_taps, coarse_lat, coarse_lon):
    count, levels, height, extent = perturbations.shape
    members = count * lax.axis_size(MEM)
    scale = 1.0 / (members - 1)
    place = jnp.stack([lax.axis_index("tile"), lax.axis_index(MEM)]).astype(jnp.int32)
    x = perturbations.reshape(count * levels * height, extent)
    r = right_side.reshape(levels * height, extent)
    half = ((128, LON), F32)
    edge = ((PAIRS, 8, LON), F32)
    shared = ((GROUPS, 32, 128), F32)
    up = [(i, (i + 1) % TILES) for i in range(TILES)]
    down = [(j, i) for i, j in up]

    def edges(top, bottom):
        return lax.ppermute(bottom, "tile", up), lax.ppermute(top, "tile", down)

    own = ((64, 256), F32)
    c, c_own, top, bottom = call(
        first_detail_kernel,
        [((TILES, 64, 256), F32), own, edge, edge],
        [HBM] * 2,
        (x, r),
        10**9,
        12,
        scratch=(
            pltpu.VMEM((256, LON), BF16),
            pltpu.VMEM((128, LON), F32),
            pltpu.SemaphoreType.DMA((4,)),
            pltpu.SemaphoreType.DMA((4,)),
        ),
    )
    c_first = exchange(c, "tile")
    table_shapes = [((256, 192), BF16), ((256, 192), BF16), ((4, 4, 384, 128), BF16)]
    table_scratch = [pltpu.VMEM(*shape) for shape in table_shapes]
    table_scratch.append(pltpu.SemaphoreType.DMA((3,)))
    *tables, mix = call(
        table_kernel,
        table_shapes + [((64, 512), F32)],
        [SMEM, VMEM, VMEM],
        (place, fine_taps.reshape(2 * levels, 5), coarse_lat),
        10**9,
        8,
        scratch=table_scratch,
        out_specs=[HBM] * 3 + [VMEM],
    )
    fine = call(
        functools.partial(fine_kernel, False),
        [half],
        [VMEM] * 5 + [HBM] * 3,
        (r, x, c_own, *edges(top, bottom), *tables),
        5 * 10**9,
        16,
        scratch=table_scratch,
    )
    shares, c_first = call(
        partial_kernel,
        [shared, own],
        [SMEM] + [VMEM] * 5,
        (place, x, fine, c_first, mix, coarse_lon),
        10**9,
        12,
    )
    arrived = exchange(shares, MEM)
    share = call(
        functools.partial(share_kernel, scale),
        [shared],
        [SMEM, VMEM, VMEM],
        (place, arrived, r),
        10**6,
        6,
    )
    a = exchange(share, MEM)

    c, c_own, top, bottom = call(
        detail_kernel,
        [((PAIRS, 8, 256), F32), own, edge, edge],
        [VMEM] * 2,
        (x, a),
        10**9,
        12,
    )
    beside = edges(top, bottom)
    c = exchange(c, "tile")
    fine, sums = call(
        functools.partial(fine_kernel, True),
        [half, ((8, 128), F32)],
        [VMEM] * 6 + [HBM] * 3,
        (r, a, x, c_own, *beside, *tables),
        5 * 10**9,
        16,
        scratch=table_scratch,
    )
    smoothed = call(
        smooth_dots_kernel,
        [((TILES, 24, 128), F32)],
        [VMEM] * 5,
        (c, c_first, coarse_lat, coarse_lon, sums),
        10**8,
        6,
    )
    smoothed = exchange(smoothed, "tile")
    shares = call(
        last_partial_kernel, [((GROUPS, 40, 128), F32)], [VMEM] * 3, (x, fine, smoothed), 10**9, 12
    )
    arrived = exchange(shares, MEM)
    out = ((levels, height, extent // GROUPS), F32)
    return tuple(
        call(
            functools.partial(final_kernel, scale),
            [out, out],
            [SMEM, VMEM, VMEM, VMEM],
            (place, arrived, r, a),
            10**6,
            6,
            scratch=(pltpu.VMEM((128, 128), F32), pltpu.VMEM((128, 128), F32)),
        )
    )


def solution(mesh):
    torus = Mesh(
        mesh.devices.reshape(4, 4, 2, mesh.shape["tile"]), ("mem_0", "mem_1", "mem_2", "tile")
    )
    placed = (P(MEM, None, "tile", None), P(None, "tile", None), P(), P(), P())
    return jax.shard_map(
        local,
        mesh=torus,
        in_specs=placed,
        out_specs=(P(None, "tile", MEM), P(None, "tile", MEM)),
        check_vma=False,
    )
```

```python
import functools

import jax
import jax.numpy as jnp
from jax import lax
from jax.experimental import pallas as pl
from jax.experimental.pallas import tpu as pltpu
from jax.sharding import Mesh
from jax.sharding import PartitionSpec as P

MEM = ("mem_0", "mem_1", "mem_2")
F32 = jnp.float32
BF16 = jnp.bfloat16
EXACT = lax.Precision.HIGHEST
PAIRS, ROWS, LON = 8, 32, 1024
GROUPS, TILES = 32, 8


def mm(a, b):
    return jnp.dot(a, b, preferred_element_type=F32)


def exact_mm(a, b):
    return jnp.dot(a, b, preferred_element_type=F32, precision=EXACT)


def split2(x):
    high = x.astype(BF16)
    return high, (x - high.astype(F32)).astype(BF16)


def split3(x):
    high = x.astype(BF16)
    rest = x - high.astype(F32)
    mid = rest.astype(BF16)
    return high, mid, (rest - mid.astype(F32)).astype(BF16)


def iotas(rows, cols):
    return (
        lax.broadcasted_iota(jnp.int32, (rows, cols), 0),
        lax.broadcasted_iota(jnp.int32, (rows, cols), 1),
    )


def shrink_table(rows, cols, along_rows):
    i, j = iotas(rows, cols)
    hit = (i >> 2) == j if along_rows else i == (j >> 2)
    return jnp.where(hit, 0.25, 0.0).astype(BF16)


def expand_table(rows, cols, along_rows):
    i, j = iotas(rows, cols)
    hit = (i >> 2) == j if along_rows else i == (j >> 2)
    return jnp.where(hit, 1.0, 0.0).astype(BF16)


def block_mean(w, split):
    table = shrink_table(64, 256, False)
    part = sum(mm(table, piece) for piece in split(w))
    stacked = jnp.concatenate([part[:, :512], part[:, 512:]], axis=0)
    table = shrink_table(512, 128, True)
    small = sum(mm(piece, table) for piece in split(stacked))
    return jnp.concatenate([small[:64], small[64:]], axis=1)


def prolong(c, edges=False):
    if edges:
        i, j = iotas(128, 64)
        spot = 8 * (i >> 4) + ((i & 15) >> 2) + 4 * ((i & 15) >> 3)
        table = jnp.where(spot == j, 1.0, 0.0).astype(BF16)
    else:
        table = expand_table(256, 64, True)
    rows = table.shape[0]
    tall = sum(mm(table, piece) for piece in split2(c))
    stacked = jnp.concatenate([tall[:, :128], tall[:, 128:]], axis=0)
    table = expand_table(128, 512, False)
    wide = sum(mm(piece, table) for piece in split2(stacked))
    return jnp.concatenate([wide[:rows], wide[rows:]], axis=1)


def natural(blocks):
    rows = []
    for tall in range(16):
        lanes = [
            blocks[2 * tall + wide // 4, 8 * (wide % 4) : 8 * (wide % 4) + 8, :]
            for wide in range(8)
        ]
        rows.append(jnp.concatenate(lanes, axis=1))
    return jnp.concatenate(rows, axis=0)


def detail_kernel(x_ref, v_ref, *out_refs):
    detail(x_ref[...], natural(v_ref), *out_refs)


def first_detail_kernel(x_hbm, v_hbm, *refs):
    *out_refs, x_ref, v_ref, x_sems, v_sems = refs
    copies = []
    for k in range(8):
        rows = pl.ds(16 * k, 16)
        copies.append(pltpu.make_async_copy(v_hbm.at[rows], v_ref.at[rows], v_sems.at[k]))
        rows = pl.ds(32 * k, 32)
        copies.append(pltpu.make_async_copy(x_hbm.at[rows], x_ref.at[rows], x_sems.at[k]))
    for copy in copies:
        copy.start()
    for copy in copies:
        copy.wait()
    detail(x_ref[...], v_ref[...], *out_refs)


def detail(x, v, c_ref, own_ref, top_ref, bottom_ref):
    w = x.astype(F32) * jnp.concatenate([v, v], axis=0)
    c = block_mean(w, split3)
    if c_ref.shape == (TILES, 64, 256):
        for tile in range(TILES):
            c_ref[tile] = c
    else:
        c_ref[...] = c.reshape(PAIRS, 8, 256)
    own_ref[...] = c
    spread = prolong(c, edges=True)
    for pair in range(PAIRS):
        at = ROWS * pair
        top_ref[pair] = w[at : at + 8] - spread[16 * pair : 16 * pair + 8]
        bottom_ref[pair] = w[at + 24 : at + 32] - spread[16 * pair + 8 : 16 * pair + 16]


def table_kernel(place_ref, taps_ref, lat_ref, *refs):
    rows_ref, band_ref, mix_ref = refs
    tile = place_ref[0]
    taps = taps_ref[...]
    square = taps * taps
    energy = square[:, 0:1] + 2.0 * jnp.sum(square[:, 1:5], axis=1, keepdims=True)
    taps = taps / jnp.sqrt(energy)
    single = [taps[:, o : o + 1] for o in range(5)]
    once = [single[abs(o)] for o in range(-4, 5)]
    double = []
    for o in range(9):
        terms = [once[i] * once[o + 8 - i] for i in range(o, 9)]
        double.append(functools.reduce(jnp.add, terms))
    i, j = iotas(160, 192)
    first = jnp.zeros((160, 192), F32)
    for level in range(4):
        row, col = i - 40 * level, j - 48 * level
        dist = jnp.abs(col - row - 4)
        spot, source = tile * ROWS - 4 + row, tile * ROWS - 8 + col
        fits = (row >= 0) & (row < 40) & (col >= 0) & (col < 48)
        fits = fits & (spot >= 0) & (spot < ROWS * TILES)
        fits = fits & (source >= 0) & (source < ROWS * TILES)
        dist = jnp.where(fits, dist, 9)
        for o in range(5):
            first = jnp.where(dist == o, single[o][level : level + 1], first)
    i, j = iotas(128, 160)
    second = jnp.zeros((128, 160), F32)
    for level in range(4):
        row, col = i - 32 * level, j - 40 * level
        fits = (row >= 0) & (row < 32) & (col >= 0) & (col < 40)
        dist = jnp.where(fits, jnp.abs(col - row - 4), 9)
        for o in range(5):
            second = jnp.where(dist == o, single[o][level : level + 1], second)
    both = exact_mm(second, first)
    for kind, piece in enumerate(split2(both)):
        rows_ref[kind] = piece
    i, j = iotas(8, 128)
    before = jnp.abs(i - 8 - j)
    after = jnp.abs(i + 128 - j)
    i, j = iotas(128, 128)
    inner = jnp.abs(i - j)
    for level in range(4):
        corner = (jnp.zeros((8, 128), F32), jnp.zeros((8, 128), F32))
        middle = jnp.zeros((128, 128), F32)
        for o in range(9):
            tap = double[o][4 + level : 5 + level]
            corner = tuple(
                jnp.where(dist == o, tap, c) for dist, c in zip((before, after), corner)
            )
            middle = jnp.where(inner == o, tap, middle)
        rest = jnp.zeros((8, 128), F32)
        band = jnp.concatenate([rest, corner[0], middle, corner[1], rest], axis=0)
        for kind, piece in enumerate(split2(band)):
            band_ref[level, kind] = piece
    i, j = iotas(64, 512)
    repeat = jnp.where((i >> 3) == (j >> 6), jnp.where((i & 7) == (j & 7), 1.0, 0.0), 0.0)
    mine = lat_ref[pl.ds(pl.multiple_of(8 * tile, 8), 8), :]
    wide = exact_mm(mine, repeat)
    mix = jnp.concatenate([wide] * PAIRS, axis=0)
    mix_ref[...] = jnp.where((i >> 3) == ((j >> 3) & 7), mix, 0.0)


def banded(band_ref, level, kind):
    band = band_ref[level, kind]
    edge, half = jnp.zeros((112, 128), BF16), jnp.zeros((128, 128), BF16)
    left = jnp.concatenate([edge, band, edge, half], axis=0)
    right = jnp.concatenate([half, edge, band, edge], axis=0)
    return jnp.concatenate([left, right], axis=1)


def windows(parts, first_row):
    rows = []
    for block in range(4):
        for part in parts:
            lanes = [
                part[first_row : first_row + ROWS, 128 * tile : 128 * tile + 128]
                for tile in ((2 * block - 1) % 8, 2 * block, 2 * block + 1, (2 * block + 2) % 8)
            ]
            rows.append(jnp.concatenate(lanes, axis=1))
    return jnp.concatenate(rows, axis=0)


def lane_sums(values):
    i, j = iotas(8, 128)
    result = jnp.zeros((8, 128), F32)
    for lane, value in values:
        result = jnp.where((i == 0) & (j == lane), value, result)
    return result


def total(x):
    return jnp.sum(x, axis=(0, 1), keepdims=True)


def fine_kernel(last, *refs):
    if last:
        r_ref, *refs = refs
    v_ref, x_ref, c_ref, before_ref, after_ref, rows_ref, band_ref, *refs = refs
    fine_ref, mean_ref, *refs = refs
    f_ref = refs[-1]
    v = natural(v_ref) if last else v_ref[...]
    d = x_ref[...].astype(F32) * jnp.concatenate([v, v], axis=0) - prolong(c_ref[...])
    highs, lows = [], []
    for member in range(2):
        rows = []
        for level in range(4):
            pair = 4 * member + level
            rows += [before_ref[pair], d[ROWS * pair : ROWS * pair + ROWS], after_ref[pair]]
        high, low = split2(jnp.concatenate(rows, axis=0))
        passed = mm(rows_ref[0], high) + mm(rows_ref[0], low) + mm(rows_ref[1], high)
        high, low = split2(passed)
        highs.append(high)
        lows.append(low)
    for level in range(4):
        high = windows(highs, ROWS * level)
        low = windows(lows, ROWS * level)
        table_high, table_low = banded(band_ref, level, 0), banded(band_ref, level, 1)
        result = mm(high, table_high) + mm(low, table_high) + mm(high, table_low)
        for block in range(4):
            lanes = slice(256 * block, 256 * block + 256)
            summed = None
            for member in range(2):
                row = ROWS * (4 * member + level)
                at = 64 * block + ROWS * member
                f = result[at : at + ROWS]
                f_ref[row : row + ROWS, lanes] = f
                term = x_ref[row : row + ROWS, lanes].astype(F32) * f
                summed = term if summed is None else summed + term
            fine_ref[ROWS * level : ROWS * level + ROWS, lanes] = summed
    means = block_mean(f_ref[...], split2)
    mean_ref[...] = means
    if last:
        r = r_ref[...]
        products = total(v * fine_ref[...]) - 16.0 * total(c_ref[...] * means)
        refs[0][...] = lane_sums(
            ((0, total(r * r)), (1, total(r * v)), (2, total(v * v)), (3, products))
        )


def smooth_kernel(c_ref, lat_ref, lon_ref, sums_ref, out_ref):
    c = c_ref[...].reshape(64, 256)
    smoothed = exact_mm(exact_mm(lat_ref[...], c), lon_ref[...])
    sums = sums_ref[...] + lane_sums([(4, 16.0 * total(c * smoothed))])
    for tile in range(TILES):
        out_ref[tile, 0:8, :] = smoothed[8 * tile : 8 * tile + 8, :128]
        out_ref[tile, 8:16, :] = smoothed[8 * tile : 8 * tile + 8, 128:]
        out_ref[tile, 16:24, :] = sums


def blended(x_ref, fine_ref, smoothed):
    spread = prolong(smoothed)
    return (
        fine_ref[...]
        + x_ref[:128].astype(F32) * spread[:128]
        + x_ref[128:].astype(F32) * spread[128:]
    )


def partial_kernel(x_ref, fine_ref, mean_ref, c_ref, mix_ref, lon_ref, out_ref):
    across = exact_mm(mix_ref[...], c_ref[...].reshape(512, 256))
    p = blended(x_ref, fine_ref, exact_mm(across, lon_ref[...]) - mean_ref[...])
    for tall in range(16):
        for wide in range(8):
            out_ref[2 * tall + wide // 4, 8 * (wide % 4) : 8 * (wide % 4) + 8, :] = p[
                8 * tall : 8 * tall + 8, 128 * wide : 128 * wide + 128
            ]


def last_partial_kernel(x_ref, fine_ref, mean_ref, smoothed_ref, out_ref):
    halves = [smoothed_ref[:, 8 * k : 8 * k + 8, :].reshape(64, 128) for k in range(2)]
    p = blended(x_ref, fine_ref, jnp.concatenate(halves, axis=1) - mean_ref[...])
    turned = p.T
    sums = jnp.sum(smoothed_ref[:, 16:24, :], axis=0)
    for group in range(GROUPS):
        out_ref[group, :32, :] = turned[32 * group : 32 * group + 32]
        out_ref[group, 32:40, :] = sums


def share_kernel(scale, place_ref, arrived_ref, r_ref, out_ref):
    group = place_ref[1]
    share = r_ref[
        pl.ds(pl.multiple_of(8 * (group >> 1), 8), 8),
        pl.ds(pl.multiple_of(512 * (group & 1), 512), 512),
    ]
    share = jnp.concatenate([share[:, 128 * k : 128 * k + 128] for k in range(4)], axis=0)
    share = share + jnp.sum(arrived_ref[...], axis=0) * scale
    for other in range(GROUPS):
        out_ref[other] = share


def final_kernel(scale, place_ref, arrived_ref, r_ref, a_ref, x_out, res_out, r_turned, a_turned):
    group = place_ref[1]
    wide = group >> 2
    lanes = pl.ds(pl.multiple_of(128 * wide, 128), 128)
    r_turned[...] = r_ref[:, lanes].T
    rows = [
        a_ref[2 * tall + (wide >> 2), pl.ds(pl.multiple_of(8 * (wide & 3), 8), 8), :]
        for tall in range(16)
    ]
    a_turned[...] = jnp.concatenate(rows, axis=0).T
    mine = pl.ds(pl.multiple_of(32 * (group & 3), 32), 32)
    r, a = r_turned[mine, :], a_turned[mine, :]
    arrived = jnp.sum(arrived_ref[...], axis=0)
    b = a + arrived[:32] * scale
    i, j = iotas(8, 128)
    rr, ra, aa, af, ac = (
        total(jnp.where((i == 0) & (j == k), arrived[32:40], 0.0)) for k in range(5)
    )
    rr, ra, aa = rr / GROUPS, ra / GROUPS, aa / GROUPS
    step = rr / ra
    ab = aa + (af + ac) * scale
    squares = step * step * aa - rr
    next_step = squares / ((ra - step * aa) - step * (aa - step * ab))
    r_next = r - step * a
    x_out[...] = (step * r + next_step * r_next).T.reshape(4, ROWS, 32)
    res_out[...] = (r_next - next_step * (a - step * b)).T.reshape(4, ROWS, 32)


VMEM = pl.BlockSpec(memory_space=pltpu.VMEM)
SMEM = pl.BlockSpec(memory_space=pltpu.SMEM)
HBM = pl.BlockSpec(memory_space=pltpu.HBM)


def call(kernel, outs, specs, args, flops, limit, scratch=(), out_specs=None):
    out_specs = out_specs or [VMEM] * len(outs)
    shapes = [
        pltpu.HBM(*out) if spec is HBM else jax.ShapeDtypeStruct(*out)
        for out, spec in zip(outs, out_specs)
    ]
    size = sum(a.size * a.dtype.itemsize for a in args)
    args = [
        pltpu.with_memory_space_constraint(arg, pltpu.HBM) if spec is HBM else arg
        for arg, spec in zip(args, specs)
    ]
    return pl.pallas_call(
        kernel,
        out_shape=shapes if len(shapes) > 1 else shapes[0],
        in_specs=specs,
        out_specs=out_specs if len(shapes) > 1 else out_specs[0],
        scratch_shapes=list(scratch),
        compiler_params=pltpu.CompilerParams(vmem_limit_bytes=limit << 20),
        cost_estimate=pl.CostEstimate(flops=flops, bytes_accessed=size, transcendentals=0),
    )(*args)


def exchange(blocks, axis):
    return lax.all_to_all(blocks, axis, 0, 0, tiled=True)


def local(perturbations, right_side, fine_taps, coarse_lat, coarse_lon):
    count, levels, height, extent = perturbations.shape
    members = count * lax.axis_size(MEM)
    scale = 1.0 / (members - 1)
    place = jnp.stack([lax.axis_index("tile"), lax.axis_index(MEM)]).astype(jnp.int32)
    x = perturbations.reshape(count * levels * height, extent)
    r = right_side.reshape(levels * height, extent)
    half = ((128, LON), F32)
    edge = ((PAIRS, 8, LON), F32)
    shared = ((GROUPS, 32, 128), F32)
    up = [(i, (i + 1) % TILES) for i in range(TILES)]
    down = [(j, i) for i, j in up]

    def edges(top, bottom):
        return lax.ppermute(bottom, "tile", up), lax.ppermute(top, "tile", down)

    own = ((64, 256), F32)
    c, c_own, top, bottom = call(
        first_detail_kernel,
        [((TILES, 64, 256), F32), own, edge, edge],
        [HBM] * 2,
        (x, r),
        10**9,
        12,
        scratch=(
            pltpu.VMEM((256, LON), BF16),
            pltpu.VMEM((128, LON), F32),
            pltpu.SemaphoreType.DMA((8,)),
            pltpu.SemaphoreType.DMA((8,)),
        ),
    )
    c_first = exchange(c, "tile")
    *tables, mix = call(
        table_kernel,
        [
            ((2, 128, 192), BF16),
            ((levels, 2, 160, 128), BF16),
            ((64, 512), F32),
        ],
        [SMEM, VMEM, VMEM],
        (place, fine_taps.reshape(2 * levels, 5), coarse_lat),
        10**9,
        6,
    )
    fine_scratch = [pltpu.VMEM((256, LON), F32)]
    fine, means = call(
        functools.partial(fine_kernel, False),
        [half, own],
        [VMEM] * 7,
        (r, x, c_own, *edges(top, bottom), *tables),
        10**11,
        16,
        scratch=fine_scratch,
    )
    shares = call(
        partial_kernel,
        [shared],
        [VMEM] * 6,
        (x, fine, means, c_first, mix, coarse_lon),
        10**9,
        12,
    )
    arrived = exchange(shares, MEM)
    share = call(
        functools.partial(share_kernel, scale),
        [shared],
        [SMEM, VMEM, VMEM],
        (place, arrived, r),
        10**6,
        6,
    )
    a = exchange(share, MEM)

    c, c_own, top, bottom = call(
        detail_kernel,
        [((PAIRS, 8, 256), F32), own, edge, edge],
        [VMEM] * 2,
        (x, a),
        10**9,
        12,
    )
    beside = edges(top, bottom)
    c = exchange(c, "tile")
    fine, means, sums = call(
        functools.partial(fine_kernel, True),
        [half, own, ((8, 128), F32)],
        [VMEM] * 8,
        (r, a, x, c_own, *beside, *tables),
        10**11,
        16,
        scratch=fine_scratch,
    )
    smoothed = call(
        smooth_kernel,
        [((TILES, 24, 128), F32)],
        [VMEM] * 4,
        (c, coarse_lat, coarse_lon, sums),
        10**8,
        6,
    )
    smoothed = exchange(smoothed, "tile")
    shares = call(
        last_partial_kernel,
        [((GROUPS, 40, 128), F32)],
        [VMEM] * 4,
        (x, fine, means, smoothed),
        10**9,
        12,
    )
    arrived = exchange(shares, MEM)
    out = ((levels, height, extent // GROUPS), F32)
    return tuple(
        call(
            functools.partial(final_kernel, scale),
            [out, out],
            [SMEM, VMEM, VMEM, VMEM],
            (place, arrived, r, a),
            10**6,
            6,
            scratch=(pltpu.VMEM((128, 128), F32), pltpu.VMEM((128, 128), F32)),
        )
    )


def solution(mesh):
    torus = Mesh(
        mesh.devices.reshape(4, 4, 2, mesh.shape["tile"]), ("mem_0", "mem_1", "mem_2", "tile")
    )
    placed = (P(MEM, None, "tile", None), P(None, "tile", None), P(), P(), P())
    return jax.shard_map(
        local,
        mesh=torus,
        in_specs=placed,
        out_specs=(P(None, "tile", MEM), P(None, "tile", MEM)),
        check_vma=False,
    )
```

```python
import functools

import jax
import jax.numpy as jnp
from jax import lax
from jax.experimental import pallas as pl
from jax.experimental.pallas import tpu as pltpu
from jax.sharding import Mesh
from jax.sharding import PartitionSpec as P

MEM = ("mem_0", "mem_1", "mem_2")
F32 = jnp.float32
BF16 = jnp.bfloat16
EXACT = lax.Precision.HIGHEST
PAIRS, ROWS, LON = 8, 32, 1024
GROUPS, TILES = 32, 8


def mm(a, b):
    return jnp.dot(a, b, preferred_element_type=F32)


def exact_mm(a, b):
    return jnp.dot(a, b, preferred_element_type=F32, precision=EXACT)


def split2(x):
    high = x.astype(BF16)
    return high, (x - high.astype(F32)).astype(BF16)


def split3(x):
    high = x.astype(BF16)
    rest = x - high.astype(F32)
    mid = rest.astype(BF16)
    return high, mid, (rest - mid.astype(F32)).astype(BF16)


def iotas(rows, cols):
    return (
        lax.broadcasted_iota(jnp.int32, (rows, cols), 0),
        lax.broadcasted_iota(jnp.int32, (rows, cols), 1),
    )


def shrink_table(rows, cols, along_rows):
    i, j = iotas(rows, cols)
    hit = (i >> 2) == j if along_rows else i == (j >> 2)
    return jnp.where(hit, 0.25, 0.0).astype(BF16)


def expand_table(rows, cols, along_rows):
    i, j = iotas(rows, cols)
    hit = (i >> 2) == j if along_rows else i == (j >> 2)
    return jnp.where(hit, 1.0, 0.0).astype(BF16)


def block_mean(w, split):
    table = shrink_table(64, 256, False)
    part = sum(mm(table, piece) for piece in split(w))
    stacked = jnp.concatenate([part[:, :512], part[:, 512:]], axis=0)
    table = shrink_table(512, 128, True)
    small = sum(mm(piece, table) for piece in split(stacked))
    return jnp.concatenate([small[:64], small[64:]], axis=1)


def prolong(c, edges=False):
    if edges:
        i, j = iotas(128, 64)
        spot = 8 * (i >> 4) + ((i & 15) >> 2) + 4 * ((i & 15) >> 3)
        table = jnp.where(spot == j, 1.0, 0.0).astype(BF16)
    else:
        table = expand_table(256, 64, True)
    rows = table.shape[0]
    tall = sum(mm(table, piece) for piece in split2(c))
    stacked = jnp.concatenate([tall[:, :128], tall[:, 128:]], axis=0)
    table = expand_table(128, 512, False)
    wide = sum(mm(piece, table) for piece in split2(stacked))
    return jnp.concatenate([wide[:rows], wide[rows:]], axis=1)


def natural(blocks):
    rows = []
    for tall in range(blocks.shape[0] // 2):
        lanes = [
            blocks[2 * tall + wide // 4, 8 * (wide % 4) : 8 * (wide % 4) + 8, :]
            for wide in range(8)
        ]
        rows.append(jnp.concatenate(lanes, axis=1))
    return jnp.concatenate(rows, axis=0)


def for_each(v):
    return jnp.concatenate([v] * (256 // v.shape[0]), axis=0)


def members_of(refs):
    return refs[0][...] if len(refs) == 1 else jnp.concatenate([ref[...] for ref in refs], axis=0)


def detail_kernel(v_ref, *refs):
    detail(members_of(refs[:4]), natural(v_ref), *refs[4:])


def first_detail_kernel(x_hbm, v_hbm, *refs):
    *out_refs, x_ref, v_ref, x_sems, v_sems = refs
    copies = []
    for k in range(8):
        rows = pl.ds(16 * k, 16)
        copies.append(pltpu.make_async_copy(v_hbm.at[rows], v_ref.at[rows], v_sems.at[k]))
        rows = pl.ds(32 * k, 32)
        copies.append(pltpu.make_async_copy(x_hbm.at[rows], x_ref.at[rows], x_sems.at[k]))
    for copy in copies:
        copy.start()
    for copy in copies:
        copy.wait()
    detail(x_ref[...], v_ref[...], *out_refs)


def detail(x, v, top_ref, bottom_ref, c_ref, own_ref=None):
    w = x.astype(F32) * for_each(v)
    c = block_mean(w, split3)
    if own_ref is None:
        for tile in range(TILES):
            c_ref[tile] = c
    else:
        c_ref[...] = c.reshape(PAIRS, 8, 256)
        own_ref[...] = c
    spread = prolong(c, edges=True)
    for pair in range(PAIRS):
        at = ROWS * pair
        top_ref[pair] = w[at : at + 8] - spread[16 * pair : 16 * pair + 8]
        bottom_ref[pair] = w[at + 24 : at + 32] - spread[16 * pair + 8 : 16 * pair + 16]


def row_table(taps, tile):
    i, j = iotas(160, 192)
    first = jnp.zeros((160, 192), F32)
    for k in range(4):
        row, col = i - 40 * k, j - 48 * k
        dist = jnp.abs(col - row - 4)
        spot, source = tile * ROWS - 4 + row, tile * ROWS - 8 + col
        fits = (row >= 0) & (row < 40) & (col >= 0) & (col < 48)
        fits = fits & (spot >= 0) & (spot < ROWS * TILES)
        fits = fits & (source >= 0) & (source < ROWS * TILES)
        dist = jnp.where(fits, dist, 9)
        for o in range(5):
            first = jnp.where(dist == o, taps[o][k], first)
    i, j = iotas(128, 160)
    second = jnp.zeros((128, 160), F32)
    for k in range(4):
        row, col = i - 32 * k, j - 40 * k
        fits = (row >= 0) & (row < 32) & (col >= 0) & (col < 40)
        dist = jnp.where(fits, jnp.abs(col - row - 4), 9)
        for o in range(5):
            second = jnp.where(dist == o, taps[o][k], second)
    return exact_mm(second, first)


def band_table(taps):
    i, j = iotas(8, 128)
    before, after = jnp.abs(i - 8 - j), jnp.abs(i + 128 - j)
    i, j = iotas(128, 128)
    inner = jnp.abs(i - j)
    left, right = jnp.zeros((8, 128), F32), jnp.zeros((8, 128), F32)
    middle = jnp.zeros((128, 128), F32)
    for o in range(9):
        left = jnp.where(before == o, taps[o], left)
        right = jnp.where(after == o, taps[o], right)
        middle = jnp.where(inner == o, taps[o], middle)
    rest = jnp.zeros((8, 128), F32)
    return jnp.concatenate([rest, left, middle, right, rest], axis=0)


def taps_of(taps_ref):
    taps = taps_ref[...]
    square = taps * taps
    energy = square[:, 0:1] + 2.0 * jnp.sum(square[:, 1:5], axis=1, keepdims=True)
    taps = taps / jnp.sqrt(energy)
    single = [taps[:, o : o + 1] for o in range(5)]
    once = [single[abs(o)] for o in range(-4, 5)]
    double = []
    for o in range(9):
        terms = [once[i] * once[o + 8 - i] for i in range(o, 9)]
        double.append(functools.reduce(jnp.add, terms))
    lat = [[tap[k : k + 1] for k in range(4)] for tap in single]
    lon = [[tap[4 + k : 5 + k] for k in range(4)] for tap in double]
    return lat, lon


def fill_tables(lat, lon, tile, rows_ref, band_ref):
    for kind, piece in enumerate(split2(row_table(lat, tile))):
        rows_ref[kind] = piece
    for level in range(band_ref.shape[0]):
        for kind, piece in enumerate(split2(band_table([tap[level] for tap in lon]))):
            band_ref[level, kind] = piece


def table_kernel(place_ref, taps_ref, lat_ref, x_ref, *refs):
    mix_ref, rows_ref, band_ref, *x_next_refs = refs
    tile, own = place_ref[0], place_ref[1] >> 3

    def picked(values):
        value = values[3]
        for k in range(3):
            value = jnp.where(own == k, values[k], value)
        return value

    lat, lon = ([[picked(tap)] * 4 for tap in taps] for taps in taps_of(taps_ref))
    fill_tables(lat, lon, tile, rows_ref, band_ref)
    for ahead, x_next_ref in enumerate(x_next_refs):
        for member in range(2):
            row = ROWS * (4 * member + ((own + ahead) & 3))
            x_next_ref[ROWS * member : ROWS * member + ROWS] = x_ref[
                pl.ds(pl.multiple_of(row, ROWS), ROWS), :
            ]
    i, j = iotas(64, 512)
    repeat = jnp.where((i >> 3) == (j >> 6), jnp.where((i & 7) == (j & 7), 1.0, 0.0), 0.0)
    mine = lat_ref[pl.ds(pl.multiple_of(8 * tile, 8), 8), :]
    wide = exact_mm(mine, repeat)
    mix = jnp.concatenate([wide] * PAIRS, axis=0)
    mix_ref[...] = jnp.where((i >> 3) == ((j >> 3) & 7), mix, 0.0)


def banded(band_ref, level, kind):
    band = band_ref[level, kind]
    edge, half = jnp.zeros((112, 128), BF16), jnp.zeros((128, 128), BF16)
    left = jnp.concatenate([edge, band, edge, half], axis=0)
    right = jnp.concatenate([half, edge, band, edge], axis=0)
    return jnp.concatenate([left, right], axis=1)


def windows(parts, first_row, height):
    rows = []
    for block in range(4):
        for part in parts:
            lanes = [
                part[first_row : first_row + height, 128 * tile : 128 * tile + 128]
                for tile in ((2 * block - 1) % 8, 2 * block, 2 * block + 1, (2 * block + 2) % 8)
            ]
            rows.append(jnp.concatenate(lanes, axis=1))
    return jnp.concatenate(rows, axis=0)


def lane_sums(values):
    i, j = iotas(8, 128)
    result = jnp.zeros((8, 128), F32)
    for lane, value in values:
        result = jnp.where((i == 0) & (j == lane), value, result)
    return result


def total(x):
    return jnp.sum(x, axis=(0, 1), keepdims=True)


def fine_kernel(last, *refs):
    if last:
        place_ref, r_ref, *refs = refs
        v_ref, c_ref, *refs = refs
    else:
        *refs, fine_ref, c_ref, rows_ref, band_ref, sems = refs
        place_ref, v_ref, c_hbm, taps_ref, *refs = refs
        loading = pltpu.make_async_copy(c_hbm.at[0], c_ref, sems.at[0])
        loading.start()
        fill_tables(*taps_of(taps_ref), place_ref[0], rows_ref, band_ref)
    before_ref, after_ref, *refs = refs
    if last:
        rows_ref, band_ref, *refs = refs
    x_refs, refs = (refs[:4], refs[4:]) if last else (refs[:1], refs[1:])
    x = members_of(x_refs)
    if last:
        fine_ref, mean_ref, sums_ref, f_ref = refs
        v = natural(v_ref)
    else:
        fine_hbm, mean_ref, f_ref = refs
        v = v_ref[...]
        loading.wait()
    d = x.astype(F32) * for_each(v) - prolong(c_ref[...])
    highs, lows = [], []
    for part in range(2):
        rows = []
        for pair in range(4 * part, 4 * part + 4):
            rows += [before_ref[pair], d[ROWS * pair : ROWS * pair + ROWS], after_ref[pair]]
        high, low = split2(jnp.concatenate(rows, axis=0))
        passed = mm(rows_ref[0], high) + mm(rows_ref[0], low) + mm(rows_ref[1], high)
        high, low = split2(passed)
        highs.append(high)
        lows.append(low)
    levels = band_ref.shape[0]
    height = 128 // levels
    for level in range(levels):
        high = windows(highs, height * level, height)
        low = windows(lows, height * level, height)
        table_high, table_low = banded(band_ref, level, 0), banded(band_ref, level, 1)
        result = mm(high, table_high) + mm(low, table_high) + mm(high, table_low)
        for block in range(4):
            lanes = slice(256 * block, 256 * block + 256)
            summed = None
            for part in range(2):
                for inner in range(height // ROWS):
                    row = 128 * part + height * level + ROWS * inner
                    at = height * (2 * block + part) + ROWS * inner
                    f = result[at : at + ROWS]
                    f_ref[row : row + ROWS, lanes] = f
                    term = x[row : row + ROWS, lanes].astype(F32) * f
                    summed = term if summed is None else summed + term
            fine_ref[ROWS * level : ROWS * level + ROWS, lanes] = summed
    if not last:
        copy = pltpu.make_async_copy(fine_ref, fine_hbm, sems.at[1])
        copy.start()
    means = block_mean(f_ref[...], split2)
    mean_ref[...] = means
    if not last:
        copy.wait()
    else:
        own = place_ref[1] >> 3
        r = r_ref[pl.ds(pl.multiple_of(ROWS * own, ROWS), ROWS), :]
        products = total(v * fine_ref[...]) - 16.0 * total(c_ref[...] * means)
        sums_ref[...] = lane_sums(
            ((0, total(r * r)), (1, total(r * v)), (2, total(v * v)), (3, products))
        )


def smooth_kernel(c_ref, lat_ref, lon_ref, sums_ref, out_ref):
    c = c_ref[...].reshape(64, 256)
    smoothed = exact_mm(exact_mm(lat_ref[...], c), lon_ref[...])
    sums = sums_ref[...] + lane_sums([(4, 16.0 * total(c * smoothed))])
    for tile in range(TILES):
        out_ref[tile, 0:8, :] = smoothed[8 * tile : 8 * tile + 8, :128]
        out_ref[tile, 8:16, :] = smoothed[8 * tile : 8 * tile + 8, 128:]
        out_ref[tile, 16:24, :] = sums


def blended(x, fine_ref, smoothed):
    product = x.astype(F32) * prolong(smoothed)
    height = fine_ref.shape[0]
    pieces = [product[k : k + height] for k in range(0, 256, height)]
    return functools.reduce(jnp.add, pieces, fine_ref[...])


def partial_kernel(x_ref, fine_hbm, mean_ref, c_ref, mix_ref, lon_ref, out_ref, fine_ref, sem):
    copy = pltpu.make_async_copy(fine_hbm, fine_ref, sem)
    copy.start()
    across = exact_mm(mix_ref[...], c_ref[...].reshape(512, 256))
    smoothed = exact_mm(across, lon_ref[...]) - mean_ref[...]
    copy.wait()
    p = blended(x_ref[...], fine_ref, smoothed)
    for tall in range(16):
        for wide in range(8):
            out_ref[2 * tall + wide // 4, 8 * (wide % 4) : 8 * (wide % 4) + 8, :] = p[
                8 * tall : 8 * tall + 8, 128 * wide : 128 * wide + 128
            ]


def packed(field):
    group = lax.broadcasted_iota(jnp.int32, (8, 128), 1) >> 5
    shares = []
    for wide in range(8):
        tiles = [field[8 * i : 8 * i + 8, 128 * wide : 128 * wide + 128] for i in range(4)]
        for g in range(4):
            share = None
            for i in range(4):
                turned = pltpu.roll(tiles[i], (32 * (i - g)) % 128, 1) if i != g else tiles[i]
                share = turned if share is None else jnp.where(group == i, turned, share)
            shares.append(share)
    return shares


def last_partial_kernel(place_ref, fine_ref, mean_ref, smoothed_ref, v_ref, *refs):
    *x_refs, out_ref, v_packed = refs
    halves = [smoothed_ref[:, 8 * k : 8 * k + 8, :].reshape(64, 128) for k in range(2)]
    p = blended(members_of(x_refs), fine_ref, jnp.concatenate(halves, axis=1) - mean_ref[...])
    sums = jnp.sum(smoothed_ref[:, 16:24, :], axis=0)
    for group, share in enumerate(packed(p)):
        out_ref[group, 0:8, :] = share
    for group, share in enumerate(packed(natural(v_ref))):
        v_packed[group] = share
    i, j = iotas(8, 128)
    mine = pl.ds(place_ref[1] & 7, 1)
    for group in range(GROUPS):
        row = jnp.broadcast_to(v_packed[group, mine, :], (8, 128))
        out_ref[group, 8:16, :] = jnp.where(i == 1, row, sums)


def share_kernel(scale, place_ref, arrived_ref, r_ref, out_ref):
    group = place_ref[1]
    share = r_ref[
        pl.ds(pl.multiple_of(8 * (group >> 1), 8), 8),
        pl.ds(pl.multiple_of(512 * (group & 1), 512), 512),
    ]
    share = jnp.concatenate([share[:, 128 * k : 128 * k + 128] for k in range(4)], axis=0)
    share = share + jnp.sum(arrived_ref[...], axis=0) * scale
    for other in range(out_ref.shape[0]):
        out_ref[other] = share


def final_kernel(scale, place_ref, arrived_ref, r_ref, x_out, res_out):
    group = place_ref[1]
    lanes = pl.ds(pl.multiple_of(128 * (group >> 2), 128), 128)
    i, j = iotas(8, 128)
    sums = jnp.sum(arrived_ref[:, 8:16, :], axis=0)
    rr, ra, aa, af, ac = (total(jnp.where((i == 0) & (j == k), sums, 0.0)) for k in range(5))
    rr, ra, aa = rr / 8, ra / 8, aa / 8
    step = rr / ra
    ab = aa + (af + ac) * scale
    squares = step * step * aa - rr
    next_step = squares / ((ra - step * aa) - step * (aa - step * ab))
    for level in range(4):
        r = jnp.zeros((8, 128), F32)
        for k in range(4):
            row = ROWS * level + 8 * k
            tile = r_ref[row : row + 8, lanes]
            turned = pltpu.roll(tile, (32 * (k + 4 - (group & 3))) & 127, 1)
            r = jnp.where((j >> 5) == k, turned, r)
        a = jnp.concatenate([arrived_ref[8 * level + k, 9:10, :] for k in range(8)], axis=0)
        p = jnp.sum(arrived_ref[8 * level : 8 * level + 8, 0:8, :], axis=0)
        b = a + p * scale
        r_next = r - step * a
        x_new = step * r + next_step * r_next
        res_new = r_next - next_step * (a - step * b)
        for k in range(4):
            x_out[level, 8 * k : 8 * k + 8, :] = x_new[:, 32 * k : 32 * k + 32]
            res_out[level, 8 * k : 8 * k + 8, :] = res_new[:, 32 * k : 32 * k + 32]


VMEM = pl.BlockSpec(memory_space=pltpu.VMEM)
SMEM = pl.BlockSpec(memory_space=pltpu.SMEM)
HBM = pl.BlockSpec(memory_space=pltpu.HBM)


def call(kernel, outs, specs, args, flops, limit, scratch=(), out_specs=None):
    out_specs = out_specs or [VMEM] * len(outs)
    shapes = [
        pltpu.HBM(*out) if spec is HBM else jax.ShapeDtypeStruct(*out)
        for out, spec in zip(outs, out_specs)
    ]
    size = sum(a.size * a.dtype.itemsize for a in args)
    args = [
        pltpu.with_memory_space_constraint(arg, pltpu.HBM) if spec is HBM else arg
        for arg, spec in zip(args, specs)
    ]
    return pl.pallas_call(
        kernel,
        out_shape=shapes if len(shapes) > 1 else shapes[0],
        in_specs=specs,
        out_specs=out_specs if len(shapes) > 1 else out_specs[0],
        scratch_shapes=list(scratch),
        compiler_params=pltpu.CompilerParams(vmem_limit_bytes=limit << 20),
        cost_estimate=pl.CostEstimate(flops=flops, bytes_accessed=size, transcendentals=0),
    )(*args)


def exchange(blocks, axis):
    return lax.all_to_all(blocks, axis, 0, 0, tiled=True)


def local(perturbations, right_side, fine_taps, coarse_lat, coarse_lon):
    count, levels, height, extent = perturbations.shape
    members = count * lax.axis_size(MEM)
    scale = 1.0 / (members - 1)
    place = jnp.stack([lax.axis_index("tile"), lax.axis_index(MEM)]).astype(jnp.int32)
    x = perturbations.reshape(count * levels * height, extent)
    r = right_side.reshape(levels * height, extent)
    half = ((128, LON), F32)
    edge = ((PAIRS, 8, LON), F32)
    shared = ((GROUPS, 32, 128), F32)
    up = [(i, (i + 1) % TILES) for i in range(TILES)]
    down = [(j, i) for i, j in up]

    def edges(top, bottom):
        return lax.ppermute(bottom, "tile", up), lax.ppermute(top, "tile", down)

    own = ((64, 256), F32)
    top, bottom, c = call(
        first_detail_kernel,
        [edge, edge, ((TILES, 64, 256), F32)],
        [HBM] * 2,
        (x, r),
        10**9,
        12,
        scratch=(
            pltpu.VMEM((256, LON), BF16),
            pltpu.VMEM((128, LON), F32),
            pltpu.SemaphoreType.DMA((8,)),
            pltpu.SemaphoreType.DMA((8,)),
        ),
    )
    c_first = exchange(c, "tile")
    taps = fine_taps.reshape(2 * levels, 5)
    rows_shape, band_shape = (2, 128, 192), (2, 160, 128)
    fine_scratch = [pltpu.VMEM((256, LON), F32)]
    fine, means = call(
        functools.partial(fine_kernel, False),
        [half, own],
        [SMEM, VMEM, HBM] + [VMEM] * 4,
        (place, r, c, taps, *edges(top, bottom), x),
        10**11,
        16,
        scratch=[
            *fine_scratch,
            pltpu.VMEM(*half),
            pltpu.VMEM(*own),
            pltpu.VMEM(rows_shape, BF16),
            pltpu.VMEM((levels, *band_shape), BF16),
            pltpu.SemaphoreType.DMA((2,)),
        ],
        out_specs=[HBM, VMEM],
    )
    means, x_again = lax.optimization_barrier((means, x))
    mix, rows_next, band_next, *x_next = call(
        table_kernel,
        [
            ((64, 512), F32),
            (rows_shape, BF16),
            ((1, *band_shape), BF16),
            *[((count * height, extent), BF16)] * 4,
        ],
        [SMEM] + [VMEM] * 3,
        (place, taps, coarse_lat, x_again),
        10**9,
        6,
    )
    for ahead in range(1, 4):
        ring = [(i, (i + ahead) % 4) for i in range(4)]
        x_next[ahead] = lax.ppermute(x_next[ahead], "mem_0", ring)
    fine, x_next = lax.optimization_barrier((fine, x_next))
    shares = call(
        partial_kernel,
        [shared],
        [VMEM, HBM] + [VMEM] * 4,
        (x, fine, means, c_first, mix, coarse_lon),
        10**9,
        12,
        scratch=[pltpu.VMEM(*half), pltpu.SemaphoreType.DMA],
    )
    arrived = exchange(shares, MEM)
    share = call(
        functools.partial(share_kernel, scale),
        [((TILES, 32, 128), F32)],
        [SMEM, VMEM, VMEM],
        (place, arrived, r),
        10**6,
        6,
    )
    a = exchange(share, ("mem_1", "mem_2"))

    top, bottom, c, c_own = call(
        detail_kernel,
        [edge, edge, ((PAIRS, 8, 256), F32), own],
        [VMEM] * 5,
        (a, *x_next),
        10**9,
        12,
    )
    beside = edges(top, bottom)
    c = exchange(c, "tile")
    level = ((height, LON), F32)
    fine, means, sums = call(
        functools.partial(fine_kernel, True),
        [level, own, ((8, 128), F32)],
        [SMEM] + [VMEM] * 11,
        (place, r, a, c_own, *beside, rows_next, band_next, *x_next),
        10**11,
        16,
        scratch=fine_scratch,
    )
    smoothed = call(
        smooth_kernel,
        [((TILES, 24, 128), F32)],
        [VMEM] * 4,
        (c, coarse_lat, coarse_lon, sums),
        10**8,
        6,
    )
    smoothed = exchange(smoothed, "tile")
    shares = call(
        last_partial_kernel,
        [((GROUPS, 16, 128), F32)],
        [SMEM] + [VMEM] * 8,
        (place, fine, means, smoothed, a, *x_next),
        10**9,
        12,
        scratch=[pltpu.VMEM((GROUPS, 8, 128), F32)],
    )
    arrived = exchange(shares, MEM)
    out = ((levels, height, extent // GROUPS), F32)
    return tuple(
        call(
            functools.partial(final_kernel, scale),
            [out, out],
            [SMEM, VMEM, VMEM],
            (place, arrived, r),
            10**6,
            6,
        )
    )


def solution(mesh):
    torus = Mesh(
        mesh.devices.reshape(4, 4, 2, mesh.shape["tile"]), ("mem_0", "mem_1", "mem_2", "tile")
    )
    placed = (P(MEM, None, "tile", None), P(None, "tile", None), P(), P(), P())
    return jax.shard_map(
        local,
        mesh=torus,
        in_specs=placed,
        out_specs=(P(None, "tile", MEM), P(None, "tile", MEM)),
        check_vma=False,
    )
```

```python
import functools

import jax
import jax.numpy as jnp
from jax import lax
from jax.experimental import pallas as pl
from jax.experimental.pallas import tpu as pltpu
from jax.sharding import Mesh
from jax.sharding import PartitionSpec as P

MEM = ("mem_0", "mem_1", "mem_2")
F32 = jnp.float32
BF16 = jnp.bfloat16
EXACT = lax.Precision.HIGHEST
PAIRS, ROWS, LON = 8, 32, 1024
GROUPS, TILES = 32, 8


def mm(a, b):
    return jnp.dot(a, b, preferred_element_type=F32)


def exact_mm(a, b):
    return jnp.dot(a, b, preferred_element_type=F32, precision=EXACT)


def split2(x):
    high = x.astype(BF16)
    return high, (x - high.astype(F32)).astype(BF16)


def split3(x):
    high = x.astype(BF16)
    rest = x - high.astype(F32)
    mid = rest.astype(BF16)
    return high, mid, (rest - mid.astype(F32)).astype(BF16)


def iotas(rows, cols):
    return (
        lax.broadcasted_iota(jnp.int32, (rows, cols), 0),
        lax.broadcasted_iota(jnp.int32, (rows, cols), 1),
    )


def shrink_table(rows, cols, along_rows):
    i, j = iotas(rows, cols)
    hit = (i >> 2) == j if along_rows else i == (j >> 2)
    return jnp.where(hit, 0.25, 0.0).astype(BF16)


def expand_table(rows, cols, along_rows):
    i, j = iotas(rows, cols)
    hit = (i >> 2) == j if along_rows else i == (j >> 2)
    return jnp.where(hit, 1.0, 0.0).astype(BF16)


def block_mean(w, split):
    table = shrink_table(64, 256, False)
    part = sum(mm(table, piece) for piece in split(w))
    stacked = jnp.concatenate([part[:, :512], part[:, 512:]], axis=0)
    table = shrink_table(512, 128, True)
    small = sum(mm(piece, table) for piece in split(stacked))
    return jnp.concatenate([small[:64], small[64:]], axis=1)


def prolong(c, edges=False):
    if edges:
        i, j = iotas(128, 64)
        spot = 8 * (i >> 4) + ((i & 15) >> 2) + 4 * ((i & 15) >> 3)
        table = jnp.where(spot == j, 1.0, 0.0).astype(BF16)
    else:
        table = expand_table(256, 64, True)
    rows = table.shape[0]
    tall = sum(mm(table, piece) for piece in split2(c))
    stacked = jnp.concatenate([tall[:, :128], tall[:, 128:]], axis=0)
    table = expand_table(128, 512, False)
    wide = sum(mm(piece, table) for piece in split2(stacked))
    return jnp.concatenate([wide[:rows], wide[rows:]], axis=1)


def natural(blocks):
    rows = []
    for tall in range(blocks.shape[0] // 2):
        lanes = [
            blocks[2 * tall + wide // 4, 8 * (wide % 4) : 8 * (wide % 4) + 8, :]
            for wide in range(8)
        ]
        rows.append(jnp.concatenate(lanes, axis=1))
    return jnp.concatenate(rows, axis=0)


def for_each(v):
    return jnp.concatenate([v] * (256 // v.shape[0]), axis=0)


def members_of(refs):
    return refs[0][...] if len(refs) == 1 else jnp.concatenate([ref[...] for ref in refs], axis=0)


def detail_kernel(v_ref, *refs):
    detail(members_of(refs[:4]), natural(v_ref), *refs[4:])


def first_detail_kernel(x_hbm, v_hbm, *refs):
    *out_refs, x_ref, v_ref, x_sems, v_sems = refs
    copies = []
    for k in range(8):
        rows = pl.ds(16 * k, 16)
        copies.append(pltpu.make_async_copy(v_hbm.at[rows], v_ref.at[rows], v_sems.at[k]))
        rows = pl.ds(32 * k, 32)
        copies.append(pltpu.make_async_copy(x_hbm.at[rows], x_ref.at[rows], x_sems.at[k]))
    for copy in copies:
        copy.start()
    for copy in copies:
        copy.wait()
    detail(x_ref[...], v_ref[...], *out_refs)


def detail(x, v, top_ref, bottom_ref, c_ref, own_ref=None):
    w = x.astype(F32) * for_each(v)
    c = block_mean(w, split3)
    if own_ref is None:
        for tile in range(TILES):
            c_ref[tile] = c
    else:
        c_ref[...] = c.reshape(PAIRS, 8, 256)
        own_ref[...] = c
    spread = prolong(c, edges=True)
    for pair in range(PAIRS):
        at = ROWS * pair
        top_ref[pair] = w[at : at + 8] - spread[16 * pair : 16 * pair + 8]
        bottom_ref[pair] = w[at + 24 : at + 32] - spread[16 * pair + 8 : 16 * pair + 16]


def row_table(taps, tile):
    i, j = iotas(160, 192)
    first = jnp.zeros((160, 192), F32)
    for k in range(4):
        row, col = i - 40 * k, j - 48 * k
        dist = jnp.abs(col - row - 4)
        spot, source = tile * ROWS - 4 + row, tile * ROWS - 8 + col
        fits = (row >= 0) & (row < 40) & (col >= 0) & (col < 48)
        fits = fits & (spot >= 0) & (spot < ROWS * TILES)
        fits = fits & (source >= 0) & (source < ROWS * TILES)
        dist = jnp.where(fits, dist, 9)
        for o in range(5):
            first = jnp.where(dist == o, taps[o][k], first)
    i, j = iotas(128, 160)
    second = jnp.zeros((128, 160), F32)
    for k in range(4):
        row, col = i - 32 * k, j - 40 * k
        fits = (row >= 0) & (row < 32) & (col >= 0) & (col < 40)
        dist = jnp.where(fits, jnp.abs(col - row - 4), 9)
        for o in range(5):
            second = jnp.where(dist == o, taps[o][k], second)
    return exact_mm(second, first)


def band_table(taps):
    i, j = iotas(8, 128)
    before, after = jnp.abs(i - 8 - j), jnp.abs(i + 128 - j)
    i, j = iotas(128, 128)
    inner = jnp.abs(i - j)
    left, right = jnp.zeros((8, 128), F32), jnp.zeros((8, 128), F32)
    middle = jnp.zeros((128, 128), F32)
    for o in range(9):
        left = jnp.where(before == o, taps[o], left)
        right = jnp.where(after == o, taps[o], right)
        middle = jnp.where(inner == o, taps[o], middle)
    rest = jnp.zeros((8, 128), F32)
    return jnp.concatenate([rest, left, middle, right, rest], axis=0)


def own_tile():
    return lax.axis_index("tile")


def own_group():
    return 8 * lax.axis_index("mem_0") + 2 * lax.axis_index("mem_1") + lax.axis_index("mem_2")


def taps_of(taps_ref):
    taps = taps_ref[...]
    square = taps * taps
    energy = square[:, 0:1] + 2.0 * jnp.sum(square[:, 1:5], axis=1, keepdims=True)
    taps = taps / jnp.sqrt(energy)
    single = [taps[:, o : o + 1] for o in range(5)]
    once = [single[abs(o)] for o in range(-4, 5)]
    double = []
    for o in range(9):
        terms = [once[i] * once[o + 8 - i] for i in range(o, 9)]
        double.append(functools.reduce(jnp.add, terms))
    lat = [[tap[k : k + 1] for k in range(4)] for tap in single]
    lon = [[tap[4 + k : 5 + k] for k in range(4)] for tap in double]
    return lat, lon


def fill_tables(lat, lon, tile, rows_ref, band_ref):
    for kind, piece in enumerate(split2(row_table(lat, tile))):
        rows_ref[kind] = piece
    for level in range(band_ref.shape[0]):
        for kind, piece in enumerate(split2(band_table([tap[level] for tap in lon]))):
            band_ref[level, kind] = piece


def table_kernel(taps_ref, lat_ref, x_ref, *refs):
    mix_ref, rows_ref, band_ref, *x_next_refs = refs
    tile, own = own_tile(), lax.axis_index("mem_0")

    def picked(values):
        value = values[3]
        for k in range(3):
            value = jnp.where(own == k, values[k], value)
        return value

    lat, lon = ([[picked(tap)] * 4 for tap in taps] for taps in taps_of(taps_ref))
    fill_tables(lat, lon, tile, rows_ref, band_ref)
    for ahead, x_next_ref in enumerate(x_next_refs):
        for member in range(2):
            row = ROWS * (4 * member + ((own + ahead) & 3))
            x_next_ref[ROWS * member : ROWS * member + ROWS] = x_ref[
                pl.ds(pl.multiple_of(row, ROWS), ROWS), :
            ]
    i, j = iotas(64, 512)
    repeat = jnp.where((i >> 3) == (j >> 6), jnp.where((i & 7) == (j & 7), 1.0, 0.0), 0.0)
    mine = lat_ref[pl.ds(pl.multiple_of(8 * tile, 8), 8), :]
    wide = exact_mm(mine, repeat)
    mix = jnp.concatenate([wide] * PAIRS, axis=0)
    mix_ref[...] = jnp.where((i >> 3) == ((j >> 3) & 7), mix, 0.0)


def banded(band_ref, level, kind):
    band = band_ref[level, kind]
    edge, half = jnp.zeros((112, 128), BF16), jnp.zeros((128, 128), BF16)
    left = jnp.concatenate([edge, band, edge, half], axis=0)
    right = jnp.concatenate([half, edge, band, edge], axis=0)
    return jnp.concatenate([left, right], axis=1)


def windows(parts, first_row, height):
    rows = []
    for block in range(4):
        for part in parts:
            lanes = [
                part[first_row : first_row + height, 128 * tile : 128 * tile + 128]
                for tile in ((2 * block - 1) % 8, 2 * block, 2 * block + 1, (2 * block + 2) % 8)
            ]
            rows.append(jnp.concatenate(lanes, axis=1))
    return jnp.concatenate(rows, axis=0)


def lane_sums(values):
    i, j = iotas(8, 128)
    result = jnp.zeros((8, 128), F32)
    for lane, value in values:
        result = jnp.where((i == 0) & (j == lane), value, result)
    return result


def total(x):
    return jnp.sum(x, axis=(0, 1), keepdims=True)


def fine_kernel(last, *refs):
    if last:
        r_ref, v_ref, c_ref, *refs = refs
    else:
        *refs, f_ref, c_ref, rows_ref, band_ref, sem = refs
        v_ref, c_hbm, taps_ref, *refs = refs
        load = pltpu.make_async_copy(c_hbm.at[0], c_ref, sem)
        load.start()
        fill_tables(*taps_of(taps_ref), own_tile(), rows_ref, band_ref)
    before_ref, after_ref, *refs = refs
    if last:
        rows_ref, band_ref, *refs = refs
    x_refs, refs = (refs[:4], refs[4:]) if last else (refs[:1], refs[1:])
    x = members_of(x_refs)
    if last:
        fine_ref, mean_ref, sums_ref, f_ref = refs
        v = natural(v_ref)
    else:
        fine_ref, mean_ref = refs
        v = v_ref[...]
        load.wait()
    d = x.astype(F32) * for_each(v) - prolong(c_ref[...])
    highs, lows = [], []
    for part in range(2):
        rows = []
        for pair in range(4 * part, 4 * part + 4):
            rows += [before_ref[pair], d[ROWS * pair : ROWS * pair + ROWS], after_ref[pair]]
        high, low = split2(jnp.concatenate(rows, axis=0))
        passed = mm(rows_ref[0], high) + mm(rows_ref[0], low) + mm(rows_ref[1], high)
        high, low = split2(passed)
        highs.append(high)
        lows.append(low)
    levels = band_ref.shape[0]
    height = 128 // levels
    for level in range(levels):
        high = windows(highs, height * level, height)
        low = windows(lows, height * level, height)
        table_high, table_low = banded(band_ref, level, 0), banded(band_ref, level, 1)
        result = mm(high, table_high) + mm(low, table_high) + mm(high, table_low)
        for block in range(4):
            lanes = slice(256 * block, 256 * block + 256)
            summed = None
            for part in range(2):
                for inner in range(height // ROWS):
                    row = 128 * part + height * level + ROWS * inner
                    at = height * (2 * block + part) + ROWS * inner
                    f = result[at : at + ROWS]
                    f_ref[row : row + ROWS, lanes] = f
                    term = x[row : row + ROWS, lanes].astype(F32) * f
                    summed = term if summed is None else summed + term
            fine_ref[ROWS * level : ROWS * level + ROWS, lanes] = summed
    means = block_mean(f_ref[...], split2)
    mean_ref[...] = means
    if last:
        own = lax.axis_index("mem_0")
        r = r_ref[pl.ds(pl.multiple_of(ROWS * own, ROWS), ROWS), :]
        products = total(v * fine_ref[...]) - 16.0 * total(c_ref[...] * means)
        sums_ref[...] = lane_sums(
            ((0, total(r * r)), (1, total(r * v)), (2, total(v * v)), (3, products))
        )


def smooth_kernel(c_ref, lat_ref, lon_ref, sums_ref, out_ref):
    c = c_ref[...].reshape(64, 256)
    smoothed = exact_mm(exact_mm(lat_ref[...], c), lon_ref[...])
    sums = sums_ref[...] + lane_sums([(4, 16.0 * total(c * smoothed))])
    for tile in range(TILES):
        out_ref[tile, 0:8, :] = smoothed[8 * tile : 8 * tile + 8, :128]
        out_ref[tile, 8:16, :] = smoothed[8 * tile : 8 * tile + 8, 128:]
        out_ref[tile, 16:24, :] = sums


def blended(x, fine_ref, smoothed):
    product = x.astype(F32) * prolong(smoothed)
    height = fine_ref.shape[0]
    pieces = [product[k : k + height] for k in range(0, 256, height)]
    return functools.reduce(jnp.add, pieces, fine_ref[...])


def partial_kernel(x_ref, fine_ref, mean_ref, c_ref, mix_ref, lon_ref, out_ref):
    across = exact_mm(mix_ref[...], c_ref[...].reshape(512, 256))
    p = blended(x_ref[...], fine_ref, exact_mm(across, lon_ref[...]) - mean_ref[...])
    for tall in range(16):
        for wide in range(8):
            out_ref[2 * tall + wide // 4, 8 * (wide % 4) : 8 * (wide % 4) + 8, :] = p[
                8 * tall : 8 * tall + 8, 128 * wide : 128 * wide + 128
            ]


def packed(field):
    group = lax.broadcasted_iota(jnp.int32, (8, 128), 1) >> 5
    shares = []
    for wide in range(8):
        tiles = [field[8 * i : 8 * i + 8, 128 * wide : 128 * wide + 128] for i in range(4)]
        for g in range(4):
            share = None
            for i in range(4):
                turned = pltpu.roll(tiles[i], (32 * (i - g)) % 128, 1) if i != g else tiles[i]
                share = turned if share is None else jnp.where(group == i, turned, share)
            shares.append(share)
    return shares


def last_partial_kernel(fine_ref, mean_ref, smoothed_ref, v_ref, *refs):
    *x_refs, out_ref, v_packed = refs
    halves = [smoothed_ref[:, 8 * k : 8 * k + 8, :].reshape(64, 128) for k in range(2)]
    p = blended(members_of(x_refs), fine_ref, jnp.concatenate(halves, axis=1) - mean_ref[...])
    sums = jnp.sum(smoothed_ref[:, 16:24, :], axis=0)
    for group, share in enumerate(packed(p)):
        out_ref[group, 0:8, :] = share
    for group, share in enumerate(packed(natural(v_ref))):
        v_packed[group] = share
    i, j = iotas(8, 128)
    mine = pl.ds(own_group() & 7, 1)
    for group in range(GROUPS):
        row = jnp.broadcast_to(v_packed[group, mine, :], (8, 128))
        out_ref[group, 8:16, :] = jnp.where(i == 1, row, sums)


def share_kernel(scale, arrived_ref, r_ref, out_ref):
    group = own_group()
    share = r_ref[
        pl.ds(pl.multiple_of(8 * (group >> 1), 8), 8),
        pl.ds(pl.multiple_of(512 * (group & 1), 512), 512),
    ]
    share = jnp.concatenate([share[:, 128 * k : 128 * k + 128] for k in range(4)], axis=0)
    share = share + jnp.sum(arrived_ref[...], axis=0) * scale
    for other in range(out_ref.shape[0]):
        out_ref[other] = share


def final_kernel(scale, arrived_ref, r_ref, x_out, res_out):
    group = own_group()
    lanes = pl.ds(pl.multiple_of(128 * (group >> 2), 128), 128)
    i, j = iotas(8, 128)
    sums = jnp.sum(arrived_ref[:, 8:16, :], axis=0)
    rr, ra, aa, af, ac = (total(jnp.where((i == 0) & (j == k), sums, 0.0)) for k in range(5))
    rr, ra, aa = rr / 8, ra / 8, aa / 8
    step = rr / ra
    ab = aa + (af + ac) * scale
    squares = step * step * aa - rr
    next_step = squares / ((ra - step * aa) - step * (aa - step * ab))
    for level in range(4):
        r = jnp.zeros((8, 128), F32)
        for k in range(4):
            row = ROWS * level + 8 * k
            tile = r_ref[row : row + 8, lanes]
            turned = pltpu.roll(tile, (32 * (k + 4 - (group & 3))) & 127, 1)
            r = jnp.where((j >> 5) == k, turned, r)
        a = jnp.concatenate([arrived_ref[8 * level + k, 9:10, :] for k in range(8)], axis=0)
        p = jnp.sum(arrived_ref[8 * level : 8 * level + 8, 0:8, :], axis=0)
        b = a + p * scale
        r_next = r - step * a
        x_new = step * r + next_step * r_next
        res_new = r_next - next_step * (a - step * b)
        for k in range(4):
            x_out[level, 8 * k : 8 * k + 8, :] = x_new[:, 32 * k : 32 * k + 32]
            res_out[level, 8 * k : 8 * k + 8, :] = res_new[:, 32 * k : 32 * k + 32]


VMEM = pl.BlockSpec(memory_space=pltpu.VMEM)
HBM = pl.BlockSpec(memory_space=pltpu.HBM)


def call(kernel, outs, specs, args, flops, limit, scratch=(), out_specs=None):
    out_specs = out_specs or [VMEM] * len(outs)
    shapes = [
        pltpu.HBM(*out) if spec is HBM else jax.ShapeDtypeStruct(*out)
        for out, spec in zip(outs, out_specs)
    ]
    size = sum(a.size * a.dtype.itemsize for a in args)
    args = [
        pltpu.with_memory_space_constraint(arg, pltpu.HBM) if spec is HBM else arg
        for arg, spec in zip(args, specs)
    ]
    return pl.pallas_call(
        kernel,
        out_shape=shapes if len(shapes) > 1 else shapes[0],
        in_specs=specs,
        out_specs=out_specs if len(shapes) > 1 else out_specs[0],
        scratch_shapes=list(scratch),
        compiler_params=pltpu.CompilerParams(vmem_limit_bytes=limit << 20),
        cost_estimate=pl.CostEstimate(flops=flops, bytes_accessed=size, transcendentals=0),
    )(*args)


def exchange(blocks, axis):
    return lax.all_to_all(blocks, axis, 0, 0, tiled=True)


def local(perturbations, right_side, fine_taps, coarse_lat, coarse_lon):
    count, levels, height, extent = perturbations.shape
    members = count * lax.axis_size(MEM)
    scale = 1.0 / (members - 1)
    x = perturbations.reshape(count * levels * height, extent)
    r = right_side.reshape(levels * height, extent)
    half = ((128, LON), F32)
    edge = ((PAIRS, 8, LON), F32)
    shared = ((GROUPS, 32, 128), F32)
    up = [(i, (i + 1) % TILES) for i in range(TILES)]
    down = [(j, i) for i, j in up]

    def edges(top, bottom):
        return lax.ppermute(bottom, "tile", up), lax.ppermute(top, "tile", down)

    own = ((64, 256), F32)
    taps = fine_taps.reshape(2 * levels, 5)
    rows_shape, band_shape = (2, 128, 192), (2, 160, 128)
    top, bottom, c = call(
        first_detail_kernel,
        [edge, edge, ((TILES, 64, 256), F32)],
        [HBM] * 2,
        (x, r),
        10**9,
        12,
        scratch=(
            pltpu.VMEM((256, LON), BF16),
            pltpu.VMEM((128, LON), F32),
            pltpu.SemaphoreType.DMA((8,)),
            pltpu.SemaphoreType.DMA((8,)),
        ),
    )
    before, after = edges(top, bottom)
    c_first = exchange(c, "tile")
    before, x_again = lax.optimization_barrier((before, x))
    mix, rows_next, band_next, *x_next = call(
        table_kernel,
        [
            ((64, 512), F32),
            (rows_shape, BF16),
            ((1, *band_shape), BF16),
            *[((count * height, extent), BF16)] * 4,
        ],
        [VMEM] * 3,
        (taps, coarse_lat, x_again),
        10**11,
        6,
    )
    before, mix = lax.optimization_barrier((before, mix))
    for ahead in range(1, 4):
        ring = [(i, (i + ahead) % 4) for i in range(4)]
        x_next[ahead] = lax.ppermute(x_next[ahead], "mem_0", ring)
    fine_scratch = [pltpu.VMEM((256, LON), F32)]
    fine, means = call(
        functools.partial(fine_kernel, False),
        [half, own],
        [VMEM, HBM] + [VMEM] * 4,
        (r, c, taps, before, after, x),
        10**11,
        16,
        scratch=[
            *fine_scratch,
            pltpu.VMEM(*own),
            pltpu.VMEM(rows_shape, BF16),
            pltpu.VMEM((levels, *band_shape), BF16),
            pltpu.SemaphoreType.DMA,
        ],
    )
    fine, x_next = lax.optimization_barrier((fine, x_next))
    shares = call(
        partial_kernel,
        [shared],
        [VMEM] * 6,
        (x, fine, means, c_first, mix, coarse_lon),
        10**9,
        12,
    )
    arrived = exchange(shares, MEM)
    share = call(
        functools.partial(share_kernel, scale),
        [((TILES, 32, 128), F32)],
        [VMEM, VMEM],
        (arrived, r),
        10**6,
        6,
    )
    a = exchange(share, ("mem_1", "mem_2"))

    top, bottom, c, c_own = call(
        detail_kernel,
        [edge, edge, ((PAIRS, 8, 256), F32), own],
        [VMEM] * 5,
        (a, *x_next),
        10**9,
        12,
    )
    beside = edges(top, bottom)
    c = exchange(c, "tile")
    level = ((height, LON), F32)
    fine, means, sums = call(
        functools.partial(fine_kernel, True),
        [level, own, ((8, 128), F32)],
        [VMEM] * 11,
        (r, a, c_own, *beside, rows_next, band_next, *x_next),
        10**11,
        16,
        scratch=fine_scratch,
    )
    smoothed = call(
        smooth_kernel,
        [((TILES, 24, 128), F32)],
        [VMEM] * 4,
        (c, coarse_lat, coarse_lon, sums),
        10**8,
        6,
    )
    smoothed = exchange(smoothed, "tile")
    shares = call(
        last_partial_kernel,
        [((GROUPS, 16, 128), F32)],
        [VMEM] * 8,
        (fine, means, smoothed, a, *x_next),
        10**9,
        12,
        scratch=[pltpu.VMEM((GROUPS, 8, 128), F32)],
    )
    arrived = exchange(shares, MEM)
    out = ((levels, height, extent // GROUPS), F32)
    return tuple(
        call(
            functools.partial(final_kernel, scale),
            [out, out],
            [VMEM, VMEM],
            (arrived, r),
            10**6,
            6,
        )
    )


def solution(mesh):
    torus = Mesh(
        mesh.devices.reshape(4, 4, 2, mesh.shape["tile"]), ("mem_0", "mem_1", "mem_2", "tile")
    )
    placed = (P(MEM, None, "tile", None), P(None, "tile", None), P(), P(), P())
    return jax.shard_map(
        local,
        mesh=torus,
        in_specs=placed,
        out_specs=(P(None, "tile", MEM), P(None, "tile", MEM)),
        check_vma=False,
    )
```

```python
import functools

import jax
import jax.numpy as jnp
from jax import lax
from jax.experimental import pallas as pl
from jax.experimental.pallas import tpu as pltpu
from jax.sharding import Mesh
from jax.sharding import PartitionSpec as P

MEM = ("mem_0", "mem_1", "mem_2")
F32 = jnp.float32
BF16 = jnp.bfloat16
EXACT = lax.Precision.HIGHEST
PAIRS, ROWS, LON = 8, 32, 1024
GROUPS, TILES = 32, 8


def mm(a, b):
    return jnp.dot(a, b, preferred_element_type=F32)


def exact_mm(a, b):
    return jnp.dot(a, b, preferred_element_type=F32, precision=EXACT)


def split2(x):
    high = x.astype(BF16)
    return high, (x - high.astype(F32)).astype(BF16)


def mm3(a, b):
    return mm(a[0], b[0]) + mm(a[0], b[1]) + mm(a[1], b[0])


def split3(x):
    high = x.astype(BF16)
    rest = x - high.astype(F32)
    mid = rest.astype(BF16)
    return high, mid, (rest - mid.astype(F32)).astype(BF16)


def iotas(rows, cols):
    return (
        lax.broadcasted_iota(jnp.int32, (rows, cols), 0),
        lax.broadcasted_iota(jnp.int32, (rows, cols), 1),
    )


def shrink_table(rows, cols, along_rows):
    i, j = iotas(rows, cols)
    hit = (i >> 2) == j if along_rows else i == (j >> 2)
    return jnp.where(hit, 0.25, 0.0).astype(BF16)


def expand_table(rows, cols, along_rows):
    i, j = iotas(rows, cols)
    hit = (i >> 2) == j if along_rows else i == (j >> 2)
    return jnp.where(hit, 1.0, 0.0).astype(BF16)


def block_mean(halves, split):
    table = shrink_table(32, 128, False)
    parts = [sum(mm(table, piece) for piece in split(half)) for half in halves]
    stacked = jnp.concatenate([part[:, k : k + 512] for k in (0, 512) for part in parts], axis=0)
    table = shrink_table(512, 128, True)
    small = sum(mm(piece, table) for piece in split(stacked))
    return jnp.concatenate([small[:64], small[64:]], axis=1)


def prolong(c, edges=False):
    if edges:
        i, j = iotas(128, 64)
        spot = 8 * (i >> 4) + ((i & 15) >> 2) + 4 * ((i & 15) >> 3)
        table = jnp.where(spot == j, 1.0, 0.0).astype(BF16)
    else:
        table = expand_table(256, 64, True)
    rows = table.shape[0]
    tall = sum(mm(table, piece) for piece in split2(c))
    stacked = jnp.concatenate([tall[:, :128], tall[:, 128:]], axis=0)
    table = expand_table(128, 512, False)
    wide = sum(mm(piece, table) for piece in split2(stacked))
    return jnp.concatenate([wide[:rows], wide[rows:]], axis=1)


def natural(blocks):
    rows = []
    for tall in range(blocks.shape[0] // 2):
        lanes = [
            blocks[2 * tall + wide // 4, 8 * (wide % 4) : 8 * (wide % 4) + 8, :]
            for wide in range(8)
        ]
        rows.append(jnp.concatenate(lanes, axis=1))
    return jnp.concatenate(rows, axis=0)


def for_each(v):
    return jnp.concatenate([v] * (128 // v.shape[0]), axis=0)


def halves_of(refs):
    if len(refs) == 1:
        return refs[0][:128], refs[0][128:]
    return [jnp.concatenate([refs[k][...], refs[k + 1][...]], axis=0) for k in (0, 2)]


def detail_kernel(v_ref, *refs):
    v = for_each(natural(v_ref))
    detail([x.astype(F32) * v for x in halves_of(refs[:4])], *refs[4:])


def first_detail_kernel(x_hbm, v_hbm, *refs):
    *out_refs, x_ref, v_ref, x_sems, v_sems = refs
    v_copies, x_copies = [], []
    for k in range(8):
        rows = pl.ds(16 * k, 16)
        v_copies.append(pltpu.make_async_copy(v_hbm.at[rows], v_ref.at[rows], v_sems.at[k]))
        rows = pl.ds(32 * k, 32)
        x_copies.append(pltpu.make_async_copy(x_hbm.at[rows], x_ref.at[rows], x_sems.at[k]))
    for copy in v_copies + x_copies:
        copy.start()
    for copy in v_copies + x_copies[:4]:
        copy.wait()
    first = x_ref[:128].astype(F32) * v_ref[...]
    for copy in x_copies[4:]:
        copy.wait()
    detail([first, x_ref[128:].astype(F32) * v_ref[...]], *out_refs)


def detail(halves, top_ref, bottom_ref, c_ref, own_ref=None):
    c = block_mean(halves, split3)
    if own_ref is None:
        for tile in range(TILES):
            c_ref[tile] = c
    else:
        c_ref[...] = c.reshape(PAIRS, 8, 256)
        own_ref[...] = c
    spread = prolong(c, edges=True)
    for pair in range(PAIRS):
        w, at = halves[pair // 4], ROWS * (pair % 4)
        top_ref[pair] = w[at : at + 8] - spread[16 * pair : 16 * pair + 8]
        bottom_ref[pair] = w[at + 24 : at + 32] - spread[16 * pair + 8 : 16 * pair + 16]


def row_table(taps, tile):
    i, j = iotas(160, 192)
    first = jnp.zeros((160, 192), F32)
    for k in range(4):
        row, col = i - 40 * k, j - 48 * k
        dist = jnp.abs(col - row - 4)
        spot, source = tile * ROWS - 4 + row, tile * ROWS - 8 + col
        fits = (row >= 0) & (row < 40) & (col >= 0) & (col < 48)
        fits = fits & (spot >= 0) & (spot < ROWS * TILES)
        fits = fits & (source >= 0) & (source < ROWS * TILES)
        dist = jnp.where(fits, dist, 9)
        for o in range(5):
            first = jnp.where(dist == o, taps[o][k], first)
    i, j = iotas(128, 160)
    second = jnp.zeros((128, 160), F32)
    for k in range(4):
        row, col = i - 32 * k, j - 40 * k
        fits = (row >= 0) & (row < 32) & (col >= 0) & (col < 40)
        dist = jnp.where(fits, jnp.abs(col - row - 4), 9)
        for o in range(5):
            second = jnp.where(dist == o, taps[o][k], second)
    return exact_mm(second, first)


def band_table(taps):
    i, j = iotas(8, 128)
    before, after = jnp.abs(i - 8 - j), jnp.abs(i + 128 - j)
    i, j = iotas(128, 128)
    inner = jnp.abs(i - j)
    left, right = jnp.zeros((8, 128), F32), jnp.zeros((8, 128), F32)
    middle = jnp.zeros((128, 128), F32)
    for o in range(9):
        left = jnp.where(before == o, taps[o], left)
        right = jnp.where(after == o, taps[o], right)
        middle = jnp.where(inner == o, taps[o], middle)
    rest = jnp.zeros((8, 128), F32)
    return jnp.concatenate([rest, left, middle, right, rest], axis=0)


def own_tile():
    return lax.axis_index("tile")


def own_group():
    return 8 * lax.axis_index("mem_0") + 2 * lax.axis_index("mem_1") + lax.axis_index("mem_2")


def taps_of(taps_ref):
    taps = taps_ref[...]
    square = taps * taps
    energy = square[:, 0:1] + 2.0 * jnp.sum(square[:, 1:5], axis=1, keepdims=True)
    taps = taps / jnp.sqrt(energy)
    single = [taps[:, o : o + 1] for o in range(5)]
    once = [single[abs(o)] for o in range(-4, 5)]
    double = []
    for o in range(9):
        terms = [once[i] * once[o + 8 - i] for i in range(o, 9)]
        double.append(functools.reduce(jnp.add, terms))
    lat = [[tap[k : k + 1] for k in range(4)] for tap in single]
    lon = [[tap[4 + k : 5 + k] for k in range(4)] for tap in double]
    return lat, lon


def fill_tables(lat, lon, tile, rows_ref, band_ref):
    for kind, piece in enumerate(split2(row_table(lat, tile))):
        rows_ref[kind] = piece
    for level in range(band_ref.shape[0]):
        for kind, piece in enumerate(split2(band_table([tap[level] for tap in lon]))):
            band_ref[level, kind] = piece


def table_kernel(taps_ref, lat_ref, lon_ref, x_ref, *refs):
    mix_ref, lats_ref, lons_ref, rows_ref, band_ref, *x_next_refs = refs
    tile, own = own_tile(), lax.axis_index("mem_0")

    def picked(values):
        value = values[3]
        for k in range(3):
            value = jnp.where(own == k, values[k], value)
        return value

    lat, lon = ([[picked(tap)] * 4 for tap in taps] for taps in taps_of(taps_ref))
    fill_tables(lat, lon, tile, rows_ref, band_ref)
    for ahead, x_next_ref in enumerate(x_next_refs):
        for member in range(2):
            row = ROWS * (4 * member + ((own + ahead) & 3))
            x_next_ref[ROWS * member : ROWS * member + ROWS] = x_ref[
                pl.ds(pl.multiple_of(row, ROWS), ROWS), :
            ]
    i, j = iotas(64, 512)
    repeat = jnp.where((i >> 3) == (j >> 6), jnp.where((i & 7) == (j & 7), 1.0, 0.0), 0.0)
    mine = lat_ref[pl.ds(pl.multiple_of(8 * tile, 8), 8), :]
    wide = exact_mm(mine, repeat)
    mix = jnp.concatenate([wide] * PAIRS, axis=0)
    mix = jnp.where((i >> 3) == ((j >> 3) & 7), mix, 0.0)
    for ref, value in ((mix_ref, mix), (lats_ref, lat_ref[...]), (lons_ref, lon_ref[...])):
        ref[0], ref[1] = split2(value)


def banded(band_ref, level, kind):
    band = band_ref[level, kind]
    edge, half = jnp.zeros((112, 128), BF16), jnp.zeros((128, 128), BF16)
    left = jnp.concatenate([edge, band, edge, half], axis=0)
    right = jnp.concatenate([half, edge, band, edge], axis=0)
    return jnp.concatenate([left, right], axis=1)


def windows(parts, first_row, height):
    rows = []
    for block in range(4):
        for part in parts:
            lanes = [
                part[first_row : first_row + height, 128 * tile : 128 * tile + 128]
                for tile in ((2 * block - 1) % 8, 2 * block, 2 * block + 1, (2 * block + 2) % 8)
            ]
            rows.append(jnp.concatenate(lanes, axis=1))
    return jnp.concatenate(rows, axis=0)


def lane_sums(values):
    i, j = iotas(8, 128)
    result = jnp.zeros((8, 128), F32)
    for lane, value in values:
        result = jnp.where((i == 0) & (j == lane), value, result)
    return result


def total(x):
    return jnp.sum(x, axis=(0, 1), keepdims=True)


def fine_kernel(last, *refs):
    if last:
        r_ref, v_ref, c_ref, *refs = refs
    else:
        *refs, f_ref, c_ref, rows_ref, band_ref, sem = refs
        v_ref, c_hbm, taps_ref, *refs = refs
        load = pltpu.make_async_copy(c_hbm.at[0], c_ref, sem)
        load.start()
        fill_tables(*taps_of(taps_ref), own_tile(), rows_ref, band_ref)
    before_ref, after_ref, *refs = refs
    if last:
        rows_ref, band_ref, *refs = refs
    x_refs, refs = (refs[:4], refs[4:]) if last else (refs[:1], refs[1:])
    halves = halves_of(x_refs)
    if last:
        fine_ref, mean_ref, sums_ref, f_ref = refs
        v = natural(v_ref)
    else:
        fine_ref, mean_ref = refs
        v = v_ref[...]
        load.wait()
    v_rows, spread = for_each(v), prolong(c_ref[...])
    highs, lows = [], []
    for part in range(2):
        d = halves[part].astype(F32) * v_rows - spread[128 * part : 128 * part + 128]
        rows = []
        for k in range(4):
            pair = 4 * part + k
            rows += [before_ref[pair], d[ROWS * k : ROWS * k + ROWS], after_ref[pair]]
        high, low = split2(jnp.concatenate(rows, axis=0))
        passed = mm3((rows_ref[0], rows_ref[1]), (high, low))
        high, low = split2(passed)
        highs.append(high)
        lows.append(low)
    levels = band_ref.shape[0]
    height = 128 // levels
    for level in range(levels):
        high = windows(highs, height * level, height)
        low = windows(lows, height * level, height)
        table_high, table_low = banded(band_ref, level, 0), banded(band_ref, level, 1)
        result = mm3((high, low), (table_high, table_low))
        for block in range(4):
            lanes = slice(256 * block, 256 * block + 256)
            summed = None
            for part in range(2):
                for inner in range(height // ROWS):
                    row = height * level + ROWS * inner
                    at = height * (2 * block + part) + ROWS * inner
                    f = result[at : at + ROWS]
                    f_ref[128 * part + row : 128 * part + row + ROWS, lanes] = f
                    term = halves[part][row : row + ROWS, lanes].astype(F32) * f
                    summed = term if summed is None else summed + term
            fine_ref[ROWS * level : ROWS * level + ROWS, lanes] = summed
    means = block_mean((f_ref[:128], f_ref[128:]), split2)
    mean_ref[...] = means
    if last:
        own = lax.axis_index("mem_0")
        r = r_ref[pl.ds(pl.multiple_of(ROWS * own, ROWS), ROWS), :]
        products = total(v * fine_ref[...]) - 16.0 * total(c_ref[...] * means)
        sums_ref[...] = lane_sums(
            ((0, total(r * r)), (1, total(r * v)), (2, total(v * v)), (3, products))
        )


def smooth_kernel(c_ref, lats_ref, lons_ref, sums_ref, out_ref):
    c = c_ref[...].reshape(64, 256)
    across = mm3((lats_ref[0], lats_ref[1]), split2(c))
    smoothed = mm3(split2(across), (lons_ref[0], lons_ref[1]))
    sums = sums_ref[...] + lane_sums([(4, 16.0 * total(c * smoothed))])
    for tile in range(TILES):
        out_ref[tile, 0:8, :] = smoothed[8 * tile : 8 * tile + 8, :128]
        out_ref[tile, 8:16, :] = smoothed[8 * tile : 8 * tile + 8, 128:]
        out_ref[tile, 16:24, :] = sums


def blended(x_refs, fine_ref, smoothed):
    spread, height = prolong(smoothed), fine_ref.shape[0]
    result = fine_ref[...]
    for k, x in enumerate(halves_of(x_refs)):
        product = x.astype(F32) * spread[128 * k : 128 * k + 128]
        for row in range(0, 128, height):
            result = result + product[row : row + height]
    return result


def partial_kernel(x_ref, fine_ref, mean_ref, c_ref, mix_ref, lons_ref, out_ref):
    across = mm3((mix_ref[0], mix_ref[1]), split2(c_ref[...].reshape(512, 256)))
    smoothed = mm3(split2(across), (lons_ref[0], lons_ref[1]))
    p = blended((x_ref,), fine_ref, smoothed - mean_ref[...])
    for tall in range(16):
        for wide in range(8):
            out_ref[2 * tall + wide // 4, 8 * (wide % 4) : 8 * (wide % 4) + 8, :] = p[
                8 * tall : 8 * tall + 8, 128 * wide : 128 * wide + 128
            ]


def packed(field):
    group = lax.broadcasted_iota(jnp.int32, (8, 128), 1) >> 5
    shares = []
    for wide in range(8):
        tiles = [field[8 * i : 8 * i + 8, 128 * wide : 128 * wide + 128] for i in range(4)]
        for g in range(4):
            share = None
            for i in range(4):
                turned = pltpu.roll(tiles[i], (32 * (i - g)) % 128, 1) if i != g else tiles[i]
                share = turned if share is None else jnp.where(group == i, turned, share)
            shares.append(share)
    return shares


def last_partial_kernel(fine_ref, mean_ref, smoothed_ref, v_ref, *refs):
    *x_refs, out_ref, v_packed = refs
    halves = [smoothed_ref[:, 8 * k : 8 * k + 8, :].reshape(64, 128) for k in range(2)]
    p = blended(x_refs, fine_ref, jnp.concatenate(halves, axis=1) - mean_ref[...])
    sums = jnp.sum(smoothed_ref[:, 16:24, :], axis=0)
    for group, share in enumerate(packed(natural(v_ref))):
        v_packed[group] = share
    mine = pl.ds(own_group() & 7, 1)
    for group, share in enumerate(packed(p)):
        out_ref[10 * group : 10 * group + 8] = share
        out_ref[10 * group + 8 : 10 * group + 9] = v_packed[group, mine, :]
        out_ref[10 * group + 9 : 10 * group + 10] = sums[:1]


def share_kernel(scale, arrived_ref, r_ref, out_ref):
    group = own_group()
    share = r_ref[
        pl.ds(pl.multiple_of(8 * (group >> 1), 8), 8),
        pl.ds(pl.multiple_of(512 * (group & 1), 512), 512),
    ]
    share = jnp.concatenate([share[:, 128 * k : 128 * k + 128] for k in range(4)], axis=0)
    share = share + jnp.sum(arrived_ref[...], axis=0) * scale
    for other in range(out_ref.shape[0]):
        out_ref[other] = share


def final_kernel(scale, arrived_ref, r_ref, x_out, res_out):
    group = own_group()
    lanes = pl.ds(pl.multiple_of(128 * (group >> 2), 128), 128)
    i, j = iotas(8, 128)
    sums = arrived_ref[9:10]
    for k in range(1, GROUPS):
        sums = sums + arrived_ref[10 * k + 9 : 10 * k + 10]
    rr, ra, aa, af, ac = (total(jnp.where(j[:1] == k, sums, 0.0)) for k in range(5))
    rr, ra, aa = rr / 8, ra / 8, aa / 8
    step = rr / ra
    ab = aa + (af + ac) * scale
    squares = step * step * aa - rr
    next_step = squares / ((ra - step * aa) - step * (aa - step * ab))
    for level in range(4):
        r = jnp.zeros((8, 128), F32)
        for k in range(4):
            row = ROWS * level + 8 * k
            tile = r_ref[row : row + 8, lanes]
            turned = pltpu.roll(tile, (32 * (k + 4 - (group & 3))) & 127, 1)
            r = jnp.where((j >> 5) == k, turned, r)
        at = [10 * (8 * level + k) for k in range(8)]
        a = jnp.concatenate([arrived_ref[k + 8 : k + 9] for k in at], axis=0)
        p = functools.reduce(jnp.add, [arrived_ref[k : k + 8] for k in at])
        b = a + p * scale
        r_next = r - step * a
        x_new = step * r + next_step * r_next
        res_new = r_next - next_step * (a - step * b)
        for k in range(4):
            x_out[level, 8 * k : 8 * k + 8, :] = x_new[:, 32 * k : 32 * k + 32]
            res_out[level, 8 * k : 8 * k + 8, :] = res_new[:, 32 * k : 32 * k + 32]


VMEM = pl.BlockSpec(memory_space=pltpu.VMEM)
HBM = pl.BlockSpec(memory_space=pltpu.HBM)


def call(kernel, outs, specs, args, flops, limit, scratch=(), out_specs=None):
    out_specs = out_specs or [VMEM] * len(outs)
    shapes = [
        pltpu.HBM(*out) if spec is HBM else jax.ShapeDtypeStruct(*out)
        for out, spec in zip(outs, out_specs)
    ]
    size = sum(a.size * a.dtype.itemsize for a in args)
    args = [
        pltpu.with_memory_space_constraint(arg, pltpu.HBM) if spec is HBM else arg
        for arg, spec in zip(args, specs)
    ]
    return pl.pallas_call(
        kernel,
        out_shape=shapes if len(shapes) > 1 else shapes[0],
        in_specs=specs,
        out_specs=out_specs if len(shapes) > 1 else out_specs[0],
        scratch_shapes=list(scratch),
        compiler_params=pltpu.CompilerParams(vmem_limit_bytes=limit << 20),
        cost_estimate=pl.CostEstimate(flops=flops, bytes_accessed=size, transcendentals=0),
    )(*args)


def exchange(blocks, axis):
    return lax.all_to_all(blocks, axis, 0, 0, tiled=True)


def local(perturbations, right_side, fine_taps, coarse_lat, coarse_lon):
    count, levels, height, extent = perturbations.shape
    members = count * lax.axis_size(MEM)
    scale = 1.0 / (members - 1)
    x = perturbations.reshape(count * levels * height, extent)
    r = right_side.reshape(levels * height, extent)
    half = ((128, LON), F32)
    edge = ((PAIRS, 8, LON), F32)
    shared = ((GROUPS, 32, 128), F32)
    up = [(i, (i + 1) % TILES) for i in range(TILES)]
    down = [(j, i) for i, j in up]

    def edges(top, bottom):
        return lax.ppermute(bottom, "tile", up), lax.ppermute(top, "tile", down)

    own = ((64, 256), F32)
    taps = fine_taps.reshape(2 * levels, 5)
    rows_shape, band_shape = (2, 128, 192), (2, 160, 128)
    top, bottom, c = call(
        first_detail_kernel,
        [edge, edge, ((TILES, 64, 256), F32)],
        [HBM] * 2,
        (x, r),
        10**9,
        12,
        scratch=(
            pltpu.VMEM((256, LON), BF16),
            pltpu.VMEM((128, LON), F32),
            pltpu.SemaphoreType.DMA((8,)),
            pltpu.SemaphoreType.DMA((8,)),
        ),
    )
    before, after = edges(top, bottom)
    c_first = exchange(c, "tile")
    before, x_again = lax.optimization_barrier((before, x))
    mix, lats, lons, rows_next, band_next, *x_next = call(
        table_kernel,
        [
            ((2, 64, 512), BF16),
            ((2, 64, 64), BF16),
            ((2, 256, 256), BF16),
            (rows_shape, BF16),
            ((1, *band_shape), BF16),
            *[((count * height, extent), BF16)] * 4,
        ],
        [VMEM] * 4,
        (taps, coarse_lat, coarse_lon, x_again),
        10**11,
        6,
    )
    before, mix = lax.optimization_barrier((before, mix))
    for ahead in range(1, 4):
        ring = [(i, (i + ahead) % 4) for i in range(4)]
        x_next[ahead] = lax.ppermute(x_next[ahead], "mem_0", ring)
    fine_scratch = [pltpu.VMEM((256, LON), F32)]
    fine, means = call(
        functools.partial(fine_kernel, False),
        [half, own],
        [VMEM, HBM] + [VMEM] * 4,
        (r, c, taps, before, after, x),
        10**11,
        16,
        scratch=[
            *fine_scratch,
            pltpu.VMEM(*own),
            pltpu.VMEM(rows_shape, BF16),
            pltpu.VMEM((levels, *band_shape), BF16),
            pltpu.SemaphoreType.DMA,
        ],
    )
    fine, x_next = lax.optimization_barrier((fine, x_next))
    shares = call(
        partial_kernel,
        [shared],
        [VMEM] * 6,
        (x, fine, means, c_first, mix, lons),
        10**9,
        12,
    )
    arrived = exchange(shares, MEM)
    share = call(
        functools.partial(share_kernel, scale),
        [((TILES, 32, 128), F32)],
        [VMEM, VMEM],
        (arrived, r),
        10**6,
        6,
    )
    a = exchange(share, ("mem_1", "mem_2"))

    top, bottom, c, c_own = call(
        detail_kernel,
        [edge, edge, ((PAIRS, 8, 256), F32), own],
        [VMEM] * 5,
        (a, *x_next),
        10**9,
        12,
    )
    beside = edges(top, bottom)
    c = exchange(c, "tile")
    level = ((height, LON), F32)
    fine, means, sums = call(
        functools.partial(fine_kernel, True),
        [level, own, ((8, 128), F32)],
        [VMEM] * 11,
        (r, a, c_own, *beside, rows_next, band_next, *x_next),
        10**11,
        16,
        scratch=fine_scratch,
    )
    smoothed = call(
        smooth_kernel,
        [((TILES, 24, 128), F32)],
        [VMEM] * 4,
        (c, lats, lons, sums),
        10**8,
        6,
    )
    smoothed = exchange(smoothed, "tile")
    shares = call(
        last_partial_kernel,
        [((GROUPS * 10, 128), F32)],
        [VMEM] * 8,
        (fine, means, smoothed, a, *x_next),
        10**9,
        12,
        scratch=[pltpu.VMEM((GROUPS, 8, 128), F32)],
    )
    arrived = exchange(shares.reshape(GROUPS, 1, 1280), MEM).reshape(shares.shape)
    out = ((levels, height, extent // GROUPS), F32)
    return tuple(
        call(
            functools.partial(final_kernel, scale),
            [out, out],
            [VMEM, VMEM],
            (arrived, r),
            10**6,
            6,
        )
    )


def solution(mesh):
    torus = Mesh(
        mesh.devices.reshape(4, 4, 2, mesh.shape["tile"]), ("mem_0", "mem_1", "mem_2", "tile")
    )
    placed = (P(MEM, None, "tile", None), P(None, "tile", None), P(), P(), P())
    return jax.shard_map(
        local,
        mesh=torus,
        in_specs=placed,
        out_specs=(P(None, "tile", MEM), P(None, "tile", MEM)),
        check_vma=False,
    )
```

```python
import functools

import jax
import jax.numpy as jnp
from jax import lax
from jax.experimental import pallas as pl
from jax.experimental.pallas import tpu as pltpu
from jax.sharding import Mesh
from jax.sharding import PartitionSpec as P

MEM = ("mem_0", "mem_1", "mem_2")
F32 = jnp.float32
BF16 = jnp.bfloat16
EXACT = lax.Precision.HIGHEST
PAIRS, ROWS, LON = 8, 32, 1024
GROUPS, TILES = 32, 8


def mm(a, b):
    return jnp.dot(a, b, preferred_element_type=F32)


def exact_mm(a, b):
    return jnp.dot(a, b, preferred_element_type=F32, precision=EXACT)


def split2(x):
    high = x.astype(BF16)
    return high, (x - high.astype(F32)).astype(BF16)


def mm3(a, b):
    return mm(a[0], b[0]) + mm(a[0], b[1]) + mm(a[1], b[0])


def split3(x):
    high = x.astype(BF16)
    rest = x - high.astype(F32)
    mid = rest.astype(BF16)
    return high, mid, (rest - mid.astype(F32)).astype(BF16)


def iotas(rows, cols):
    return (
        lax.broadcasted_iota(jnp.int32, (rows, cols), 0),
        lax.broadcasted_iota(jnp.int32, (rows, cols), 1),
    )


def shrink_table(rows, cols, along_rows):
    i, j = iotas(rows, cols)
    hit = (i >> 2) == j if along_rows else i == (j >> 2)
    return jnp.where(hit, 0.25, 0.0).astype(BF16)


def expand_table(rows, cols, along_rows):
    i, j = iotas(rows, cols)
    hit = (i >> 2) == j if along_rows else i == (j >> 2)
    return jnp.where(hit, 1.0, 0.0).astype(BF16)


def block_mean(halves, split):
    table = shrink_table(32, 128, False)
    parts = [sum(mm(table, piece) for piece in split(half)) for half in halves]
    stacked = jnp.concatenate([part[:, k : k + 512] for k in (0, 512) for part in parts], axis=0)
    table = shrink_table(512, 128, True)
    small = sum(mm(piece, table) for piece in split(stacked))
    return jnp.concatenate([small[:64], small[64:]], axis=1)


def prolong(c, edges=False):
    if edges:
        i, j = iotas(128, 64)
        spot = 8 * (i >> 4) + ((i & 15) >> 2) + 4 * ((i & 15) >> 3)
        table = jnp.where(spot == j, 1.0, 0.0).astype(BF16)
    else:
        table = expand_table(256, 64, True)
    rows = table.shape[0]
    tall = sum(mm(table, piece) for piece in split2(c))
    stacked = jnp.concatenate([tall[:, :128], tall[:, 128:]], axis=0)
    table = expand_table(128, 512, False)
    wide = sum(mm(piece, table) for piece in split2(stacked))
    return jnp.concatenate([wide[:rows], wide[rows:]], axis=1)


def natural(blocks):
    rows = []
    for tall in range(blocks.shape[0] // 2):
        lanes = [
            blocks[2 * tall + wide // 4, 8 * (wide % 4) : 8 * (wide % 4) + 8, :]
            for wide in range(8)
        ]
        rows.append(jnp.concatenate(lanes, axis=1))
    return jnp.concatenate(rows, axis=0)


def for_each(v):
    return jnp.concatenate([v] * (128 // v.shape[0]), axis=0)


def halves_of(refs):
    if len(refs) == 1:
        return refs[0][:128], refs[0][128:]
    return [jnp.concatenate([refs[k][...], refs[k + 1][...]], axis=0) for k in (0, 2)]


def detail_kernel(v_ref, *refs):
    v = for_each(natural(v_ref))
    detail([x.astype(F32) * v for x in halves_of(refs[:4])], *refs[4:])


def first_detail_kernel(x_hbm, v_hbm, *refs):
    *out_refs, x_ref, v_ref, x_sems, v_sems = refs
    v_copies, x_copies = [], []
    for k in range(8):
        rows = pl.ds(16 * k, 16)
        v_copies.append(pltpu.make_async_copy(v_hbm.at[rows], v_ref.at[rows], v_sems.at[k]))
        rows = pl.ds(32 * k, 32)
        x_copies.append(pltpu.make_async_copy(x_hbm.at[rows], x_ref.at[rows], x_sems.at[k]))
    for copy in v_copies + x_copies:
        copy.start()
    for copy in v_copies + x_copies[:4]:
        copy.wait()
    first = x_ref[:128].astype(F32) * v_ref[...]
    for copy in x_copies[4:]:
        copy.wait()
    detail([first, x_ref[128:].astype(F32) * v_ref[...]], *out_refs)


def detail(halves, top_ref, bottom_ref, c_ref, own_ref=None):
    c = block_mean(halves, split3)
    if own_ref is None:
        for tile in range(TILES):
            c_ref[tile] = c
    else:
        c_ref[...] = c.reshape(PAIRS, 8, 256)
        own_ref[...] = c
    spread = prolong(c, edges=True)
    for pair in range(PAIRS):
        w, at = halves[pair // 4], ROWS * (pair % 4)
        top_ref[pair] = w[at : at + 8] - spread[16 * pair : 16 * pair + 8]
        bottom_ref[pair] = w[at + 24 : at + 32] - spread[16 * pair + 8 : 16 * pair + 16]


def row_table(taps, tile):
    i, j = iotas(160, 192)
    first = jnp.zeros((160, 192), F32)
    for k in range(4):
        row, col = i - 40 * k, j - 48 * k
        dist = jnp.abs(col - row - 4)
        spot, source = tile * ROWS - 4 + row, tile * ROWS - 8 + col
        fits = (row >= 0) & (row < 40) & (col >= 0) & (col < 48)
        fits = fits & (spot >= 0) & (spot < ROWS * TILES)
        fits = fits & (source >= 0) & (source < ROWS * TILES)
        dist = jnp.where(fits, dist, 9)
        for o in range(5):
            first = jnp.where(dist == o, taps[o][k], first)
    i, j = iotas(128, 160)
    second = jnp.zeros((128, 160), F32)
    for k in range(4):
        row, col = i - 32 * k, j - 40 * k
        fits = (row >= 0) & (row < 32) & (col >= 0) & (col < 40)
        dist = jnp.where(fits, jnp.abs(col - row - 4), 9)
        for o in range(5):
            second = jnp.where(dist == o, taps[o][k], second)
    return exact_mm(second, first)


def band_table(taps):
    i, j = iotas(8, 128)
    before, after = jnp.abs(i - 8 - j), jnp.abs(i + 128 - j)
    i, j = iotas(128, 128)
    inner = jnp.abs(i - j)
    left, right = jnp.zeros((8, 128), F32), jnp.zeros((8, 128), F32)
    middle = jnp.zeros((128, 128), F32)
    for o in range(9):
        left = jnp.where(before == o, taps[o], left)
        right = jnp.where(after == o, taps[o], right)
        middle = jnp.where(inner == o, taps[o], middle)
    rest = jnp.zeros((8, 128), F32)
    return jnp.concatenate([rest, left, middle, right, rest], axis=0)


def own_tile():
    return lax.axis_index("tile")


def own_group():
    return 8 * lax.axis_index("mem_0") + 2 * lax.axis_index("mem_1") + lax.axis_index("mem_2")


def taps_of(taps_ref):
    taps = taps_ref[...]
    square = taps * taps
    energy = square[:, 0:1] + 2.0 * jnp.sum(square[:, 1:5], axis=1, keepdims=True)
    taps = taps / jnp.sqrt(energy)
    single = [taps[:, o : o + 1] for o in range(5)]
    once = [single[abs(o)] for o in range(-4, 5)]
    double = []
    for o in range(9):
        terms = [once[i] * once[o + 8 - i] for i in range(o, 9)]
        double.append(functools.reduce(jnp.add, terms))
    lat = [[tap[k : k + 1] for k in range(4)] for tap in single]
    lon = [[tap[4 + k : 5 + k] for k in range(4)] for tap in double]
    return lat, lon


def fill_tables(lat, lon, tile, rows_ref, band_ref):
    for kind, piece in enumerate(split2(row_table(lat, tile))):
        rows_ref[kind] = piece
    for level in range(band_ref.shape[0]):
        for kind, piece in enumerate(split2(band_table([tap[level] for tap in lon]))):
            band_ref[level, kind] = piece


def table_kernel(x_hbm, r_hbm, taps_ref, lat_ref, lon_ref, *refs):
    *refs, lats_ref, rows_ref, band_ref, lanes_ref, sems = refs
    mix_ref, lons_ref, share_ref, level_ref, packed_ref, *refs = refs
    x_next_refs, hbm_refs = refs[:4], refs[4:]
    tile, own, group = own_tile(), lax.axis_index("mem_0"), own_group()
    lanes = pl.ds(pl.multiple_of(128 * (group >> 2), 128), 128)
    pieces = [
        (r_hbm.at[:, lanes], lanes_ref),
        (r_hbm.at[pl.ds(pl.multiple_of(ROWS * own, ROWS), ROWS)], level_ref),
    ]
    for k in range(4):
        at = pl.multiple_of(512 * (group & 1) + 128 * k, 128)
        rows = pl.ds(pl.multiple_of(8 * (group >> 1), 8), 8)
        pieces.append((r_hbm.at[rows, pl.ds(at, 128)], share_ref.at[pl.ds(8 * k, 8)]))
    for ahead, x_next_ref in enumerate(x_next_refs):
        for member in range(2):
            row = pl.multiple_of(ROWS * (4 * member + ((own + ahead) & 3)), ROWS)
            target = x_next_ref.at[pl.ds(ROWS * member, ROWS)]
            pieces.append((x_hbm.at[pl.ds(row, ROWS)], target))
    loads = [
        pltpu.make_async_copy(source, target, sems.at[3 + k])
        for k, (source, target) in enumerate(pieces)
    ]
    for load in loads:
        load.start()

    def picked(values):
        value = values[3]
        for k in range(3):
            value = jnp.where(own == k, values[k], value)
        return value

    lat, lon = ([[picked(tap)] * 4 for tap in taps] for taps in taps_of(taps_ref))
    fill_tables(lat, lon, tile, rows_ref, band_ref)
    lats_ref[0], lats_ref[1] = split2(lat_ref[...])
    copies = [
        pltpu.make_async_copy(source, target, sems.at[k])
        for k, (source, target) in enumerate(zip((lats_ref, rows_ref, band_ref), hbm_refs))
    ]
    for copy in copies:
        copy.start()
    i, j = iotas(64, 512)
    repeat = jnp.where((i >> 3) == (j >> 6), jnp.where((i & 7) == (j & 7), 1.0, 0.0), 0.0)
    mine = lat_ref[pl.ds(pl.multiple_of(8 * tile, 8), 8), :]
    wide = exact_mm(mine, repeat)
    mix = jnp.concatenate([wide] * PAIRS, axis=0)
    mix = jnp.where((i >> 3) == ((j >> 3) & 7), mix, 0.0)
    mix_ref[0], mix_ref[1] = split2(mix)
    lons_ref[0], lons_ref[1] = split2(lon_ref[...])
    for load in loads:
        load.wait()
    j = lax.broadcasted_iota(jnp.int32, (8, 128), 1)
    for level in range(4):
        packed_r = jnp.zeros((8, 128), F32)
        for k in range(4):
            row = ROWS * level + 8 * k
            shift = (32 * (k + 4 - (group & 3))) & 127
            turned = pltpu.roll(lanes_ref[row : row + 8], shift, 1)
            packed_r = jnp.where((j >> 5) == k, turned, packed_r)
        packed_ref[level] = packed_r
    for copy in copies:
        copy.wait()


def banded(band_ref, level, kind):
    band = band_ref[level, kind]
    edge, half = jnp.zeros((112, 128), BF16), jnp.zeros((128, 128), BF16)
    left = jnp.concatenate([edge, band, edge, half], axis=0)
    right = jnp.concatenate([half, edge, band, edge], axis=0)
    return jnp.concatenate([left, right], axis=1)


def windows(parts, first_row, height):
    rows = []
    for block in range(4):
        for part in parts:
            lanes = [
                part[first_row : first_row + height, 128 * tile : 128 * tile + 128]
                for tile in ((2 * block - 1) % 8, 2 * block, 2 * block + 1, (2 * block + 2) % 8)
            ]
            rows.append(jnp.concatenate(lanes, axis=1))
    return jnp.concatenate(rows, axis=0)


def lane_sums(values):
    i, j = iotas(8, 128)
    result = jnp.zeros((8, 128), F32)
    for lane, value in values:
        result = jnp.where((i == 0) & (j == lane), value, result)
    return result


def total(x):
    return jnp.sum(x, axis=(0, 1), keepdims=True)


def fine_kernel(last, *refs):
    if last:
        r_ref, v_ref, c_ref, *refs = refs
    else:
        *refs, f_ref, c_ref, v_ref, x_ref, rows_ref, band_ref, sems = refs
        v_hbm, c_hbm, x_hbm, taps_ref, *refs = refs
        loads = [
            pltpu.make_async_copy(source, target, sems.at[k])
            for k, (source, target) in enumerate(
                ((c_hbm.at[0], c_ref), (v_hbm, v_ref), (x_hbm, x_ref))
            )
        ]
        for load in loads:
            load.start()
        fill_tables(*taps_of(taps_ref), own_tile(), rows_ref, band_ref)
    before_ref, after_ref, *refs = refs
    if last:
        rows_ref, band_ref, *refs = refs
    x_refs, refs = (refs[:4], refs[4:]) if last else ((x_ref,), refs)
    if last:
        fine_ref, mean_ref, sums_ref, f_ref = refs
        v = natural(v_ref)
    else:
        fine_ref, mean_ref = refs
        for load in loads:
            load.wait()
        v = v_ref[...]
    halves = halves_of(x_refs)
    v_rows, spread = for_each(v), prolong(c_ref[...])
    highs, lows = [], []
    for part in range(2):
        d = halves[part].astype(F32) * v_rows - spread[128 * part : 128 * part + 128]
        rows = []
        for k in range(4):
            pair = 4 * part + k
            rows += [before_ref[pair], d[ROWS * k : ROWS * k + ROWS], after_ref[pair]]
        high, low = split2(jnp.concatenate(rows, axis=0))
        passed = mm3((rows_ref[0], rows_ref[1]), (high, low))
        high, low = split2(passed)
        highs.append(high)
        lows.append(low)
    levels = band_ref.shape[0]
    height = 128 // levels
    for level in range(levels):
        high = windows(highs, height * level, height)
        low = windows(lows, height * level, height)
        table_high, table_low = banded(band_ref, level, 0), banded(band_ref, level, 1)
        result = mm3((high, low), (table_high, table_low))
        for block in range(4):
            lanes = slice(256 * block, 256 * block + 256)
            summed = None
            for part in range(2):
                for inner in range(height // ROWS):
                    row = height * level + ROWS * inner
                    at = height * (2 * block + part) + ROWS * inner
                    f = result[at : at + ROWS]
                    f_ref[128 * part + row : 128 * part + row + ROWS, lanes] = f
                    term = halves[part][row : row + ROWS, lanes].astype(F32) * f
                    summed = term if summed is None else summed + term
            fine_ref[ROWS * level : ROWS * level + ROWS, lanes] = summed
    means = block_mean((f_ref[:128], f_ref[128:]), split2)
    mean_ref[...] = means
    if last:
        r = r_ref[...]
        products = total(v * fine_ref[...]) - 16.0 * total(c_ref[...] * means)
        sums_ref[...] = lane_sums(
            ((0, total(r * r)), (1, total(r * v)), (2, total(v * v)), (3, products))
        )


def smooth_kernel(c_ref, lats_ref, lons_ref, sums_ref, out_ref):
    c = c_ref[...].reshape(64, 256)
    across = mm3((lats_ref[0], lats_ref[1]), split2(c))
    smoothed = mm3(split2(across), (lons_ref[0], lons_ref[1]))
    sums = sums_ref[...] + lane_sums([(4, 16.0 * total(c * smoothed))])
    for tile in range(TILES):
        out_ref[tile, 0:8, :] = smoothed[8 * tile : 8 * tile + 8, :128]
        out_ref[tile, 8:16, :] = smoothed[8 * tile : 8 * tile + 8, 128:]
        out_ref[tile, 16:24, :] = sums


def blended(x_refs, fine_ref, smoothed, loads=()):
    spread, height = prolong(smoothed), fine_ref.shape[0]
    for load in loads:
        load.wait()
    result = fine_ref[...]
    for k, x in enumerate(halves_of(x_refs)):
        product = x.astype(F32) * spread[128 * k : 128 * k + 128]
        for row in range(0, 128, height):
            result = result + product[row : row + height]
    return result


def partial_kernel(x_hbm, c_hbm, fine_ref, mean_ref, mix_ref, lons_ref, out_ref, *refs):
    x_ref, c_ref, sems = refs
    spans = [(c_hbm, c_ref, k, 1) for k in range(TILES)]
    spans += [(x_hbm, x_ref, 64 * k, 64) for k in range(4)]
    loads = [
        pltpu.make_async_copy(source.at[pl.ds(at, size)], target.at[pl.ds(at, size)], sems.at[k])
        for k, (source, target, at, size) in enumerate(spans)
    ]
    for load in loads:
        load.start()
    across = None
    for part in range(2):
        for load in loads[4 * part : 4 * part + 4]:
            load.wait()
        lanes = slice(256 * part, 256 * part + 256)
        c = c_ref[4 * part : 4 * part + 4].reshape(256, 256)
        term = mm3((mix_ref[0, :, lanes], mix_ref[1, :, lanes]), split2(c))
        across = term if across is None else across + term
    smoothed = mm3(split2(across), (lons_ref[0], lons_ref[1])) - mean_ref[...]
    p = blended((x_ref,), fine_ref, smoothed, loads[8:])
    for tall in range(16):
        for wide in range(8):
            out_ref[2 * tall + wide // 4, 8 * (wide % 4) : 8 * (wide % 4) + 8, :] = p[
                8 * tall : 8 * tall + 8, 128 * wide : 128 * wide + 128
            ]


def packed(field):
    group = lax.broadcasted_iota(jnp.int32, (8, 128), 1) >> 5
    shares = []
    for wide in range(8):
        tiles = [field[8 * i : 8 * i + 8, 128 * wide : 128 * wide + 128] for i in range(4)]
        for g in range(4):
            share = None
            for i in range(4):
                turned = pltpu.roll(tiles[i], (32 * (i - g)) % 128, 1) if i != g else tiles[i]
                share = turned if share is None else jnp.where(group == i, turned, share)
            shares.append(share)
    return shares


def last_partial_kernel(fine_ref, mean_ref, smoothed_ref, v_ref, *refs):
    *x_refs, out_ref, v_packed = refs
    halves = [smoothed_ref[:, 8 * k : 8 * k + 8, :].reshape(64, 128) for k in range(2)]
    p = blended(x_refs, fine_ref, jnp.concatenate(halves, axis=1) - mean_ref[...])
    sums = jnp.sum(smoothed_ref[:, 16:24, :], axis=0)
    for group, share in enumerate(packed(natural(v_ref))):
        v_packed[group] = share
    mine = pl.ds(own_group() & 7, 1)
    for group, share in enumerate(packed(p)):
        out_ref[10 * group : 10 * group + 8] = share
        out_ref[10 * group + 8 : 10 * group + 9] = v_packed[group, mine, :]
        out_ref[10 * group + 9 : 10 * group + 10] = sums[:1]


def share_kernel(scale, arrived_ref, r_ref, out_ref):
    share = r_ref[...] + jnp.sum(arrived_ref[...], axis=0) * scale
    for other in range(out_ref.shape[0]):
        out_ref[other] = share


def final_kernel(scale, arrived_ref, r_ref, x_out, res_out):
    i, j = iotas(8, 128)
    sums = arrived_ref[9:10]
    for k in range(1, GROUPS):
        sums = sums + arrived_ref[10 * k + 9 : 10 * k + 10]
    rr, ra, aa, af, ac = (total(jnp.where(j[:1] == k, sums, 0.0)) for k in range(5))
    rr, ra, aa = rr / 8, ra / 8, aa / 8
    step = rr / ra
    ab = aa + (af + ac) * scale
    squares = step * step * aa - rr
    next_step = squares / ((ra - step * aa) - step * (aa - step * ab))
    for level in range(4):
        r = r_ref[level]
        at = [10 * (8 * level + k) for k in range(8)]
        a = jnp.concatenate([arrived_ref[k + 8 : k + 9] for k in at], axis=0)
        p = functools.reduce(jnp.add, [arrived_ref[k : k + 8] for k in at])
        b = a + p * scale
        r_next = r - step * a
        x_new = step * r + next_step * r_next
        res_new = r_next - next_step * (a - step * b)
        for k in range(4):
            x_out[level, 8 * k : 8 * k + 8, :] = x_new[:, 32 * k : 32 * k + 32]
            res_out[level, 8 * k : 8 * k + 8, :] = res_new[:, 32 * k : 32 * k + 32]


VMEM = pl.BlockSpec(memory_space=pltpu.VMEM)
HBM = pl.BlockSpec(memory_space=pltpu.HBM)


def call(kernel, outs, specs, args, flops, limit, scratch=(), out_specs=None):
    out_specs = out_specs or [VMEM] * len(outs)
    shapes = [
        pltpu.HBM(*out) if spec is HBM else jax.ShapeDtypeStruct(*out)
        for out, spec in zip(outs, out_specs)
    ]
    size = sum(a.size * a.dtype.itemsize for a in args)
    args = [
        pltpu.with_memory_space_constraint(arg, pltpu.HBM) if spec is HBM else arg
        for arg, spec in zip(args, specs)
    ]
    return pl.pallas_call(
        kernel,
        out_shape=shapes if len(shapes) > 1 else shapes[0],
        in_specs=specs,
        out_specs=out_specs if len(shapes) > 1 else out_specs[0],
        scratch_shapes=list(scratch),
        compiler_params=pltpu.CompilerParams(vmem_limit_bytes=limit << 20),
        cost_estimate=pl.CostEstimate(flops=flops, bytes_accessed=size, transcendentals=0),
    )(*args)


def exchange(blocks, axis):
    return lax.all_to_all(blocks, axis, 0, 0, tiled=True)


def local(perturbations, right_side, fine_taps, coarse_lat, coarse_lon):
    count, levels, height, extent = perturbations.shape
    members = count * lax.axis_size(MEM)
    scale = 1.0 / (members - 1)
    x = perturbations.reshape(count * levels * height, extent)
    r = right_side.reshape(levels * height, extent)
    half = ((128, LON), F32)
    edge = ((PAIRS, 8, LON), F32)
    shared = ((GROUPS, 32, 128), F32)
    up = [(i, (i + 1) % TILES) for i in range(TILES)]
    down = [(j, i) for i, j in up]

    def edges(top, bottom):
        return lax.ppermute(bottom, "tile", up), lax.ppermute(top, "tile", down)

    own = ((64, 256), F32)
    taps = fine_taps.reshape(2 * levels, 5)
    rows_shape, band_shape = (2, 128, 192), (2, 160, 128)
    top, bottom, c = call(
        first_detail_kernel,
        [edge, edge, ((TILES, 64, 256), F32)],
        [HBM] * 2,
        (x, r),
        10**9,
        12,
        scratch=(
            pltpu.VMEM((256, LON), BF16),
            pltpu.VMEM((128, LON), F32),
            pltpu.SemaphoreType.DMA((8,)),
            pltpu.SemaphoreType.DMA((8,)),
        ),
    )
    before, after = edges(top, bottom)
    c_first = exchange(c, "tile")
    before, x_again = lax.optimization_barrier((before, x))
    next_tables = [((2, 64, 64), BF16), (rows_shape, BF16), ((1, *band_shape), BF16)]
    level = ((height, LON), F32)
    outs = [
        ((2, 64, 512), BF16),
        ((2, 256, 256), BF16),
        ((32, 128), F32),
        level,
        ((levels, 8, 128), F32),
        *[((count * height, extent), BF16)] * 4,
    ]
    mix, lons, r_share, r_level, r_packed, *x_next = call(
        table_kernel,
        outs + next_tables,
        [HBM] * 2 + [VMEM] * 3,
        (x_again, r, taps, coarse_lat, coarse_lon),
        10**11,
        6,
        scratch=[
            *(pltpu.VMEM(*shape) for shape in next_tables),
            pltpu.VMEM((128, 128), F32),
            pltpu.SemaphoreType.DMA((17,)),
        ],
        out_specs=[VMEM] * len(outs) + [HBM] * 3,
    )
    *x_next, lats, rows_next, band_next = x_next
    before, mix = lax.optimization_barrier((before, mix))
    for ahead in range(1, 4):
        ring = [(i, (i + ahead) % 4) for i in range(4)]
        x_next[ahead] = lax.ppermute(x_next[ahead], "mem_0", ring)
    fine_scratch = [pltpu.VMEM((256, LON), F32)]
    fine, means = call(
        functools.partial(fine_kernel, False),
        [half, own],
        [HBM] * 3 + [VMEM] * 3,
        (r, c, x, taps, before, after),
        10**11,
        16,
        scratch=[
            *fine_scratch,
            pltpu.VMEM(*own),
            pltpu.VMEM(r.shape, F32),
            pltpu.VMEM(x.shape, BF16),
            pltpu.VMEM(rows_shape, BF16),
            pltpu.VMEM((levels, *band_shape), BF16),
            pltpu.SemaphoreType.DMA((3,)),
        ],
    )
    fine, x_next = lax.optimization_barrier((fine, x_next))
    shares = call(
        partial_kernel,
        [shared],
        [HBM] * 2 + [VMEM] * 4,
        (x, c_first, fine, means, mix, lons),
        10**9,
        12,
        scratch=[
            pltpu.VMEM(x.shape, BF16),
            pltpu.VMEM(c.shape, F32),
            pltpu.SemaphoreType.DMA((12,)),
        ],
    )
    arrived = exchange(shares, MEM)
    share = call(
        functools.partial(share_kernel, scale),
        [((TILES, 32, 128), F32)],
        [VMEM, VMEM],
        (arrived, r_share),
        10**6,
        6,
    )
    a = exchange(share, ("mem_1", "mem_2"))

    top, bottom, c, c_own = call(
        detail_kernel,
        [edge, edge, ((PAIRS, 8, 256), F32), own],
        [VMEM] * 5,
        (a, *x_next),
        10**9,
        12,
    )
    beside = edges(top, bottom)
    c = exchange(c, "tile")
    fine, means, sums = call(
        functools.partial(fine_kernel, True),
        [level, own, ((8, 128), F32)],
        [VMEM] * 11,
        (r_level, a, c_own, *beside, rows_next, band_next, *x_next),
        10**11,
        16,
        scratch=fine_scratch,
    )
    smoothed = call(
        smooth_kernel,
        [((TILES, 24, 128), F32)],
        [VMEM] * 4,
        (c, lats, lons, sums),
        10**8,
        6,
    )
    smoothed = exchange(smoothed, "tile")
    shares = call(
        last_partial_kernel,
        [((GROUPS * 10, 128), F32)],
        [VMEM] * 8,
        (fine, means, smoothed, a, *x_next),
        10**9,
        12,
        scratch=[pltpu.VMEM((GROUPS, 8, 128), F32)],
    )
    arrived = exchange(shares.reshape(GROUPS, 1, 1280), MEM).reshape(shares.shape)
    out = ((levels, height, extent // GROUPS), F32)
    return tuple(
        call(
            functools.partial(final_kernel, scale),
            [out, out],
            [VMEM, VMEM],
            (arrived, r_packed),
            10**6,
            6,
        )
    )


def solution(mesh):
    torus = Mesh(
        mesh.devices.reshape(4, 4, 2, mesh.shape["tile"]), ("mem_0", "mem_1", "mem_2", "tile")
    )
    placed = (P(MEM, None, "tile", None), P(None, "tile", None), P(), P(), P())
    return jax.shard_map(
        local,
        mesh=torus,
        in_specs=placed,
        out_specs=(P(None, "tile", MEM), P(None, "tile", MEM)),
        check_vma=False,
    )
```

```python
import functools

import jax
import jax.numpy as jnp
from jax import lax
from jax.experimental import pallas as pl
from jax.experimental.pallas import tpu as pltpu
from jax.sharding import Mesh
from jax.sharding import PartitionSpec as P

MEM = ("mem_0", "mem_1", "mem_2")
F32 = jnp.float32
BF16 = jnp.bfloat16
EXACT = lax.Precision.HIGHEST
PAIRS, ROWS, LON = 8, 32, 1024
GROUPS, TILES = 32, 8


def mm(a, b):
    return jnp.dot(a, b, preferred_element_type=F32)


def exact_mm(a, b):
    return jnp.dot(a, b, preferred_element_type=F32, precision=EXACT)


def split2(x):
    high = x.astype(BF16)
    return high, (x - high.astype(F32)).astype(BF16)


def mm3(a, b):
    return mm(a[0], b[0]) + mm(a[0], b[1]) + mm(a[1], b[0])


def iotas(rows, cols):
    return (
        lax.broadcasted_iota(jnp.int32, (rows, cols), 0),
        lax.broadcasted_iota(jnp.int32, (rows, cols), 1),
    )


def shrink_table(rows, cols, along_rows):
    i, j = iotas(rows, cols)
    hit = (i >> 2) == j if along_rows else i == (j >> 2)
    return jnp.where(hit, 0.25, 0.0).astype(BF16)


def expand_table(rows, cols, along_rows):
    i, j = iotas(rows, cols)
    hit = (i >> 2) == j if along_rows else i == (j >> 2)
    return jnp.where(hit, 1.0, 0.0).astype(BF16)


def lat_mean(field):
    table = shrink_table(field.shape[0] // 4, field.shape[0], False)
    return sum(mm(table, piece) for piece in split2(field))


def lon_mean(parts):
    stacked = jnp.concatenate([part[:, k : k + 512] for k in (0, 512) for part in parts], axis=0)
    table = shrink_table(512, 128, True)
    small = sum(mm(piece, table) for piece in split2(stacked))
    return jnp.concatenate([small[:64], small[64:]], axis=1)


def prolong(c, edges=False):
    if edges:
        i, j = iotas(128, 64)
        spot = 8 * (i >> 4) + ((i & 15) >> 2) + 4 * ((i & 15) >> 3)
        table = jnp.where(spot == j, 1.0, 0.0).astype(BF16)
    else:
        table = expand_table(256, 64, True)
    rows = table.shape[0]
    tall = sum(mm(table, piece) for piece in split2(c))
    stacked = jnp.concatenate([tall[:, :128], tall[:, 128:]], axis=0)
    table = expand_table(128, 512, False)
    wide = sum(mm(piece, table) for piece in split2(stacked))
    return jnp.concatenate([wide[:rows], wide[rows:]], axis=1)


def natural(blocks):
    rows = []
    for tall in range(blocks.shape[0] // 2):
        lanes = [
            blocks[2 * tall + wide // 4, 8 * (wide % 4) : 8 * (wide % 4) + 8, :]
            for wide in range(8)
        ]
        rows.append(jnp.concatenate(lanes, axis=1))
    return jnp.concatenate(rows, axis=0)


def for_each(v):
    return jnp.concatenate([v] * (128 // v.shape[0]), axis=0)


def halves_of(refs):
    if len(refs) == 1:
        return refs[0][:128], refs[0][128:]
    return [jnp.concatenate([refs[k][...], refs[k + 1][...]], axis=0) for k in (0, 2)]


def detail_kernel(v_ref, *refs):
    *x_refs, top_ref, bottom_ref, c_ref, own_ref = refs
    v = for_each(natural(v_ref))
    halves = [x.astype(F32) * v for x in halves_of(x_refs)]
    c = lon_mean([lat_mean(half) for half in halves])
    c_ref[...] = c.reshape(PAIRS, 8, 256)
    own_ref[...] = c
    fields = [half[ROWS * k : ROWS * k + ROWS] for half in halves for k in range(4)]
    fill_edges(fields, c, top_ref, bottom_ref)


def first_detail_kernel(x_hbm, v_hbm, top_ref, bottom_ref, c_hbm, *refs):
    x_ref, v_ref, c_ref, x_sems, v_sems, c_sems = refs
    pieces = {}
    for pair in range(2):
        rows = [pl.ds(64 * pair + 32 * k, 32) for k in range(2)]
        pieces[pair] = [
            pltpu.make_async_copy(v_hbm.at[row], v_ref.at[row], v_sems.at[2 * pair + k])
            for k, row in enumerate(rows)
        ]
        for member in range(2):
            rows = [pl.ds(128 * member + 64 * pair + 32 * k, 32) for k in range(2)]
            pieces[pair] += [
                pltpu.make_async_copy(
                    x_hbm.at[row], x_ref.at[row], x_sems.at[4 * pair + 2 * member + k]
                )
                for k, row in enumerate(rows)
            ]
    for pair in range(2):
        for copy in pieces[pair]:
            copy.start()
    fields, parts = [None] * PAIRS, [None] * 4
    for pair in range(2):
        for copy in pieces[pair]:
            copy.wait()
        v = v_ref[64 * pair : 64 * pair + 64]
        for member in range(2):
            at = 128 * member + 64 * pair
            w = x_ref[at : at + 64].astype(F32) * v
            parts[2 * member + pair] = lat_mean(w)
            for k in range(2):
                fields[4 * member + 2 * pair + k] = w[ROWS * k : ROWS * k + ROWS]
    c = lon_mean(parts)
    c_ref[...] = c
    copies = [
        pltpu.make_async_copy(c_ref, c_hbm.at[tile], c_sems.at[tile]) for tile in range(TILES)
    ]
    for copy in copies:
        copy.start()
    fill_edges(fields, c, top_ref, bottom_ref)
    for copy in copies:
        copy.wait()


def fill_edges(fields, c, top_ref, bottom_ref):
    spread = prolong(c, edges=True)
    for pair, w in enumerate(fields):
        top_ref[pair] = w[:8] - spread[16 * pair : 16 * pair + 8]
        bottom_ref[pair] = w[24:] - spread[16 * pair + 8 : 16 * pair + 16]


def row_table(taps, tile):
    i, j = iotas(160, 192)
    first = jnp.zeros((160, 192), F32)
    for k in range(4):
        row, col = i - 40 * k, j - 48 * k
        dist = jnp.abs(col - row - 4)
        spot, source = tile * ROWS - 4 + row, tile * ROWS - 8 + col
        fits = (row >= 0) & (row < 40) & (col >= 0) & (col < 48)
        fits = fits & (spot >= 0) & (spot < ROWS * TILES)
        fits = fits & (source >= 0) & (source < ROWS * TILES)
        dist = jnp.where(fits, dist, 9)
        for o in range(5):
            first = jnp.where(dist == o, taps[o][k], first)
    i, j = iotas(128, 160)
    second = jnp.zeros((128, 160), F32)
    for k in range(4):
        row, col = i - 32 * k, j - 40 * k
        fits = (row >= 0) & (row < 32) & (col >= 0) & (col < 40)
        dist = jnp.where(fits, jnp.abs(col - row - 4), 9)
        for o in range(5):
            second = jnp.where(dist == o, taps[o][k], second)
    return exact_mm(second, first)


def band_table(taps):
    i, j = iotas(8, 128)
    before, after = jnp.abs(i - 8 - j), jnp.abs(i + 128 - j)
    i, j = iotas(128, 128)
    inner = jnp.abs(i - j)
    left, right = jnp.zeros((8, 128), F32), jnp.zeros((8, 128), F32)
    middle = jnp.zeros((128, 128), F32)
    for o in range(9):
        left = jnp.where(before == o, taps[o], left)
        right = jnp.where(after == o, taps[o], right)
        middle = jnp.where(inner == o, taps[o], middle)
    rest = jnp.zeros((8, 128), F32)
    return jnp.concatenate([rest, left, middle, right, rest], axis=0)


def own_tile():
    return lax.axis_index("tile")


def own_group():
    return 8 * lax.axis_index("mem_0") + 2 * lax.axis_index("mem_1") + lax.axis_index("mem_2")


def taps_of(taps_ref):
    taps = taps_ref[...]
    square = taps * taps
    energy = square[:, 0:1] + 2.0 * jnp.sum(square[:, 1:5], axis=1, keepdims=True)
    taps = taps / jnp.sqrt(energy)
    single = [taps[:, o : o + 1] for o in range(5)]
    once = [single[abs(o)] for o in range(-4, 5)]
    double = []
    for o in range(9):
        terms = [once[i] * once[o + 8 - i] for i in range(o, 9)]
        double.append(functools.reduce(jnp.add, terms))
    lat = [[tap[k : k + 1] for k in range(4)] for tap in single]
    lon = [[tap[4 + k : 5 + k] for k in range(4)] for tap in double]
    return lat, lon


def fill_tables(lat, lon, tile, rows_ref, band_ref):
    for kind, piece in enumerate(split2(row_table(lat, tile))):
        rows_ref[kind] = piece
    for level in range(band_ref.shape[0]):
        for kind, piece in enumerate(split2(band_table([tap[level] for tap in lon]))):
            band_ref[level, kind] = piece


def table_kernel(x_hbm, r_hbm, taps_ref, lat_ref, lon_ref, *refs):
    *refs, lats_ref, rows_ref, band_ref, lanes_ref, sems = refs
    mix_ref, lons_ref, share_ref, level_ref, packed_ref, *refs = refs
    x_next_refs, hbm_refs = refs[:4], refs[4:]
    tile, own, group = own_tile(), lax.axis_index("mem_0"), own_group()
    lanes = pl.ds(pl.multiple_of(128 * (group >> 2), 128), 128)
    pieces = [
        (r_hbm.at[:, lanes], lanes_ref),
        (r_hbm.at[pl.ds(pl.multiple_of(ROWS * own, ROWS), ROWS)], level_ref),
    ]
    for k in range(4):
        at = pl.multiple_of(512 * (group & 1) + 128 * k, 128)
        rows = pl.ds(pl.multiple_of(8 * (group >> 1), 8), 8)
        pieces.append((r_hbm.at[rows, pl.ds(at, 128)], share_ref.at[pl.ds(8 * k, 8)]))
    for ahead, x_next_ref in enumerate(x_next_refs):
        for member in range(2):
            row = pl.multiple_of(ROWS * (4 * member + ((own + ahead) & 3)), ROWS)
            target = x_next_ref.at[pl.ds(ROWS * member, ROWS)]
            pieces.append((x_hbm.at[pl.ds(row, ROWS)], target))
    loads = [
        pltpu.make_async_copy(source, target, sems.at[3 + k])
        for k, (source, target) in enumerate(pieces)
    ]
    for load in loads:
        load.start()

    def picked(values):
        value = values[3]
        for k in range(3):
            value = jnp.where(own == k, values[k], value)
        return value

    lat, lon = ([[picked(tap)] * 4 for tap in taps] for taps in taps_of(taps_ref))
    fill_tables(lat, lon, tile, rows_ref, band_ref)
    lats_ref[0], lats_ref[1] = split2(lat_ref[...])
    copies = [
        pltpu.make_async_copy(source, target, sems.at[k])
        for k, (source, target) in enumerate(zip((lats_ref, rows_ref, band_ref), hbm_refs))
    ]
    for copy in copies:
        copy.start()
    i, j = iotas(64, 512)
    repeat = jnp.where((i >> 3) == (j >> 6), jnp.where((i & 7) == (j & 7), 1.0, 0.0), 0.0)
    mine = lat_ref[pl.ds(pl.multiple_of(8 * tile, 8), 8), :]
    wide = exact_mm(mine, repeat)
    mix = jnp.concatenate([wide] * PAIRS, axis=0)
    mix = jnp.where((i >> 3) == ((j >> 3) & 7), mix, 0.0)
    mix_ref[0], mix_ref[1] = split2(mix)
    lons_ref[0], lons_ref[1] = split2(lon_ref[...])
    for load in loads:
        load.wait()
    j = lax.broadcasted_iota(jnp.int32, (8, 128), 1)
    for level in range(4):
        packed_r = jnp.zeros((8, 128), F32)
        for k in range(4):
            row = ROWS * level + 8 * k
            shift = (32 * (k + 4 - (group & 3))) & 127
            turned = pltpu.roll(lanes_ref[row : row + 8], shift, 1)
            packed_r = jnp.where((j >> 5) == k, turned, packed_r)
        packed_ref[level] = packed_r
    for copy in copies:
        copy.wait()


def banded(band_ref, level, kind):
    band = band_ref[level, kind]
    edge, half = jnp.zeros((112, 128), BF16), jnp.zeros((128, 128), BF16)
    left = jnp.concatenate([edge, band, edge, half], axis=0)
    right = jnp.concatenate([half, edge, band, edge], axis=0)
    return jnp.concatenate([left, right], axis=1)


def windows(parts, first_row, height):
    rows = []
    for block in range(4):
        for part in parts:
            lanes = [
                part[first_row : first_row + height, 128 * tile : 128 * tile + 128]
                for tile in ((2 * block - 1) % 8, 2 * block, 2 * block + 1, (2 * block + 2) % 8)
            ]
            rows.append(jnp.concatenate(lanes, axis=1))
    return jnp.concatenate(rows, axis=0)


def lane_sums(values):
    i, j = iotas(8, 128)
    result = jnp.zeros((8, 128), F32)
    for lane, value in values:
        result = jnp.where((i == 0) & (j == lane), value, result)
    return result


def total(x):
    return jnp.sum(x, axis=(0, 1), keepdims=True)


def fine_kernel(last, *refs):
    if last:
        r_ref, v_ref, c_ref, *refs = refs
    else:
        *refs, f_ref, c_ref, v_ref, x_ref, rows_ref, band_ref, sems = refs
        v_hbm, c_hbm, x_hbm, taps_ref, *refs = refs
        loads = [
            pltpu.make_async_copy(source, target, sems.at[k])
            for k, (source, target) in enumerate(
                ((c_hbm.at[0], c_ref), (v_hbm, v_ref), (x_hbm, x_ref))
            )
        ]
        for load in loads:
            load.start()
        fill_tables(*taps_of(taps_ref), own_tile(), rows_ref, band_ref)
    before_ref, after_ref, *refs = refs
    if last:
        rows_ref, band_ref, *refs = refs
    x_refs, refs = (refs[:4], refs[4:]) if last else ((x_ref,), refs)
    if last:
        fine_ref, mean_ref, sums_ref, f_ref = refs
        v = natural(v_ref)
    else:
        fine_ref, mean_ref = refs
        for load in loads:
            load.wait()
        v = v_ref[...]
    halves = halves_of(x_refs)
    v_rows, spread = for_each(v), prolong(c_ref[...])
    highs, lows = [], []
    for part in range(2):
        d = halves[part].astype(F32) * v_rows - spread[128 * part : 128 * part + 128]
        rows = []
        for k in range(4):
            pair = 4 * part + k
            rows += [before_ref[pair], d[ROWS * k : ROWS * k + ROWS], after_ref[pair]]
        high, low = split2(jnp.concatenate(rows, axis=0))
        passed = mm3((rows_ref[0], rows_ref[1]), (high, low))
        high, low = split2(passed)
        highs.append(high)
        lows.append(low)
    levels = band_ref.shape[0]
    height = 128 // levels
    for level in range(levels):
        high = windows(highs, height * level, height)
        low = windows(lows, height * level, height)
        table_high, table_low = banded(band_ref, level, 0), banded(band_ref, level, 1)
        result = mm3((high, low), (table_high, table_low))
        for block in range(4):
            lanes = slice(256 * block, 256 * block + 256)
            summed = None
            for part in range(2):
                for inner in range(height // ROWS):
                    row = height * level + ROWS * inner
                    at = height * (2 * block + part) + ROWS * inner
                    f = result[at : at + ROWS]
                    f_ref[128 * part + row : 128 * part + row + ROWS, lanes] = f
                    term = halves[part][row : row + ROWS, lanes].astype(F32) * f
                    summed = term if summed is None else summed + term
            fine_ref[ROWS * level : ROWS * level + ROWS, lanes] = summed
    means = lon_mean([lat_mean(f_ref[128 * k : 128 * k + 128]) for k in range(2)])
    mean_ref[...] = means
    if last:
        r = r_ref[...]
        products = total(v * fine_ref[...]) - 16.0 * total(c_ref[...] * means)
        sums_ref[...] = lane_sums(
            ((0, total(r * r)), (1, total(r * v)), (2, total(v * v)), (3, products))
        )


def smooth_kernel(c_ref, lats_ref, lons_ref, sums_ref, out_ref):
    c = c_ref[...].reshape(64, 256)
    across = mm3((lats_ref[0], lats_ref[1]), split2(c))
    smoothed = mm3(split2(across), (lons_ref[0], lons_ref[1]))
    sums = sums_ref[...] + lane_sums([(4, 16.0 * total(c * smoothed))])
    for tile in range(TILES):
        out_ref[tile, 0:8, :] = smoothed[8 * tile : 8 * tile + 8, :128]
        out_ref[tile, 8:16, :] = smoothed[8 * tile : 8 * tile + 8, 128:]
        out_ref[tile, 16:24, :] = sums


def blended(x_refs, fine_ref, smoothed, loads=()):
    spread, height = prolong(smoothed), fine_ref.shape[0]
    for load in loads:
        load.wait()
    result = fine_ref[...]
    for k, x in enumerate(halves_of(x_refs)):
        product = x.astype(F32) * spread[128 * k : 128 * k + 128]
        for row in range(0, 128, height):
            result = result + product[row : row + height]
    return result


def partial_kernel(x_hbm, c_hbm, fine_ref, mean_ref, mix_ref, lons_ref, out_ref, *refs):
    x_ref, c_ref, sems = refs
    spans = [(c_hbm, c_ref, k, 1) for k in range(TILES)]
    spans += [(x_hbm, x_ref, 64 * k, 64) for k in range(4)]
    loads = [
        pltpu.make_async_copy(source.at[pl.ds(at, size)], target.at[pl.ds(at, size)], sems.at[k])
        for k, (source, target, at, size) in enumerate(spans)
    ]
    for load in loads:
        load.start()
    across = None
    for part in range(2):
        for load in loads[4 * part : 4 * part + 4]:
            load.wait()
        lanes = slice(256 * part, 256 * part + 256)
        c = c_ref[4 * part : 4 * part + 4].reshape(256, 256)
        term = mm3((mix_ref[0, :, lanes], mix_ref[1, :, lanes]), split2(c))
        across = term if across is None else across + term
    smoothed = mm3(split2(across), (lons_ref[0], lons_ref[1])) - mean_ref[...]
    p = blended((x_ref,), fine_ref, smoothed, loads[8:])
    for tall in range(16):
        for wide in range(8):
            out_ref[2 * tall + wide // 4, 8 * (wide % 4) : 8 * (wide % 4) + 8, :] = p[
                8 * tall : 8 * tall + 8, 128 * wide : 128 * wide + 128
            ]


def packed(field):
    group = lax.broadcasted_iota(jnp.int32, (8, 128), 1) >> 5
    shares = []
    for wide in range(8):
        tiles = [field[8 * i : 8 * i + 8, 128 * wide : 128 * wide + 128] for i in range(4)]
        for g in range(4):
            share = None
            for i in range(4):
                turned = pltpu.roll(tiles[i], (32 * (i - g)) % 128, 1) if i != g else tiles[i]
                share = turned if share is None else jnp.where(group == i, turned, share)
            shares.append(share)
    return shares


def last_partial_kernel(fine_ref, mean_ref, smoothed_ref, v_ref, *refs):
    *x_refs, out_ref, v_packed = refs
    halves = [smoothed_ref[:, 8 * k : 8 * k + 8, :].reshape(64, 128) for k in range(2)]
    p = blended(x_refs, fine_ref, jnp.concatenate(halves, axis=1) - mean_ref[...])
    sums = jnp.sum(smoothed_ref[:, 16:24, :], axis=0)
    for group, share in enumerate(packed(natural(v_ref))):
        v_packed[group] = share
    mine = pl.ds(own_group() & 7, 1)
    for group, share in enumerate(packed(p)):
        out_ref[10 * group : 10 * group + 8] = share
        out_ref[10 * group + 8 : 10 * group + 9] = v_packed[group, mine, :]
        out_ref[10 * group + 9 : 10 * group + 10] = sums[:1]


def share_kernel(scale, arrived_ref, r_ref, out_ref):
    share = r_ref[...] + jnp.sum(arrived_ref[...], axis=0) * scale
    for other in range(out_ref.shape[0]):
        out_ref[other] = share


def final_kernel(scale, arrived_ref, r_ref, x_out, res_out):
    i, j = iotas(8, 128)
    sums = arrived_ref[9:10]
    for k in range(1, GROUPS):
        sums = sums + arrived_ref[10 * k + 9 : 10 * k + 10]
    rr, ra, aa, af, ac = (total(jnp.where(j[:1] == k, sums, 0.0)) for k in range(5))
    rr, ra, aa = rr / 8, ra / 8, aa / 8
    step = rr / ra
    ab = aa + (af + ac) * scale
    squares = step * step * aa - rr
    next_step = squares / ((ra - step * aa) - step * (aa - step * ab))
    for level in range(4):
        r = r_ref[level]
        at = [10 * (8 * level + k) for k in range(8)]
        a = jnp.concatenate([arrived_ref[k + 8 : k + 9] for k in at], axis=0)
        p = functools.reduce(jnp.add, [arrived_ref[k : k + 8] for k in at])
        b = a + p * scale
        r_next = r - step * a
        x_new = step * r + next_step * r_next
        res_new = r_next - next_step * (a - step * b)
        for k in range(4):
            x_out[level, 8 * k : 8 * k + 8, :] = x_new[:, 32 * k : 32 * k + 32]
            res_out[level, 8 * k : 8 * k + 8, :] = res_new[:, 32 * k : 32 * k + 32]


VMEM = pl.BlockSpec(memory_space=pltpu.VMEM)
HBM = pl.BlockSpec(memory_space=pltpu.HBM)


def call(kernel, outs, specs, args, flops, limit, scratch=(), out_specs=None):
    out_specs = out_specs or [VMEM] * len(outs)
    shapes = [
        pltpu.HBM(*out) if spec is HBM else jax.ShapeDtypeStruct(*out)
        for out, spec in zip(outs, out_specs)
    ]
    size = sum(a.size * a.dtype.itemsize for a in args)
    args = [
        pltpu.with_memory_space_constraint(arg, pltpu.HBM) if spec is HBM else arg
        for arg, spec in zip(args, specs)
    ]
    return pl.pallas_call(
        kernel,
        out_shape=shapes if len(shapes) > 1 else shapes[0],
        in_specs=specs,
        out_specs=out_specs if len(shapes) > 1 else out_specs[0],
        scratch_shapes=list(scratch),
        compiler_params=pltpu.CompilerParams(vmem_limit_bytes=limit << 20),
        cost_estimate=pl.CostEstimate(flops=flops, bytes_accessed=size, transcendentals=0),
    )(*args)


def exchange(blocks, axis):
    return lax.all_to_all(blocks, axis, 0, 0, tiled=True)


def local(perturbations, right_side, fine_taps, coarse_lat, coarse_lon):
    count, levels, height, extent = perturbations.shape
    members = count * lax.axis_size(MEM)
    scale = 1.0 / (members - 1)
    x = perturbations.reshape(count * levels * height, extent)
    r = right_side.reshape(levels * height, extent)
    half = ((128, LON), F32)
    edge = ((PAIRS, 8, LON), F32)
    shared = ((GROUPS, 32, 128), F32)
    up = [(i, (i + 1) % TILES) for i in range(TILES)]
    down = [(j, i) for i, j in up]

    def edges(top, bottom):
        return lax.ppermute(bottom, "tile", up), lax.ppermute(top, "tile", down)

    own = ((64, 256), F32)
    taps = fine_taps.reshape(2 * levels, 5)
    rows_shape, band_shape = (2, 128, 192), (2, 160, 128)
    top, bottom, c = call(
        first_detail_kernel,
        [edge, edge, ((TILES, 64, 256), F32)],
        [HBM] * 2,
        (x, r),
        10**9,
        12,
        scratch=(
            pltpu.VMEM((256, LON), BF16),
            pltpu.VMEM((128, LON), F32),
            pltpu.VMEM(*own),
            pltpu.SemaphoreType.DMA((8,)),
            pltpu.SemaphoreType.DMA((4,)),
            pltpu.SemaphoreType.DMA((TILES,)),
        ),
        out_specs=[VMEM, VMEM, HBM],
    )
    before, after = edges(top, bottom)
    c_first = exchange(c, "tile")
    before, x_again = lax.optimization_barrier((before, x))
    next_tables = [((2, 64, 64), BF16), (rows_shape, BF16), ((1, *band_shape), BF16)]
    level = ((height, LON), F32)
    outs = [
        ((2, 64, 512), BF16),
        ((2, 256, 256), BF16),
        ((32, 128), F32),
        level,
        ((levels, 8, 128), F32),
        *[((count * height, extent), BF16)] * 4,
    ]
    mix, lons, r_share, r_level, r_packed, *x_next = call(
        table_kernel,
        outs + next_tables,
        [HBM] * 2 + [VMEM] * 3,
        (x_again, r, taps, coarse_lat, coarse_lon),
        10**11,
        6,
        scratch=[
            *(pltpu.VMEM(*shape) for shape in next_tables),
            pltpu.VMEM((128, 128), F32),
            pltpu.SemaphoreType.DMA((17,)),
        ],
        out_specs=[VMEM] * len(outs) + [HBM] * 3,
    )
    *x_next, lats, rows_next, band_next = x_next
    before, mix = lax.optimization_barrier((before, mix))
    for ahead in range(1, 4):
        ring = [(i, (i + ahead) % 4) for i in range(4)]
        x_next[ahead] = lax.ppermute(x_next[ahead], "mem_0", ring)
    fine_scratch = [pltpu.VMEM((256, LON), F32)]
    fine, means = call(
        functools.partial(fine_kernel, False),
        [half, own],
        [HBM] * 3 + [VMEM] * 3,
        (r, c, x, taps, before, after),
        10**11,
        16,
        scratch=[
            *fine_scratch,
            pltpu.VMEM(*own),
            pltpu.VMEM(r.shape, F32),
            pltpu.VMEM(x.shape, BF16),
            pltpu.VMEM(rows_shape, BF16),
            pltpu.VMEM((levels, *band_shape), BF16),
            pltpu.SemaphoreType.DMA((3,)),
        ],
    )
    fine, x_next = lax.optimization_barrier((fine, x_next))
    shares = call(
        partial_kernel,
        [shared],
        [HBM] * 2 + [VMEM] * 4,
        (x, c_first, fine, means, mix, lons),
        10**9,
        12,
        scratch=[
            pltpu.VMEM(x.shape, BF16),
            pltpu.VMEM(c.shape, F32),
            pltpu.SemaphoreType.DMA((12,)),
        ],
    )
    arrived = exchange(shares, MEM)
    share = call(
        functools.partial(share_kernel, scale),
        [((TILES, 32, 128), F32)],
        [VMEM, VMEM],
        (arrived, r_share),
        10**6,
        6,
    )
    a = exchange(share, ("mem_1", "mem_2"))

    top, bottom, c, c_own = call(
        detail_kernel,
        [edge, edge, ((PAIRS, 8, 256), F32), own],
        [VMEM] * 5,
        (a, *x_next),
        10**9,
        12,
    )
    beside = edges(top, bottom)
    c = exchange(c, "tile")
    fine, means, sums = call(
        functools.partial(fine_kernel, True),
        [level, own, ((8, 128), F32)],
        [VMEM] * 11,
        (r_level, a, c_own, *beside, rows_next, band_next, *x_next),
        10**11,
        16,
        scratch=fine_scratch,
    )
    smoothed = call(
        smooth_kernel,
        [((TILES, 24, 128), F32)],
        [VMEM] * 4,
        (c, lats, lons, sums),
        10**8,
        6,
    )
    smoothed = exchange(smoothed, "tile")
    shares = call(
        last_partial_kernel,
        [((GROUPS * 10, 128), F32)],
        [VMEM] * 8,
        (fine, means, smoothed, a, *x_next),
        10**9,
        12,
        scratch=[pltpu.VMEM((GROUPS, 8, 128), F32)],
    )
    arrived = exchange(shares.reshape(GROUPS, 1, 1280), MEM).reshape(shares.shape)
    out = ((levels, height, extent // GROUPS), F32)
    return tuple(
        call(
            functools.partial(final_kernel, scale),
            [out, out],
            [VMEM, VMEM],
            (arrived, r_packed),
            10**6,
            6,
        )
    )


def solution(mesh):
    torus = Mesh(
        mesh.devices.reshape(4, 4, 2, mesh.shape["tile"]), ("mem_0", "mem_1", "mem_2", "tile")
    )
    placed = (P(MEM, None, "tile", None), P(None, "tile", None), P(), P(), P())
    return jax.shard_map(
        local,
        mesh=torus,
        in_specs=placed,
        out_specs=(P(None, "tile", MEM), P(None, "tile", MEM)),
        check_vma=False,
    )
```

```python
import functools

import jax
import jax.numpy as jnp
from jax import lax
from jax.experimental import pallas as pl
from jax.experimental.pallas import tpu as pltpu
from jax.sharding import Mesh
from jax.sharding import PartitionSpec as P

MEM = ("mem_0", "mem_1", "mem_2")
F32 = jnp.float32
BF16 = jnp.bfloat16
EXACT = lax.Precision.HIGHEST
PAIRS, ROWS, LON = 8, 32, 1024
GROUPS, TILES = 32, 8


def mm(a, b):
    return jnp.dot(a, b, preferred_element_type=F32)


def exact_mm(a, b):
    return jnp.dot(a, b, preferred_element_type=F32, precision=EXACT)


def split2(x):
    high = x.astype(BF16)
    return high, (x - high.astype(F32)).astype(BF16)


def mm3(a, b):
    return mm(a[0], b[0]) + mm(a[0], b[1]) + mm(a[1], b[0])


def iotas(rows, cols):
    return (
        lax.broadcasted_iota(jnp.int32, (rows, cols), 0),
        lax.broadcasted_iota(jnp.int32, (rows, cols), 1),
    )


def shrink_table(rows, cols, along_rows):
    i, j = iotas(rows, cols)
    hit = (i >> 2) == j if along_rows else i == (j >> 2)
    return jnp.where(hit, 0.25, 0.0).astype(BF16)


def expand_table(rows, cols, along_rows):
    i, j = iotas(rows, cols)
    hit = (i >> 2) == j if along_rows else i == (j >> 2)
    return jnp.where(hit, 1.0, 0.0).astype(BF16)


def lat_mean(field):
    table = shrink_table(field.shape[0] // 4, field.shape[0], False)
    return sum(mm(table, piece) for piece in split2(field))


def lon_mean(parts):
    stacked = jnp.concatenate([part[:, k : k + 512] for k in (0, 512) for part in parts], axis=0)
    table = shrink_table(512, 128, True)
    small = sum(mm(piece, table) for piece in split2(stacked))
    return jnp.concatenate([small[:64], small[64:]], axis=1)


def prolong(c, edges=False):
    if edges:
        i, j = iotas(128, 64)
        spot = 8 * (i >> 4) + ((i & 15) >> 2) + 4 * ((i & 15) >> 3)
        table = jnp.where(spot == j, 1.0, 0.0).astype(BF16)
    else:
        table = expand_table(256, 64, True)
    rows = table.shape[0]
    tall = sum(mm(table, piece) for piece in split2(c))
    stacked = jnp.concatenate([tall[:, :128], tall[:, 128:]], axis=0)
    table = expand_table(128, 512, False)
    wide = sum(mm(piece, table) for piece in split2(stacked))
    return jnp.concatenate([wide[:rows], wide[rows:]], axis=1)


def natural(blocks):
    rows = []
    for tall in range(blocks.shape[0] // 2):
        lanes = [
            blocks[2 * tall + wide // 4, 8 * (wide % 4) : 8 * (wide % 4) + 8, :]
            for wide in range(8)
        ]
        rows.append(jnp.concatenate(lanes, axis=1))
    return jnp.concatenate(rows, axis=0)


def for_each(v):
    return jnp.concatenate([v] * (128 // v.shape[0]), axis=0)


def halves_of(refs):
    if len(refs) == 1:
        return refs[0][:128], refs[0][128:]
    return [jnp.concatenate([refs[k][...], refs[k + 1][...]], axis=0) for k in (0, 2)]


def detail_kernel(v_ref, *refs):
    *x_refs, top_ref, bottom_ref, c_hbm, own_ref, c_ref, sem = refs
    v = for_each(natural(v_ref))
    halves = [x.astype(F32) * v for x in halves_of(x_refs)]
    c = lon_mean([lat_mean(half) for half in halves])
    c_ref[...] = c.reshape(PAIRS, 8, 256)
    copy = pltpu.make_async_copy(c_ref, c_hbm, sem)
    copy.start()
    own_ref[...] = c
    fields = [half[ROWS * k : ROWS * k + ROWS] for half in halves for k in range(4)]
    fill_edges(fields, c, top_ref, bottom_ref)
    copy.wait()


def first_detail_kernel(x_hbm, v_hbm, top_ref, bottom_ref, c_hbm, *refs):
    x_ref, v_ref, c_ref, x_sems, v_sems, c_sems = refs
    pieces = {}
    for pair in range(2):
        rows = [pl.ds(64 * pair + 16 * k, 16) for k in range(4)]
        pieces[pair] = [
            pltpu.make_async_copy(v_hbm.at[row], v_ref.at[row], v_sems.at[4 * pair + k])
            for k, row in enumerate(rows)
        ]
        for member in range(2):
            rows = [pl.ds(128 * member + 64 * pair + 32 * k, 32) for k in range(2)]
            pieces[pair] += [
                pltpu.make_async_copy(
                    x_hbm.at[row], x_ref.at[row], x_sems.at[4 * pair + 2 * member + k]
                )
                for k, row in enumerate(rows)
            ]
    for pair in range(2):
        for copy in pieces[pair]:
            copy.start()
    fields, parts = [None] * PAIRS, [None] * 4
    for pair in range(2):
        for copy in pieces[pair]:
            copy.wait()
        v = v_ref[64 * pair : 64 * pair + 64]
        for member in range(2):
            at = 128 * member + 64 * pair
            w = x_ref[at : at + 64].astype(F32) * v
            parts[2 * member + pair] = lat_mean(w)
            for k in range(2):
                fields[4 * member + 2 * pair + k] = w[ROWS * k : ROWS * k + ROWS]
    c = lon_mean(parts)
    c_ref[...] = c
    copies = [
        pltpu.make_async_copy(c_ref, c_hbm.at[tile], c_sems.at[tile]) for tile in range(TILES)
    ]
    for copy in copies:
        copy.start()
    fill_edges(fields, c, top_ref, bottom_ref)
    for copy in copies:
        copy.wait()


def fill_edges(fields, c, top_ref, bottom_ref):
    spread = prolong(c, edges=True)
    for pair, w in enumerate(fields):
        top_ref[pair] = w[:8] - spread[16 * pair : 16 * pair + 8]
        bottom_ref[pair] = w[24:] - spread[16 * pair + 8 : 16 * pair + 16]


def row_table(taps, tile):
    i, j = iotas(160, 192)
    first = jnp.zeros((160, 192), F32)
    for k in range(4):
        row, col = i - 40 * k, j - 48 * k
        dist = jnp.abs(col - row - 4)
        spot, source = tile * ROWS - 4 + row, tile * ROWS - 8 + col
        fits = (row >= 0) & (row < 40) & (col >= 0) & (col < 48)
        fits = fits & (spot >= 0) & (spot < ROWS * TILES)
        fits = fits & (source >= 0) & (source < ROWS * TILES)
        dist = jnp.where(fits, dist, 9)
        for o in range(5):
            first = jnp.where(dist == o, taps[o][k], first)
    i, j = iotas(128, 160)
    second = jnp.zeros((128, 160), F32)
    for k in range(4):
        row, col = i - 32 * k, j - 40 * k
        fits = (row >= 0) & (row < 32) & (col >= 0) & (col < 40)
        dist = jnp.where(fits, jnp.abs(col - row - 4), 9)
        for o in range(5):
            second = jnp.where(dist == o, taps[o][k], second)
    return exact_mm(second, first)


def band_table(taps):
    i, j = iotas(8, 128)
    before, after = jnp.abs(i - 8 - j), jnp.abs(i + 128 - j)
    i, j = iotas(128, 128)
    inner = jnp.abs(i - j)
    left, right = jnp.zeros((8, 128), F32), jnp.zeros((8, 128), F32)
    middle = jnp.zeros((128, 128), F32)
    for o in range(9):
        left = jnp.where(before == o, taps[o], left)
        right = jnp.where(after == o, taps[o], right)
        middle = jnp.where(inner == o, taps[o], middle)
    rest = jnp.zeros((8, 128), F32)
    return jnp.concatenate([rest, left, middle, right, rest], axis=0)


def own_tile():
    return lax.axis_index("tile")


def own_group():
    return 8 * lax.axis_index("mem_0") + 2 * lax.axis_index("mem_1") + lax.axis_index("mem_2")


def taps_of(taps_ref):
    taps = taps_ref[...]
    square = taps * taps
    energy = square[:, 0:1] + 2.0 * jnp.sum(square[:, 1:5], axis=1, keepdims=True)
    taps = taps / jnp.sqrt(energy)
    single = [taps[:, o : o + 1] for o in range(5)]
    once = [single[abs(o)] for o in range(-4, 5)]
    double = []
    for o in range(9):
        terms = [once[i] * once[o + 8 - i] for i in range(o, 9)]
        double.append(functools.reduce(jnp.add, terms))
    lat = [[tap[k : k + 1] for k in range(4)] for tap in single]
    lon = [[tap[4 + k : 5 + k] for k in range(4)] for tap in double]
    return lat, lon


def fill_tables(lat, lon, tile, rows_ref, band_ref):
    for kind, piece in enumerate(split2(row_table(lat, tile))):
        rows_ref[kind] = piece
    for level in range(band_ref.shape[0]):
        for kind, piece in enumerate(split2(band_table([tap[level] for tap in lon]))):
            band_ref[level, kind] = piece


def table_kernel(x_hbm, r_hbm, taps_ref, lat_ref, lon_ref, *refs):
    *refs, lats_ref, rows_ref, band_ref, lanes_ref, sems = refs
    mix_ref, lons_ref, share_ref, level_ref, packed_ref, *refs = refs
    x_next_refs, hbm_refs = refs[:4], refs[4:]
    tile, own, group = own_tile(), lax.axis_index("mem_0"), own_group()
    lanes = pl.ds(pl.multiple_of(128 * (group >> 2), 128), 128)
    pieces = [
        (r_hbm.at[:, lanes], lanes_ref),
        (r_hbm.at[pl.ds(pl.multiple_of(ROWS * own, ROWS), ROWS)], level_ref),
    ]
    for k in range(4):
        at = pl.multiple_of(512 * (group & 1) + 128 * k, 128)
        rows = pl.ds(pl.multiple_of(8 * (group >> 1), 8), 8)
        pieces.append((r_hbm.at[rows, pl.ds(at, 128)], share_ref.at[pl.ds(8 * k, 8)]))
    for ahead, x_next_ref in enumerate(x_next_refs):
        for member in range(2):
            row = pl.multiple_of(ROWS * (4 * member + ((own + ahead) & 3)), ROWS)
            target = x_next_ref.at[pl.ds(ROWS * member, ROWS)]
            pieces.append((x_hbm.at[pl.ds(row, ROWS)], target))
    loads = [
        pltpu.make_async_copy(source, target, sems.at[3 + k])
        for k, (source, target) in enumerate(pieces)
    ]
    for load in loads:
        load.start()

    def picked(values):
        value = values[3]
        for k in range(3):
            value = jnp.where(own == k, values[k], value)
        return value

    lat, lon = ([[picked(tap)] * 4 for tap in taps] for taps in taps_of(taps_ref))
    fill_tables(lat, lon, tile, rows_ref, band_ref)
    lats_ref[0], lats_ref[1] = split2(lat_ref[...])
    copies = [
        pltpu.make_async_copy(source, target, sems.at[k])
        for k, (source, target) in enumerate(zip((lats_ref, rows_ref, band_ref), hbm_refs))
    ]
    for copy in copies:
        copy.start()
    i, j = iotas(64, 512)
    repeat = jnp.where((i >> 3) == (j >> 6), jnp.where((i & 7) == (j & 7), 1.0, 0.0), 0.0)
    mine = lat_ref[pl.ds(pl.multiple_of(8 * tile, 8), 8), :]
    wide = exact_mm(mine, repeat)
    mix = jnp.concatenate([wide] * PAIRS, axis=0)
    mix = jnp.where((i >> 3) == ((j >> 3) & 7), mix, 0.0)
    mix_ref[0], mix_ref[1] = split2(mix)
    lons_ref[0], lons_ref[1] = split2(lon_ref[...])
    for load in loads:
        load.wait()
    j = lax.broadcasted_iota(jnp.int32, (8, 128), 1)
    for level in range(4):
        packed_r = jnp.zeros((8, 128), F32)
        for k in range(4):
            row = ROWS * level + 8 * k
            shift = (32 * (k + 4 - (group & 3))) & 127
            turned = pltpu.roll(lanes_ref[row : row + 8], shift, 1)
            packed_r = jnp.where((j >> 5) == k, turned, packed_r)
        packed_ref[level] = packed_r
    for copy in copies:
        copy.wait()


def banded(band_ref, level, kind):
    band = band_ref[level, kind]
    edge, half = jnp.zeros((112, 128), BF16), jnp.zeros((128, 128), BF16)
    left = jnp.concatenate([edge, band, edge, half], axis=0)
    right = jnp.concatenate([half, edge, band, edge], axis=0)
    return jnp.concatenate([left, right], axis=1)


def windows(parts, first_row, height):
    rows = []
    for block in range(4):
        for part in parts:
            lanes = [
                part[first_row : first_row + height, 128 * tile : 128 * tile + 128]
                for tile in ((2 * block - 1) % 8, 2 * block, 2 * block + 1, (2 * block + 2) % 8)
            ]
            rows.append(jnp.concatenate(lanes, axis=1))
    return jnp.concatenate(rows, axis=0)


def lane_sums(values):
    i, j = iotas(8, 128)
    result = jnp.zeros((8, 128), F32)
    for lane, value in values:
        result = jnp.where((i == 0) & (j == lane), value, result)
    return result


def total(x):
    return jnp.sum(x, axis=(0, 1), keepdims=True)


def fine_kernel(last, *refs):
    if last:
        r_ref, v_ref, c_ref, *refs = refs
    else:
        *refs, f_ref, c_ref, v_ref, x_ref, rows_ref, band_ref, sems = refs
        v_hbm, c_hbm, x_hbm, taps_ref, *refs = refs
        loads = [
            pltpu.make_async_copy(source, target, sems.at[k])
            for k, (source, target) in enumerate(
                ((c_hbm.at[0], c_ref), (v_hbm, v_ref), (x_hbm, x_ref))
            )
        ]
        for load in loads:
            load.start()
        fill_tables(*taps_of(taps_ref), own_tile(), rows_ref, band_ref)
    before_ref, after_ref, *refs = refs
    if last:
        rows_ref, band_ref, *refs = refs
    x_refs, refs = (refs[:4], refs[4:]) if last else ((x_ref,), refs)
    if last:
        fine_ref, mean_ref, sums_ref, f_ref = refs
        v = natural(v_ref)
    else:
        fine_ref, mean_ref = refs
        for load in loads:
            load.wait()
        v = v_ref[...]
    halves = halves_of(x_refs)
    v_rows, spread = for_each(v), prolong(c_ref[...])
    highs, lows = [], []
    for part in range(2):
        d = halves[part].astype(F32) * v_rows - spread[128 * part : 128 * part + 128]
        rows = []
        for k in range(4):
            pair = 4 * part + k
            rows += [before_ref[pair], d[ROWS * k : ROWS * k + ROWS], after_ref[pair]]
        high, low = split2(jnp.concatenate(rows, axis=0))
        passed = mm3((rows_ref[0], rows_ref[1]), (high, low))
        high, low = split2(passed)
        highs.append(high)
        lows.append(low)
    levels = band_ref.shape[0]
    height = 128 // levels
    for level in range(levels):
        high = windows(highs, height * level, height)
        low = windows(lows, height * level, height)
        table_high, table_low = banded(band_ref, level, 0), banded(band_ref, level, 1)
        result = mm3((high, low), (table_high, table_low))
        for block in range(4):
            lanes = slice(256 * block, 256 * block + 256)
            summed = None
            for part in range(2):
                for inner in range(height // ROWS):
                    row = height * level + ROWS * inner
                    at = height * (2 * block + part) + ROWS * inner
                    f = result[at : at + ROWS]
                    f_ref[128 * part + row : 128 * part + row + ROWS, lanes] = f
                    term = halves[part][row : row + ROWS, lanes].astype(F32) * f
                    summed = term if summed is None else summed + term
            fine_ref[ROWS * level : ROWS * level + ROWS, lanes] = summed
    means = lon_mean([lat_mean(f_ref[128 * k : 128 * k + 128]) for k in range(2)])
    mean_ref[...] = means
    if last:
        r = r_ref[...]
        products = total(v * fine_ref[...]) - 16.0 * total(c_ref[...] * means)
        sums_ref[...] = lane_sums(
            ((0, total(r * r)), (1, total(r * v)), (2, total(v * v)), (3, products))
        )


def smooth_kernel(c_ref, lats_ref, lons_ref, sums_ref, out_ref):
    c = c_ref[...].reshape(64, 256)
    across = mm3((lats_ref[0], lats_ref[1]), split2(c))
    smoothed = mm3(split2(across), (lons_ref[0], lons_ref[1]))
    sums = sums_ref[...] + lane_sums([(4, 16.0 * total(c * smoothed))])
    for tile in range(TILES):
        out_ref[tile, 0:8, :] = smoothed[8 * tile : 8 * tile + 8, :128]
        out_ref[tile, 8:16, :] = smoothed[8 * tile : 8 * tile + 8, 128:]
        out_ref[tile, 16:24, :] = sums


def blended(x_refs, fine_ref, smoothed):
    spread, height = prolong(smoothed), fine_ref.shape[0]
    result = fine_ref[...]
    for k, x in enumerate(halves_of(x_refs)):
        product = x.astype(F32) * spread[128 * k : 128 * k + 128]
        for row in range(0, 128, height):
            result = result + product[row : row + height]
    return result


def partial_kernel(x_ref, c_hbm, fine_ref, mean_ref, mix_ref, lons_ref, out_ref, *refs):
    c_ref, sems = refs
    spans = [(c_hbm, c_ref, k, 1) for k in range(TILES)]
    loads = [
        pltpu.make_async_copy(source.at[pl.ds(at, size)], target.at[pl.ds(at, size)], sems.at[k])
        for k, (source, target, at, size) in enumerate(spans)
    ]
    for load in loads:
        load.start()
    across = None
    for part in range(2):
        for load in loads[4 * part : 4 * part + 4]:
            load.wait()
        lanes = slice(256 * part, 256 * part + 256)
        c = c_ref[4 * part : 4 * part + 4].reshape(256, 256)
        term = mm3((mix_ref[0, :, lanes], mix_ref[1, :, lanes]), split2(c))
        across = term if across is None else across + term
    smoothed = mm3(split2(across), (lons_ref[0], lons_ref[1])) - mean_ref[...]
    p = blended((x_ref,), fine_ref, smoothed)
    for tall in range(16):
        for wide in range(8):
            out_ref[2 * tall + wide // 4, 8 * (wide % 4) : 8 * (wide % 4) + 8, :] = p[
                8 * tall : 8 * tall + 8, 128 * wide : 128 * wide + 128
            ]


def packed(field):
    group = lax.broadcasted_iota(jnp.int32, (8, 128), 1) >> 5
    shares = []
    for wide in range(8):
        tiles = [field[8 * i : 8 * i + 8, 128 * wide : 128 * wide + 128] for i in range(4)]
        for g in range(4):
            share = None
            for i in range(4):
                turned = pltpu.roll(tiles[i], (32 * (i - g)) % 128, 1) if i != g else tiles[i]
                share = turned if share is None else jnp.where(group == i, turned, share)
            shares.append(share)
    return shares


def last_partial_kernel(fine_ref, mean_ref, smoothed_ref, v_ref, *refs):
    *x_refs, out_ref, v_packed = refs
    halves = [smoothed_ref[:, 8 * k : 8 * k + 8, :].reshape(64, 128) for k in range(2)]
    p = blended(x_refs, fine_ref, jnp.concatenate(halves, axis=1) - mean_ref[...])
    sums = jnp.sum(smoothed_ref[:, 16:24, :], axis=0)
    for group, share in enumerate(packed(natural(v_ref))):
        v_packed[group] = share
    mine = pl.ds(own_group() & 7, 1)
    for group, share in enumerate(packed(p)):
        out_ref[10 * group : 10 * group + 8] = share
        out_ref[10 * group + 8 : 10 * group + 9] = v_packed[group, mine, :]
        out_ref[10 * group + 9 : 10 * group + 10] = sums[:1]


def share_kernel(scale, arrived_ref, r_ref, out_ref):
    share = r_ref[...] + jnp.sum(arrived_ref[...], axis=0) * scale
    for other in range(out_ref.shape[0]):
        out_ref[other] = share


def final_kernel(scale, arrived_ref, r_ref, x_out, res_out):
    i, j = iotas(8, 128)
    sums = arrived_ref[9:10]
    for k in range(1, GROUPS):
        sums = sums + arrived_ref[10 * k + 9 : 10 * k + 10]
    rr, ra, aa, af, ac = (total(jnp.where(j[:1] == k, sums, 0.0)) for k in range(5))
    rr, ra, aa = rr / 8, ra / 8, aa / 8
    step = rr / ra
    ab = aa + (af + ac) * scale
    squares = step * step * aa - rr
    next_step = squares / ((ra - step * aa) - step * (aa - step * ab))
    for level in range(4):
        r = r_ref[level]
        at = [10 * (8 * level + k) for k in range(8)]
        a = jnp.concatenate([arrived_ref[k + 8 : k + 9] for k in at], axis=0)
        p = functools.reduce(jnp.add, [arrived_ref[k : k + 8] for k in at])
        b = a + p * scale
        r_next = r - step * a
        x_new = step * r + next_step * r_next
        res_new = r_next - next_step * (a - step * b)
        for k in range(4):
            x_out[level, 8 * k : 8 * k + 8, :] = x_new[:, 32 * k : 32 * k + 32]
            res_out[level, 8 * k : 8 * k + 8, :] = res_new[:, 32 * k : 32 * k + 32]


VMEM = pl.BlockSpec(memory_space=pltpu.VMEM)
HBM = pl.BlockSpec(memory_space=pltpu.HBM)


def call(kernel, outs, specs, args, flops, limit, scratch=(), out_specs=None):
    out_specs = out_specs or [VMEM] * len(outs)
    shapes = [
        pltpu.HBM(*out) if spec is HBM else jax.ShapeDtypeStruct(*out)
        for out, spec in zip(outs, out_specs)
    ]
    size = sum(a.size * a.dtype.itemsize for a in args)
    args = [
        pltpu.with_memory_space_constraint(arg, pltpu.HBM) if spec is HBM else arg
        for arg, spec in zip(args, specs)
    ]
    return pl.pallas_call(
        kernel,
        out_shape=shapes if len(shapes) > 1 else shapes[0],
        in_specs=specs,
        out_specs=out_specs if len(shapes) > 1 else out_specs[0],
        scratch_shapes=list(scratch),
        compiler_params=pltpu.CompilerParams(vmem_limit_bytes=limit << 20),
        cost_estimate=pl.CostEstimate(flops=flops, bytes_accessed=size, transcendentals=0),
    )(*args)


def exchange(blocks, axis):
    return lax.all_to_all(blocks, axis, 0, 0, tiled=True)


def local(perturbations, right_side, fine_taps, coarse_lat, coarse_lon):
    count, levels, height, extent = perturbations.shape
    members = count * lax.axis_size(MEM)
    scale = 1.0 / (members - 1)
    x = perturbations.reshape(count * levels * height, extent)
    r = right_side.reshape(levels * height, extent)
    half = ((128, LON), F32)
    edge = ((PAIRS, 8, LON), F32)
    shared = ((GROUPS, 32, 128), F32)
    up = [(i, (i + 1) % TILES) for i in range(TILES)]
    down = [(j, i) for i, j in up]

    def edges(top, bottom):
        return lax.ppermute(bottom, "tile", up), lax.ppermute(top, "tile", down)

    own = ((64, 256), F32)
    taps = fine_taps.reshape(2 * levels, 5)
    rows_shape, band_shape = (2, 128, 192), (2, 160, 128)
    top, bottom, c = call(
        first_detail_kernel,
        [edge, edge, ((TILES, 64, 256), F32)],
        [HBM] * 2,
        (x, r),
        10**9,
        12,
        scratch=(
            pltpu.VMEM((256, LON), BF16),
            pltpu.VMEM((128, LON), F32),
            pltpu.VMEM(*own),
            pltpu.SemaphoreType.DMA((8,)),
            pltpu.SemaphoreType.DMA((8,)),
            pltpu.SemaphoreType.DMA((TILES,)),
        ),
        out_specs=[VMEM, VMEM, HBM],
    )
    before, after = edges(top, bottom)
    c_first = exchange(c, "tile")
    before, x_again = lax.optimization_barrier((before, x))
    next_tables = [((2, 64, 64), BF16), (rows_shape, BF16), ((1, *band_shape), BF16)]
    level = ((height, LON), F32)
    outs = [
        ((2, 64, 512), BF16),
        ((2, 256, 256), BF16),
        ((32, 128), F32),
        level,
        ((levels, 8, 128), F32),
        *[((count * height, extent), BF16)] * 4,
    ]
    mix, lons, r_share, r_level, r_packed, *x_next = call(
        table_kernel,
        outs + next_tables,
        [HBM] * 2 + [VMEM] * 3,
        (x_again, r, taps, coarse_lat, coarse_lon),
        10**11,
        6,
        scratch=[
            *(pltpu.VMEM(*shape) for shape in next_tables),
            pltpu.VMEM((128, 128), F32),
            pltpu.SemaphoreType.DMA((17,)),
        ],
        out_specs=[VMEM] * len(outs) + [HBM] * 3,
    )
    *x_next, lats, rows_next, band_next = x_next
    before, mix = lax.optimization_barrier((before, mix))
    for ahead in range(1, 4):
        ring = [(i, (i + ahead) % 4) for i in range(4)]
        x_next[ahead] = lax.ppermute(x_next[ahead], "mem_0", ring)
    fine_scratch = [pltpu.VMEM((256, LON), F32)]
    fine, means = call(
        functools.partial(fine_kernel, False),
        [half, own],
        [HBM] * 3 + [VMEM] * 3,
        (r, c, x, taps, before, after),
        10**11,
        16,
        scratch=[
            *fine_scratch,
            pltpu.VMEM(*own),
            pltpu.VMEM(r.shape, F32),
            pltpu.VMEM(x.shape, BF16),
            pltpu.VMEM(rows_shape, BF16),
            pltpu.VMEM((levels, *band_shape), BF16),
            pltpu.SemaphoreType.DMA((3,)),
        ],
    )
    fine, x_next = lax.optimization_barrier((fine, x_next))
    shares = call(
        partial_kernel,
        [shared],
        [VMEM, HBM] + [VMEM] * 4,
        (x, c_first, fine, means, mix, lons),
        10**9,
        12,
        scratch=[
            pltpu.VMEM(c.shape, F32),
            pltpu.SemaphoreType.DMA((TILES,)),
        ],
    )
    arrived = exchange(shares, MEM)
    share = call(
        functools.partial(share_kernel, scale),
        [((TILES, 32, 128), F32)],
        [VMEM, VMEM],
        (arrived, r_share),
        10**6,
        6,
    )
    a = exchange(share, ("mem_1", "mem_2"))

    top, bottom, c, c_own = call(
        detail_kernel,
        [edge, edge, ((PAIRS, 8, 256), F32), own],
        [VMEM] * 5,
        (a, *x_next),
        10**9,
        12,
        scratch=[pltpu.VMEM((PAIRS, 8, 256), F32), pltpu.SemaphoreType.DMA],
        out_specs=[VMEM, VMEM, HBM, VMEM],
    )
    beside = edges(top, bottom)
    c = exchange(c, "tile")
    fine, means, sums = call(
        functools.partial(fine_kernel, True),
        [level, own, ((8, 128), F32)],
        [VMEM] * 11,
        (r_level, a, c_own, *beside, rows_next, band_next, *x_next),
        10**11,
        16,
        scratch=fine_scratch,
    )
    smoothed = call(
        smooth_kernel,
        [((TILES, 24, 128), F32)],
        [VMEM] * 4,
        (c, lats, lons, sums),
        10**8,
        6,
    )
    smoothed = exchange(smoothed, "tile")
    shares = call(
        last_partial_kernel,
        [((GROUPS * 10, 128), F32)],
        [VMEM] * 8,
        (fine, means, smoothed, a, *x_next),
        10**9,
        12,
        scratch=[pltpu.VMEM((GROUPS, 8, 128), F32)],
    )
    arrived = exchange(shares.reshape(GROUPS, 1, 1280), MEM).reshape(shares.shape)
    out = ((levels, height, extent // GROUPS), F32)
    return tuple(
        call(
            functools.partial(final_kernel, scale),
            [out, out],
            [VMEM, VMEM],
            (arrived, r_packed),
            10**6,
            6,
        )
    )


def solution(mesh):
    torus = Mesh(
        mesh.devices.reshape(4, 4, 2, mesh.shape["tile"]), ("mem_0", "mem_1", "mem_2", "tile")
    )
    placed = (P(MEM, None, "tile", None), P(None, "tile", None), P(), P(), P())
    return jax.shard_map(
        local,
        mesh=torus,
        in_specs=placed,
        out_specs=(P(None, "tile", MEM), P(None, "tile", MEM)),
        check_vma=False,
    )
```

```python
import functools

import jax
import jax.numpy as jnp
from jax import lax
from jax.experimental import pallas as pl
from jax.experimental.pallas import tpu as pltpu
from jax.sharding import Mesh
from jax.sharding import PartitionSpec as P

MEM = ("mem_0", "mem_1", "mem_2")
F32 = jnp.float32
BF16 = jnp.bfloat16
EXACT = lax.Precision.HIGHEST
PAIRS, ROWS, LON = 8, 32, 1024
GROUPS, TILES = 32, 8


def mm(a, b):
    return jnp.dot(a, b, preferred_element_type=F32)


def exact_mm(a, b):
    return jnp.dot(a, b, preferred_element_type=F32, precision=EXACT)


def split2(x):
    high = x.astype(BF16)
    return high, (x - high.astype(F32)).astype(BF16)


def mm3(a, b):
    return mm(a[0], b[0]) + mm(a[0], b[1]) + mm(a[1], b[0])


def iotas(rows, cols):
    return (
        lax.broadcasted_iota(jnp.int32, (rows, cols), 0),
        lax.broadcasted_iota(jnp.int32, (rows, cols), 1),
    )


def shrink_table(rows, cols, along_rows):
    i, j = iotas(rows, cols)
    hit = (i >> 2) == j if along_rows else i == (j >> 2)
    return jnp.where(hit, 0.25, 0.0).astype(BF16)


def expand_table(rows, cols, along_rows):
    i, j = iotas(rows, cols)
    hit = (i >> 2) == j if along_rows else i == (j >> 2)
    return jnp.where(hit, 1.0, 0.0).astype(BF16)


def lat_mean(field):
    table = shrink_table(field.shape[0] // 4, field.shape[0], False)
    return sum(mm(table, piece) for piece in split2(field))


def lon_mean(parts):
    stacked = jnp.concatenate([part[:, k : k + 512] for k in (0, 512) for part in parts], axis=0)
    table = shrink_table(512, 128, True)
    small = sum(mm(piece, table) for piece in split2(stacked))
    return jnp.concatenate([small[:64], small[64:]], axis=1)


def prolong(c, edges=False):
    if edges:
        i, j = iotas(128, 64)
        spot = 8 * (i >> 4) + ((i & 15) >> 2) + 4 * ((i & 15) >> 3)
        table = jnp.where(spot == j, 1.0, 0.0).astype(BF16)
    else:
        table = expand_table(256, 64, True)
    rows = table.shape[0]
    tall = sum(mm(table, piece) for piece in split2(c))
    stacked = jnp.concatenate([tall[:, :128], tall[:, 128:]], axis=0)
    table = expand_table(128, 512, False)
    wide = sum(mm(piece, table) for piece in split2(stacked))
    return jnp.concatenate([wide[:rows], wide[rows:]], axis=1)


def natural(blocks):
    rows = []
    for tall in range(blocks.shape[0] // 2):
        lanes = [
            blocks[2 * tall + wide // 4, 8 * (wide % 4) : 8 * (wide % 4) + 8, :]
            for wide in range(8)
        ]
        rows.append(jnp.concatenate(lanes, axis=1))
    return jnp.concatenate(rows, axis=0)


def for_each(v):
    return jnp.concatenate([v] * (128 // v.shape[0]), axis=0)


def halves_of(refs):
    if len(refs) == 1:
        return refs[0][:128], refs[0][128:]
    return [jnp.concatenate([refs[k][...], refs[k + 1][...]], axis=0) for k in (0, 2)]


def detail_kernel(v_ref, *refs):
    *x_refs, top_ref, bottom_ref, c_ref, own_ref = refs
    v = for_each(natural(v_ref))
    halves = [x.astype(F32) * v for x in halves_of(x_refs)]
    c = lon_mean([lat_mean(half) for half in halves])
    c_ref[...] = c.reshape(PAIRS, 8, 256)
    own_ref[...] = c
    fields = [half[ROWS * k : ROWS * k + ROWS] for half in halves for k in range(4)]
    fill_edges(fields, c, top_ref, bottom_ref)


def first_detail_kernel(x_hbm, v_hbm, top_ref, bottom_ref, c_hbm, *refs):
    x_ref, v_ref, c_ref, x_sems, v_sems, c_sems = refs
    pieces = {}
    for pair in range(2):
        rows = [pl.ds(64 * pair + 32 * k, 32) for k in range(2)]
        pieces[pair] = [
            pltpu.make_async_copy(v_hbm.at[row], v_ref.at[row], v_sems.at[2 * pair + k])
            for k, row in enumerate(rows)
        ]
        for member in range(2):
            rows = [pl.ds(128 * member + 64 * pair + 32 * k, 32) for k in range(2)]
            pieces[pair] += [
                pltpu.make_async_copy(
                    x_hbm.at[row], x_ref.at[row], x_sems.at[4 * pair + 2 * member + k]
                )
                for k, row in enumerate(rows)
            ]
    for pair in range(2):
        for copy in pieces[pair]:
            copy.start()
    fields, parts = [None] * PAIRS, [None] * 4
    for pair in range(2):
        for copy in pieces[pair]:
            copy.wait()
        v = v_ref[64 * pair : 64 * pair + 64]
        for member in range(2):
            at = 128 * member + 64 * pair
            w = x_ref[at : at + 64].astype(F32) * v
            parts[2 * member + pair] = lat_mean(w)
            for k in range(2):
                fields[4 * member + 2 * pair + k] = w[ROWS * k : ROWS * k + ROWS]
    c = lon_mean(parts)
    c_ref[...] = c
    copies = [
        pltpu.make_async_copy(c_ref, c_hbm.at[tile], c_sems.at[tile]) for tile in range(TILES)
    ]
    for copy in copies:
        copy.start()
    fill_edges(fields, c, top_ref, bottom_ref)
    for copy in copies:
        copy.wait()


def fill_edges(fields, c, top_ref, bottom_ref):
    spread = prolong(c, edges=True)
    for pair, w in enumerate(fields):
        top_ref[pair] = w[:8] - spread[16 * pair : 16 * pair + 8]
        bottom_ref[pair] = w[24:] - spread[16 * pair + 8 : 16 * pair + 16]


def row_table(taps, tile):
    i, j = iotas(160, 192)
    first = jnp.zeros((160, 192), F32)
    for k in range(4):
        row, col = i - 40 * k, j - 48 * k
        dist = jnp.abs(col - row - 4)
        spot, source = tile * ROWS - 4 + row, tile * ROWS - 8 + col
        fits = (row >= 0) & (row < 40) & (col >= 0) & (col < 48)
        fits = fits & (spot >= 0) & (spot < ROWS * TILES)
        fits = fits & (source >= 0) & (source < ROWS * TILES)
        dist = jnp.where(fits, dist, 9)
        for o in range(5):
            first = jnp.where(dist == o, taps[o][k], first)
    i, j = iotas(128, 160)
    second = jnp.zeros((128, 160), F32)
    for k in range(4):
        row, col = i - 32 * k, j - 40 * k
        fits = (row >= 0) & (row < 32) & (col >= 0) & (col < 40)
        dist = jnp.where(fits, jnp.abs(col - row - 4), 9)
        for o in range(5):
            second = jnp.where(dist == o, taps[o][k], second)
    return exact_mm(second, first)


def band_table(taps):
    i, j = iotas(8, 128)
    before, after = jnp.abs(i - 8 - j), jnp.abs(i + 128 - j)
    i, j = iotas(128, 128)
    inner = jnp.abs(i - j)
    left, right = jnp.zeros((8, 128), F32), jnp.zeros((8, 128), F32)
    middle = jnp.zeros((128, 128), F32)
    for o in range(9):
        left = jnp.where(before == o, taps[o], left)
        right = jnp.where(after == o, taps[o], right)
        middle = jnp.where(inner == o, taps[o], middle)
    rest = jnp.zeros((8, 128), F32)
    return jnp.concatenate([rest, left, middle, right, rest], axis=0)


def own_tile():
    return lax.axis_index("tile")


def own_group():
    return 8 * lax.axis_index("mem_0") + 2 * lax.axis_index("mem_1") + lax.axis_index("mem_2")


def taps_of(taps_ref):
    taps = taps_ref[...]
    square = taps * taps
    energy = square[:, 0:1] + 2.0 * jnp.sum(square[:, 1:5], axis=1, keepdims=True)
    taps = taps / jnp.sqrt(energy)
    single = [taps[:, o : o + 1] for o in range(5)]
    once = [single[abs(o)] for o in range(-4, 5)]
    double = []
    for o in range(9):
        terms = [once[i] * once[o + 8 - i] for i in range(o, 9)]
        double.append(functools.reduce(jnp.add, terms))
    lat = [[tap[k : k + 1] for k in range(4)] for tap in single]
    lon = [[tap[4 + k : 5 + k] for k in range(4)] for tap in double]
    return lat, lon


def fill_tables(lat, lon, tile, rows_ref, band_ref):
    for kind, piece in enumerate(split2(row_table(lat, tile))):
        rows_ref[kind] = piece
    for level in range(band_ref.shape[0]):
        for kind, piece in enumerate(split2(band_table([tap[level] for tap in lon]))):
            band_ref[level, kind] = piece


def table_kernel(x_hbm, r_hbm, taps_ref, lat_ref, lon_ref, *refs):
    *refs, lats_ref, rows_ref, band_ref, lanes_ref, sems = refs
    mix_ref, lons_ref, share_ref, level_ref, packed_ref, *refs = refs
    x_next_refs, hbm_refs = refs[:4], refs[4:]
    tile, own, group = own_tile(), lax.axis_index("mem_0"), own_group()
    lanes = pl.ds(pl.multiple_of(128 * (group >> 2), 128), 128)
    pieces = [
        (r_hbm.at[:, lanes], lanes_ref),
        (r_hbm.at[pl.ds(pl.multiple_of(ROWS * own, ROWS), ROWS)], level_ref),
    ]
    for k in range(4):
        at = pl.multiple_of(512 * (group & 1) + 128 * k, 128)
        rows = pl.ds(pl.multiple_of(8 * (group >> 1), 8), 8)
        pieces.append((r_hbm.at[rows, pl.ds(at, 128)], share_ref.at[pl.ds(8 * k, 8)]))
    for ahead, x_next_ref in enumerate(x_next_refs):
        for member in range(2):
            row = pl.multiple_of(ROWS * (4 * member + ((own + ahead) & 3)), ROWS)
            target = x_next_ref.at[pl.ds(ROWS * member, ROWS)]
            pieces.append((x_hbm.at[pl.ds(row, ROWS)], target))
    loads = [
        pltpu.make_async_copy(source, target, sems.at[3 + k])
        for k, (source, target) in enumerate(pieces)
    ]
    for load in loads:
        load.start()

    def picked(values):
        value = values[3]
        for k in range(3):
            value = jnp.where(own == k, values[k], value)
        return value

    lat, lon = ([[picked(tap)] * 4 for tap in taps] for taps in taps_of(taps_ref))
    fill_tables(lat, lon, tile, rows_ref, band_ref)
    lats_ref[0], lats_ref[1] = split2(lat_ref[...])
    copies = [
        pltpu.make_async_copy(source, target, sems.at[k])
        for k, (source, target) in enumerate(zip((lats_ref, rows_ref, band_ref), hbm_refs))
    ]
    for copy in copies:
        copy.start()
    i, j = iotas(64, 512)
    repeat = jnp.where((i >> 3) == (j >> 6), jnp.where((i & 7) == (j & 7), 1.0, 0.0), 0.0)
    mine = lat_ref[pl.ds(pl.multiple_of(8 * tile, 8), 8), :]
    wide = exact_mm(mine, repeat)
    mix = jnp.concatenate([wide] * PAIRS, axis=0)
    mix = jnp.where((i >> 3) == ((j >> 3) & 7), mix, 0.0)
    mix_ref[0], mix_ref[1] = split2(mix)
    lons_ref[0], lons_ref[1] = split2(lon_ref[...])
    for load in loads:
        load.wait()
    j = lax.broadcasted_iota(jnp.int32, (8, 128), 1)
    for level in range(4):
        packed_r = jnp.zeros((8, 128), F32)
        for k in range(4):
            row = ROWS * level + 8 * k
            shift = (32 * (k + 4 - (group & 3))) & 127
            turned = pltpu.roll(lanes_ref[row : row + 8], shift, 1)
            packed_r = jnp.where((j >> 5) == k, turned, packed_r)
        packed_ref[level] = packed_r
    for copy in copies:
        copy.wait()


def banded(band_ref, level, kind):
    band = band_ref[level, kind]
    edge, half = jnp.zeros((112, 128), BF16), jnp.zeros((128, 128), BF16)
    left = jnp.concatenate([edge, band, edge, half], axis=0)
    right = jnp.concatenate([half, edge, band, edge], axis=0)
    return jnp.concatenate([left, right], axis=1)


def windows(parts, first_row, height):
    rows = []
    for block in range(4):
        for part in parts:
            lanes = [
                part[first_row : first_row + height, 128 * tile : 128 * tile + 128]
                for tile in ((2 * block - 1) % 8, 2 * block, 2 * block + 1, (2 * block + 2) % 8)
            ]
            rows.append(jnp.concatenate(lanes, axis=1))
    return jnp.concatenate(rows, axis=0)


def lane_sums(values):
    i, j = iotas(8, 128)
    result = jnp.zeros((8, 128), F32)
    for lane, value in values:
        result = jnp.where((i == 0) & (j == lane), value, result)
    return result


def total(x):
    return jnp.sum(x, axis=(0, 1), keepdims=True)


def fine_kernel(last, *refs):
    if last:
        r_ref, v_ref, c_ref, *refs = refs
    else:
        *refs, f_ref, c_ref, v_ref, x_ref, rows_ref, band_ref, sems = refs
        v_hbm, c_hbm, x_hbm, taps_ref, *refs = refs
        loads = [
            pltpu.make_async_copy(source, target, sems.at[k])
            for k, (source, target) in enumerate(
                ((c_hbm.at[0], c_ref), (v_hbm, v_ref), (x_hbm, x_ref))
            )
        ]
        for load in loads:
            load.start()
        fill_tables(*taps_of(taps_ref), own_tile(), rows_ref, band_ref)
    before_ref, after_ref, *refs = refs
    if last:
        rows_ref, band_ref, *refs = refs
    x_refs, refs = (refs[:4], refs[4:]) if last else ((x_ref,), refs)
    if last:
        fine_ref, mean_ref, sums_ref, lines_ref, f_ref, v_packed = refs
        v = natural(v_ref)
    else:
        fine_ref, mean_ref = refs
        for load in loads:
            load.wait()
        v = v_ref[...]
    halves = halves_of(x_refs)
    v_rows, spread = for_each(v), prolong(c_ref[...])
    highs, lows = [], []
    for part in range(2):
        d = halves[part].astype(F32) * v_rows - spread[128 * part : 128 * part + 128]
        rows = []
        for k in range(4):
            pair = 4 * part + k
            rows += [before_ref[pair], d[ROWS * k : ROWS * k + ROWS], after_ref[pair]]
        high, low = split2(jnp.concatenate(rows, axis=0))
        passed = mm3((rows_ref[0], rows_ref[1]), (high, low))
        high, low = split2(passed)
        highs.append(high)
        lows.append(low)
    levels = band_ref.shape[0]
    height = 128 // levels
    for level in range(levels):
        high = windows(highs, height * level, height)
        low = windows(lows, height * level, height)
        table_high, table_low = banded(band_ref, level, 0), banded(band_ref, level, 1)
        result = mm3((high, low), (table_high, table_low))
        for block in range(4):
            lanes = slice(256 * block, 256 * block + 256)
            summed = None
            for part in range(2):
                for inner in range(height // ROWS):
                    row = height * level + ROWS * inner
                    at = height * (2 * block + part) + ROWS * inner
                    f = result[at : at + ROWS]
                    f_ref[128 * part + row : 128 * part + row + ROWS, lanes] = f
                    term = halves[part][row : row + ROWS, lanes].astype(F32) * f
                    summed = term if summed is None else summed + term
            fine_ref[ROWS * level : ROWS * level + ROWS, lanes] = summed
    means = lon_mean([lat_mean(f_ref[128 * k : 128 * k + 128]) for k in range(2)])
    mean_ref[...] = means
    if last:
        for group, share in enumerate(packed(v)):
            v_packed[group] = share
        mine = pl.ds(own_group() & 7, 1)
        for group in range(GROUPS):
            lines_ref[group : group + 1] = v_packed[group, mine, :]
        r = r_ref[...]
        products = total(v * fine_ref[...]) - 16.0 * total(c_ref[...] * means)
        sums_ref[...] = lane_sums(
            ((0, total(r * r)), (1, total(r * v)), (2, total(v * v)), (3, products))
        )


def smooth_kernel(c_ref, lats_ref, lons_ref, sums_ref, out_ref):
    c = c_ref[...].reshape(64, 256)
    across = mm3((lats_ref[0], lats_ref[1]), split2(c))
    smoothed = mm3(split2(across), (lons_ref[0], lons_ref[1]))
    sums = sums_ref[...] + lane_sums([(4, 16.0 * total(c * smoothed))])
    for tile in range(TILES):
        out_ref[tile, 0:8, :] = smoothed[8 * tile : 8 * tile + 8, :128]
        out_ref[tile, 8:16, :] = smoothed[8 * tile : 8 * tile + 8, 128:]
        out_ref[tile, 16:24, :] = sums


def blended(x_refs, fine_ref, smoothed, loads=()):
    spread, height = prolong(smoothed), fine_ref.shape[0]
    for load in loads:
        load.wait()
    result = fine_ref[...]
    for k, x in enumerate(halves_of(x_refs)):
        product = x.astype(F32) * spread[128 * k : 128 * k + 128]
        for row in range(0, 128, height):
            result = result + product[row : row + height]
    return result


def partial_kernel(x_hbm, c_hbm, fine_ref, mean_ref, mix_ref, lons_ref, out_ref, *refs):
    x_ref, c_ref, sems = refs
    spans = [(c_hbm, c_ref, k, 1) for k in range(TILES)]
    spans += [(x_hbm, x_ref, 64 * k, 64) for k in range(4)]
    loads = [
        pltpu.make_async_copy(source.at[pl.ds(at, size)], target.at[pl.ds(at, size)], sems.at[k])
        for k, (source, target, at, size) in enumerate(spans)
    ]
    for load in loads:
        load.start()
    across = None
    for part in range(2):
        for load in loads[4 * part : 4 * part + 4]:
            load.wait()
        lanes = slice(256 * part, 256 * part + 256)
        c = c_ref[4 * part : 4 * part + 4].reshape(256, 256)
        term = mm3((mix_ref[0, :, lanes], mix_ref[1, :, lanes]), split2(c))
        across = term if across is None else across + term
    smoothed = mm3(split2(across), (lons_ref[0], lons_ref[1])) - mean_ref[...]
    p = blended((x_ref,), fine_ref, smoothed, loads[8:])
    for tall in range(16):
        for wide in range(8):
            out_ref[2 * tall + wide // 4, 8 * (wide % 4) : 8 * (wide % 4) + 8, :] = p[
                8 * tall : 8 * tall + 8, 128 * wide : 128 * wide + 128
            ]


def packed(field):
    group = lax.broadcasted_iota(jnp.int32, (8, 128), 1) >> 5
    shares = []
    for wide in range(8):
        tiles = [field[8 * i : 8 * i + 8, 128 * wide : 128 * wide + 128] for i in range(4)]
        for g in range(4):
            share = None
            for i in range(4):
                turned = pltpu.roll(tiles[i], (32 * (i - g)) % 128, 1) if i != g else tiles[i]
                share = turned if share is None else jnp.where(group == i, turned, share)
            shares.append(share)
    return shares


def last_partial_kernel(fine_ref, mean_ref, smoothed_ref, lines_ref, *refs):
    *x_refs, out_ref = refs
    halves = [smoothed_ref[:, 8 * k : 8 * k + 8, :].reshape(64, 128) for k in range(2)]
    p = blended(x_refs, fine_ref, jnp.concatenate(halves, axis=1) - mean_ref[...])
    sums = jnp.sum(smoothed_ref[:, 16:24, :], axis=0)
    for group, share in enumerate(packed(p)):
        out_ref[10 * group : 10 * group + 8] = share
        out_ref[10 * group + 8 : 10 * group + 9] = lines_ref[group : group + 1]
        out_ref[10 * group + 9 : 10 * group + 10] = sums[:1]


def share_kernel(scale, arrived_ref, r_ref, out_ref):
    share = r_ref[...] + jnp.sum(arrived_ref[...], axis=0) * scale
    for other in range(out_ref.shape[0]):
        out_ref[other] = share


def final_kernel(scale, arrived_ref, r_ref, x_out, res_out):
    i, j = iotas(8, 128)
    sums = arrived_ref[9:10]
    for k in range(1, GROUPS):
        sums = sums + arrived_ref[10 * k + 9 : 10 * k + 10]
    rr, ra, aa, af, ac = (total(jnp.where(j[:1] == k, sums, 0.0)) for k in range(5))
    rr, ra, aa = rr / 8, ra / 8, aa / 8
    step = rr / ra
    ab = aa + (af + ac) * scale
    squares = step * step * aa - rr
    next_step = squares / ((ra - step * aa) - step * (aa - step * ab))
    for level in range(4):
        r = r_ref[level]
        at = [10 * (8 * level + k) for k in range(8)]
        a = jnp.concatenate([arrived_ref[k + 8 : k + 9] for k in at], axis=0)
        p = functools.reduce(jnp.add, [arrived_ref[k : k + 8] for k in at])
        b = a + p * scale
        r_next = r - step * a
        x_new = step * r + next_step * r_next
        res_new = r_next - next_step * (a - step * b)
        for k in range(4):
            x_out[level, 8 * k : 8 * k + 8, :] = x_new[:, 32 * k : 32 * k + 32]
            res_out[level, 8 * k : 8 * k + 8, :] = res_new[:, 32 * k : 32 * k + 32]


VMEM = pl.BlockSpec(memory_space=pltpu.VMEM)
HBM = pl.BlockSpec(memory_space=pltpu.HBM)


def call(kernel, outs, specs, args, flops, limit, scratch=(), out_specs=None):
    out_specs = out_specs or [VMEM] * len(outs)
    shapes = [
        pltpu.HBM(*out) if spec is HBM else jax.ShapeDtypeStruct(*out)
        for out, spec in zip(outs, out_specs)
    ]
    size = sum(a.size * a.dtype.itemsize for a in args)
    args = [
        pltpu.with_memory_space_constraint(arg, pltpu.HBM) if spec is HBM else arg
        for arg, spec in zip(args, specs)
    ]
    return pl.pallas_call(
        kernel,
        out_shape=shapes if len(shapes) > 1 else shapes[0],
        in_specs=specs,
        out_specs=out_specs if len(shapes) > 1 else out_specs[0],
        scratch_shapes=list(scratch),
        compiler_params=pltpu.CompilerParams(vmem_limit_bytes=limit << 20),
        cost_estimate=pl.CostEstimate(flops=flops, bytes_accessed=size, transcendentals=0),
    )(*args)


def exchange(blocks, axis):
    return lax.all_to_all(blocks, axis, 0, 0, tiled=True)


def local(perturbations, right_side, fine_taps, coarse_lat, coarse_lon):
    count, levels, height, extent = perturbations.shape
    members = count * lax.axis_size(MEM)
    scale = 1.0 / (members - 1)
    x = perturbations.reshape(count * levels * height, extent)
    r = right_side.reshape(levels * height, extent)
    half = ((128, LON), F32)
    edge = ((PAIRS, 8, LON), F32)
    shared = ((GROUPS, 32, 128), F32)
    up = [(i, (i + 1) % TILES) for i in range(TILES)]
    down = [(j, i) for i, j in up]

    def edges(top, bottom):
        return lax.ppermute(bottom, "tile", up), lax.ppermute(top, "tile", down)

    own = ((64, 256), F32)
    taps = fine_taps.reshape(2 * levels, 5)
    rows_shape, band_shape = (2, 128, 192), (2, 160, 128)
    top, bottom, c = call(
        first_detail_kernel,
        [edge, edge, ((TILES, 64, 256), F32)],
        [HBM] * 2,
        (x, r),
        10**9,
        12,
        scratch=(
            pltpu.VMEM((256, LON), BF16),
            pltpu.VMEM((128, LON), F32),
            pltpu.VMEM(*own),
            pltpu.SemaphoreType.DMA((8,)),
            pltpu.SemaphoreType.DMA((4,)),
            pltpu.SemaphoreType.DMA((TILES,)),
        ),
        out_specs=[VMEM, VMEM, HBM],
    )
    before, after = edges(top, bottom)
    c_first = exchange(c, "tile")
    before, x_again = lax.optimization_barrier((before, x))
    next_tables = [((2, 64, 64), BF16), (rows_shape, BF16), ((1, *band_shape), BF16)]
    level = ((height, LON), F32)
    outs = [
        ((2, 64, 512), BF16),
        ((2, 256, 256), BF16),
        ((32, 128), F32),
        level,
        ((levels, 8, 128), F32),
        *[((count * height, extent), BF16)] * 4,
    ]
    mix, lons, r_share, r_level, r_packed, *x_next = call(
        table_kernel,
        outs + next_tables,
        [HBM] * 2 + [VMEM] * 3,
        (x_again, r, taps, coarse_lat, coarse_lon),
        10**11,
        6,
        scratch=[
            *(pltpu.VMEM(*shape) for shape in next_tables),
            pltpu.VMEM((128, 128), F32),
            pltpu.SemaphoreType.DMA((17,)),
        ],
        out_specs=[VMEM] * len(outs) + [HBM] * 3,
    )
    *x_next, lats, rows_next, band_next = x_next
    before, mix = lax.optimization_barrier((before, mix))
    for ahead in range(1, 4):
        ring = [(i, (i + ahead) % 4) for i in range(4)]
        x_next[ahead] = lax.ppermute(x_next[ahead], "mem_0", ring)
    fine_scratch = [pltpu.VMEM((256, LON), F32)]
    fine, means = call(
        functools.partial(fine_kernel, False),
        [half, own],
        [HBM] * 3 + [VMEM] * 3,
        (r, c, x, taps, before, after),
        10**11,
        16,
        scratch=[
            *fine_scratch,
            pltpu.VMEM(*own),
            pltpu.VMEM(r.shape, F32),
            pltpu.VMEM(x.shape, BF16),
            pltpu.VMEM(rows_shape, BF16),
            pltpu.VMEM((levels, *band_shape), BF16),
            pltpu.SemaphoreType.DMA((3,)),
        ],
    )
    fine, x_next = lax.optimization_barrier((fine, x_next))
    shares = call(
        partial_kernel,
        [shared],
        [HBM] * 2 + [VMEM] * 4,
        (x, c_first, fine, means, mix, lons),
        10**9,
        12,
        scratch=[
            pltpu.VMEM(x.shape, BF16),
            pltpu.VMEM(c.shape, F32),
            pltpu.SemaphoreType.DMA((12,)),
        ],
    )
    arrived = exchange(shares, MEM)
    share = call(
        functools.partial(share_kernel, scale),
        [((TILES, 32, 128), F32)],
        [VMEM, VMEM],
        (arrived, r_share),
        10**6,
        6,
    )
    a = exchange(share, ("mem_1", "mem_2"))

    top, bottom, c, c_own = call(
        detail_kernel,
        [edge, edge, ((PAIRS, 8, 256), F32), own],
        [VMEM] * 5,
        (a, *x_next),
        10**9,
        12,
    )
    beside = edges(top, bottom)
    c = exchange(c, "tile")
    fine, means, sums, lines = call(
        functools.partial(fine_kernel, True),
        [level, own, ((8, 128), F32), ((GROUPS, 128), F32)],
        [VMEM] * 11,
        (r_level, a, c_own, *beside, rows_next, band_next, *x_next),
        10**11,
        16,
        scratch=fine_scratch + [pltpu.VMEM((GROUPS, 8, 128), F32)],
    )
    smoothed = call(
        smooth_kernel,
        [((TILES, 24, 128), F32)],
        [VMEM] * 4,
        (c, lats, lons, sums),
        10**8,
        6,
    )
    smoothed = exchange(smoothed, "tile")
    shares = call(
        last_partial_kernel,
        [((GROUPS * 10, 128), F32)],
        [VMEM] * 8,
        (fine, means, smoothed, lines, *x_next),
        10**9,
        12,
    )
    arrived = exchange(shares.reshape(GROUPS, 1, 1280), MEM).reshape(shares.shape)
    out = ((levels, height, extent // GROUPS), F32)
    return tuple(
        call(
            functools.partial(final_kernel, scale),
            [out, out],
            [VMEM, VMEM],
            (arrived, r_packed),
            10**6,
            6,
        )
    )


def solution(mesh):
    torus = Mesh(
        mesh.devices.reshape(4, 4, 2, mesh.shape["tile"]), ("mem_0", "mem_1", "mem_2", "tile")
    )
    placed = (P(MEM, None, "tile", None), P(None, "tile", None), P(), P(), P())
    return jax.shard_map(
        local,
        mesh=torus,
        in_specs=placed,
        out_specs=(P(None, "tile", MEM), P(None, "tile", MEM)),
        check_vma=False,
    )
```
